32 devices in a mesh: seq: 8 (over y, x, core), head: 4 (over z).
Axes of the slice: x: 2, y: 2, z: 4, core: 2. Of those that a mesh axis runs over, the one named last changes fastest.
Arguments:
- queries: bfloat16 [2048, 4096], P(('seq', 'head')), may hold values from -10 to 10
- keys: bfloat16 [2048, 1024], P(('seq', 'head')), may hold values from -10 to 10
- block_pos: int32 [16], replicated, may hold values from 0 to 15, each once
- query_map: float32 [32, 128, 128], P('head'), may hold values from -4 to 4
- key_map: float32 [8, 128, 128], P('head'), may hold values from -4 to 4
Outputs:
- query_map_gradient: float32 [32, 128, 128], P('head')
- key_map_gradient: float32 [8, 128, 128], P('head')
The draws below stay inside these ranges and needn't reach their ends.
Inputs may be any that keep to these rules, and one draw needn't show every extreme that they name: A permutation: stored block g (token rows g * 128 to (g + 1) * 128 - 1) holds position block block_pos[g]; position blocks below 8 form the first sequence, the others the second.
All inputs are finite; a program needn't handle non-finite values.
Results may differ from the reference program's by a relative error of at most 0.0021.
Values may be sent and summed in bfloat16 or wider, within the bound.
No kernel may reach another device: no remote copies, remote signals or barrier semaphores. Data moves between devices by JAX's collectives and lax.ppermute only.
A program may use at most 64 MiB of HBM per device.

```python
import math
import jax
import jax.numpy as jnp
from jax import lax

QUERY_HEAD_COUNT = 32
KEY_HEAD_COUNT = 8
HEAD_SIZE = 128
BLK = 128
TOKEN_TOTAL = 2048
N_SEQ = 8


def field_pair(key):
    base_offset = jax.random.fold_in(key, 7)
    key_feature_field = jnp.clip(jax.random.normal(jax.random.fold_in(base_offset, 1), (TOKEN_TOTAL, KEY_HEAD_COUNT, HEAD_SIZE), jnp.float32), -4.0, 4.0)
    query_feature_field = jnp.clip(jax.random.normal(jax.random.fold_in(base_offset, 2), (TOKEN_TOTAL, KEY_HEAD_COUNT, QUERY_HEAD_COUNT // KEY_HEAD_COUNT, HEAD_SIZE), jnp.float32), -4.0, 4.0)
    return (query_feature_field.reshape(TOKEN_TOTAL, QUERY_HEAD_COUNT * HEAD_SIZE), key_feature_field.reshape(TOKEN_TOTAL, KEY_HEAD_COUNT * HEAD_SIZE))


def feature_map_values(key, head_count):
    values = jnp.clip(jax.random.normal(key, (head_count, HEAD_SIZE, HEAD_SIZE), jnp.float32), -4.0, 4.0) / math.sqrt(HEAD_SIZE)
    return values


def draw_queries(key, part):
    return field_pair(key)[0].astype(jnp.bfloat16)


def draw_keys(key, part):
    return field_pair(key)[1].astype(jnp.bfloat16)


def draw_query_map(key, part):
    return feature_map_values(jax.random.fold_in(key, 11), QUERY_HEAD_COUNT)


def draw_key_map(key, part):
    return feature_map_values(jax.random.fold_in(key, 13), KEY_HEAD_COUNT)


def setup_inputs(seed: int = 0) -> dict:
    key_list = jax.random.split(jax.random.key(seed), 6)
    return {
        "queries": draw_queries(jax.random.fold_in(key_list[5], 71), 0),
        "keys": draw_keys(jax.random.fold_in(key_list[5], 71), 0),
        "block_pos": jax.random.permutation(key_list[2], 2 * N_SEQ).astype(jnp.int32),
        "query_map": draw_query_map(jax.random.fold_in(key_list[5], 71), 0),
        "key_map": draw_key_map(jax.random.fold_in(key_list[5], 71), 0),
    }


HIGHEST = lax.Precision.HIGHEST
NEG_FLOOR = -1e+30

def softmax_pair(logits):
    return jnp.concatenate([jax.nn.softmax(logits, axis=-1), jax.nn.softmax(-logits, axis=-1)], axis=-1)

def feature_grad(feature, upstream):
    half_width = feature.shape[-1] // 2
    positive, negative = (feature[..., :half_width], feature[..., half_width:])
    grad_positive, grad_negative = (upstream[..., :half_width], upstream[..., half_width:])
    first = positive * (grad_positive - lax.optimization_barrier(jnp.sum(grad_positive * positive, axis=-1, keepdims=True)))
    second = negative * (grad_negative - lax.optimization_barrier(jnp.sum(grad_negative * negative, axis=-1, keepdims=True)))
    return first - second

def reference(queries, keys, block_pos, query_map, key_map):
    token_count = queries.shape[0]
    group_width = QUERY_HEAD_COUNT // KEY_HEAD_COUNT
    row_index = jnp.arange(token_count, dtype=jnp.int32)
    blocks = block_pos[row_index // BLK]
    seq_ids = blocks // N_SEQ
    places = blocks * BLK + row_index % BLK
    block_count = token_count // BLK
    score_scale = HEAD_SIZE ** (-0.5)

    def single_head(kv_index):
        key_rows = lax.dynamic_slice_in_dim(keys, kv_index * HEAD_SIZE, HEAD_SIZE, 1)
        key_wide = key_rows.astype(jnp.float32)
        phi_key = softmax_pair(jnp.dot(key_wide, key_map[kv_index], precision=HIGHEST))
        phi_key_b = phi_key.astype(jnp.bfloat16)
        query_rows = lax.dynamic_slice_in_dim(queries, kv_index * group_width * HEAD_SIZE, group_width * HEAD_SIZE, 1)
        query_heads = query_rows.reshape(token_count, group_width, HEAD_SIZE).transpose(1, 0, 2)
        query_wide = query_heads.astype(jnp.float32)
        head_maps = lax.dynamic_slice_in_dim(query_map, kv_index * group_width, group_width, 0)
        phi_query = softmax_pair(jnp.einsum('gtd,gde->gte', query_wide, head_maps, precision=HIGHEST))
        phi_query_b = phi_query.astype(jnp.bfloat16)

        def one_block(key_grad, number):
            query_block = lax.dynamic_slice_in_dim(query_heads, number * BLK, BLK, 1).reshape(group_width * BLK, HEAD_SIZE)
            phi_block = lax.dynamic_slice_in_dim(phi_query_b, number * BLK, BLK, 1).reshape(group_width * BLK, 2 * HEAD_SIZE)
            block_seq = jnp.tile(lax.dynamic_slice_in_dim(seq_ids, number * BLK, BLK), group_width)
            block_place = jnp.tile(lax.dynamic_slice_in_dim(places, number * BLK, BLK), group_width)
            visible = (seq_ids[None, :] == block_seq[:, None]) & (places[None, :] <= block_place[:, None])
            scores = jnp.dot(query_block, key_rows.T, preferred_element_type=jnp.float32) * score_scale
            masked = jnp.where(visible, scores, NEG_FLOOR)
            highest = lax.optimization_barrier(jnp.max(masked, axis=-1, keepdims=True))
            exponent = jnp.where(visible, jnp.exp(masked - highest), 0.0)
            teacher_prob = exponent / lax.optimization_barrier(jnp.sum(exponent, axis=-1, keepdims=True))
            linear = jnp.dot(phi_block, phi_key_b.T, preferred_element_type=jnp.float32)
            linear_sum = lax.optimization_barrier(jnp.sum(jnp.where(visible, linear, 0.0), axis=-1, keepdims=True))
            weights = (jnp.where(visible, 1.0 / linear_sum - teacher_prob / linear, 0.0) / token_count).astype(jnp.bfloat16)
            query_grad = jnp.dot(weights, phi_key_b, preferred_element_type=jnp.float32)
            key_grad = key_grad + jnp.dot(weights.T, phi_block, preferred_element_type=jnp.float32)
            return (key_grad, query_grad)
        key_grad, query_grads = lax.scan(one_block, jnp.zeros((token_count, 2 * HEAD_SIZE), jnp.float32), jnp.arange(block_count, dtype=jnp.int32))
        query_grad = query_grads.reshape(block_count, group_width, BLK, 2 * HEAD_SIZE).transpose(1, 0, 2, 3).reshape(group_width, token_count, 2 * HEAD_SIZE)
        query_weight_grad = jnp.einsum('gtd,gte->gde', query_wide, feature_grad(phi_query, query_grad), precision=HIGHEST)
        key_weight_grad = jnp.dot(key_wide.T, feature_grad(phi_key, key_grad), precision=HIGHEST)
        return (query_weight_grad, key_weight_grad)
    query_map_gradient, key_map_gradient = lax.map(single_head, jnp.arange(KEY_HEAD_COUNT, dtype=jnp.int32))
    return (query_map_gradient.reshape(QUERY_HEAD_COUNT, HEAD_SIZE, HEAD_SIZE), key_map_gradient)
```

```python
import functools
import math

import jax
import jax.numpy as jnp
from jax import lax
from jax.experimental import pallas as pl
from jax.experimental.pallas import tpu as pltpu
from jax.sharding import PartitionSpec as P

HEAD_SIZE = 128
BLK = 128

HIGHEST = lax.Precision.HIGHEST
NEG_FLOOR = -1e30


def softmax_pair(logits):
    return jnp.concatenate(
        [jax.nn.softmax(logits, axis=-1), jax.nn.softmax(-logits, axis=-1)], axis=-1
    )


def feature_grad(feature, upstream):
    half_width = feature.shape[-1] // 2
    positive, negative = (feature[..., :half_width], feature[..., half_width:])
    grad_positive, grad_negative = (upstream[..., :half_width], upstream[..., half_width:])
    first = positive * (grad_positive - jnp.sum(grad_positive * positive, axis=-1, keepdims=True))
    second = negative * (grad_negative - jnp.sum(grad_negative * negative, axis=-1, keepdims=True))
    return first - second


def row_places(row_index, block_pos, seq_count):
    stored = row_index // BLK
    lookup = stored[:, None] == jnp.arange(block_pos.shape[0], dtype=jnp.int32)[None, :]
    blocks = jnp.sum(jnp.where(lookup, block_pos[None, :], 0), axis=1)
    return (blocks // seq_count, blocks * BLK + row_index % BLK)


def over_blocks(running, portions, step_fn):
    row_count = portions[0].shape[1]
    step_rows = math.gcd(row_count, 512)

    def advance(number, inner_carry):
        slabs = tuple(
            (
                lax.dynamic_slice_in_dim(portion, number * step_rows, step_rows, 1)
                for portion in portions
            )
        )
        return step_fn(inner_carry, slabs, number * step_rows)

    return lax.fori_loop(0, row_count // step_rows, advance, running)


def per_device_general(queries, keys, block_pos, query_map, key_map):
    local_q, local_k = (
        lax.all_to_all(queries, "head", split_axis=1, concat_axis=0, tiled=True),
        lax.all_to_all(keys, "head", split_axis=1, concat_axis=0, tiled=True),
    )
    seq_count = lax.axis_size("seq")
    seq_rank = lax.axis_index("seq")
    rows_local = local_k.shape[0]
    token_count = rows_local * seq_count
    key_heads = key_map.shape[0]
    group_width = query_map.shape[0] // key_heads
    score_scale = HEAD_SIZE ** (-0.5)
    query_index = seq_rank * rows_local + jnp.arange(rows_local, dtype=jnp.int32)
    query_heads = local_q.reshape(rows_local, key_heads, group_width, HEAD_SIZE).transpose(
        1, 2, 0, 3
    )
    query_wide = query_heads.astype(jnp.float32)
    query_logits = jnp.einsum(
        "vgnd,vgde->vgne",
        query_wide,
        query_map.reshape(key_heads, group_width, HEAD_SIZE, HEAD_SIZE),
        precision=HIGHEST,
    )
    rows_all = group_width * rows_local
    phi_query = softmax_pair(query_logits).reshape(key_heads, rows_all, 2 * HEAD_SIZE)
    phi_query_b = phi_query.astype(jnp.bfloat16)
    query_flat = query_heads.reshape(key_heads, rows_all, HEAD_SIZE)
    query_seq, query_at = row_places(query_index, block_pos, seq_count)
    query_seq = jnp.tile(query_seq, group_width)
    query_at = jnp.tile(query_at, group_width)

    def visible_for(offset, slab_rows):
        key_index = offset + jnp.arange(slab_rows, dtype=jnp.int32)
        key_seq, key_at = row_places(key_index, block_pos, seq_count)
        return (key_seq[None, :] == query_seq[:, None]) & (key_at[None, :] <= query_at[:, None])

    def key_features(key_slab):
        logits = jnp.einsum(
            "vwd,vde->vwe", key_slab.astype(jnp.float32), key_map, precision=HIGHEST
        )
        return softmax_pair(logits)

    def teacher(key_slab):
        return (
            jnp.einsum("vrd,vwd->vrw", query_flat, key_slab, preferred_element_type=jnp.float32)
            * score_scale
        )

    def stats_step(running, slabs, offset):
        key_slab = slabs[0]
        visible = visible_for(offset, key_slab.shape[1])

        def stats_compute_live(current):
            highest, denominator, linear_sum = current
            masked = jnp.where(visible[None], teacher(key_slab), NEG_FLOOR)
            new_high = jnp.maximum(highest, jnp.max(masked, axis=-1))
            exponent = jnp.where(visible[None], jnp.exp(masked - new_high[..., None]), 0.0)
            denominator = denominator * jnp.exp(highest - new_high) + jnp.sum(exponent, axis=-1)
            phi_key_b = key_features(key_slab).astype(jnp.bfloat16)
            linear = jnp.einsum(
                "vrf,vwf->vrw", phi_query_b, phi_key_b, preferred_element_type=jnp.float32
            )
            linear_sum = linear_sum + jnp.sum(jnp.where(visible[None], linear, 0.0), axis=-1)
            return (new_high, denominator, linear_sum)

        return lax.cond(jnp.any(visible), stats_compute_live, lambda current: current, running)

    def grads_step(running, slabs, offset):
        key_slab = slabs[0]
        visible = visible_for(offset, key_slab.shape[1])

        def grads_compute_live(current):
            query_grad, key_weight_grad = current
            masked = jnp.where(visible[None], teacher(key_slab), NEG_FLOOR)
            exponent = jnp.where(visible[None], jnp.exp(masked - highest[..., None]), 0.0)
            teacher_prob = exponent / denominator[..., None]
            phi_key = key_features(key_slab)
            phi_key_b = phi_key.astype(jnp.bfloat16)
            linear = jnp.einsum(
                "vrf,vwf->vrw", phi_query_b, phi_key_b, preferred_element_type=jnp.float32
            )
            weights = (
                jnp.where(visible[None], 1.0 / linear_sum[..., None] - teacher_prob / linear, 0.0)
                / token_count
            ).astype(jnp.bfloat16)
            query_grad = query_grad + jnp.einsum(
                "vrw,vwf->vrf", weights, phi_key_b, preferred_element_type=jnp.float32
            )
            key_grad = jnp.einsum(
                "vrw,vrf->vwf", weights, phi_query_b, preferred_element_type=jnp.float32
            )
            key_logit_grad = feature_grad(phi_key, key_grad)
            key_weight_grad = key_weight_grad + jnp.einsum(
                "vwd,vwe->vde", key_slab.astype(jnp.float32), key_logit_grad, precision=HIGHEST
            )
            return (query_grad, key_weight_grad)

        return lax.cond(jnp.any(visible), grads_compute_live, lambda current: current, running)

    def as_heads(pieces):
        return pieces.reshape(pieces.shape[0], key_heads, -1).transpose(1, 0, 2)

    row_zeros = jnp.zeros((key_heads, rows_all), jnp.float32)
    stats_init = (jnp.full((key_heads, rows_all), NEG_FLOOR, jnp.float32), row_zeros, row_zeros)
    grads_init = (
        jnp.zeros((key_heads, rows_all, 2 * HEAD_SIZE), jnp.float32),
        jnp.zeros((key_heads, HEAD_SIZE, HEAD_SIZE), jnp.float32),
    )
    highest, denominator, linear_sum = over_blocks(
        stats_init, (as_heads(lax.all_gather(local_k, "seq", axis=0, tiled=True)),), stats_step
    )
    query_grad, key_weight_grad = over_blocks(
        grads_init, (as_heads(lax.all_gather(local_k, "seq", axis=0, tiled=True)),), grads_step
    )
    query_logit_grad = feature_grad(phi_query, query_grad).reshape(
        key_heads, group_width, rows_local, HEAD_SIZE
    )
    query_weight_grad = jnp.einsum(
        "vgnd,vgne->vgde", query_wide, query_logit_grad, precision=HIGHEST
    ).reshape(key_heads * group_width, HEAD_SIZE, HEAD_SIZE)
    query_map_gradient, key_map_gradient = lax.psum((query_weight_grad, key_weight_grad), "seq")
    return (query_map_gradient, key_map_gradient)


NT = (((1,), (1,)), ((), ()))
F32 = jnp.float32
BF16 = jnp.bfloat16


def nn(left, right):
    return jnp.dot(left, right, preferred_element_type=F32)


def nt(left, right):
    return lax.dot_general(left, right, NT, preferred_element_type=F32)


def bf16_parts(value, count):
    parts = []
    for _ in range(count):
        part = value.astype(BF16)
        parts.append(part)
        value = value - part.astype(F32)
    return jnp.concatenate(parts, axis=0)


def fold_parts(value, count):
    rows = value.shape[0] // count
    total = value[(count - 1) * rows :]
    for number in range(count - 2, -1, -1):
        total = total + value[number * rows : (number + 1) * rows]
    return total


def features_t(logits):
    up = jnp.exp(logits - jnp.max(logits, axis=0, keepdims=True))
    down = jnp.exp(jnp.min(logits, axis=0, keepdims=True) - logits)
    up = up * (1.0 / jnp.sum(up, axis=0, keepdims=True))
    down = down * (1.0 / jnp.sum(down, axis=0, keepdims=True))
    return jnp.concatenate([up, down], axis=0)


def feature_grad_t(feature, upstream):
    halves = []
    for half in (slice(0, HEAD_SIZE), slice(HEAD_SIZE, 2 * HEAD_SIZE)):
        value, grad = feature[half], upstream[half]
        halves.append(value * (grad - jnp.sum(grad * value, axis=0, keepdims=True)))
    return halves[0] - halves[1]


def head_kernel(
    token_count,
    seq_blocks,
    pos_ref,
    which_ref,
    rows_ref,
    query_map_ref,
    key_map_ref,
    out_ref,
    stored,
    query_rows,
    key_rows,
    phi_q,
    phi_k,
    phi_qb,
    phi_kb,
    phi_kb_rows,
    pair_weights,
    acc_q,
    acc_k,
):
    del which_ref
    chunk = rows_ref.shape[1] // 2
    per_block = BLK // chunk
    seq_tokens = seq_blocks * BLK
    sequences = token_count // seq_tokens
    for number in range(token_count // BLK):
        stored[pos_ref[number]] = number
    acc_q[...] = jnp.zeros_like(acc_q)
    acc_k[...] = jnp.zeros_like(acc_k)
    query_map_t = bf16_parts(query_map_ref[0].T, 3)
    key_map_t = bf16_parts(key_map_ref[0].T, 3)
    lane = lax.broadcasted_iota(jnp.int32, (BLK, BLK), 1)
    sublane = lax.broadcasted_iota(jnp.int32, (BLK, BLK), 0)
    unit = jnp.where(lane == sublane, 1.0, 0.0).astype(BF16)
    visible = sublane <= lane
    exponent_scale = HEAD_SIZE ** (-0.5) * math.log2(math.e)

    def block_rows(place, half):
        first = place * per_block
        return rows_ref[pl.ds(first, per_block), half * chunk : (half + 1) * chunk, :].reshape(
            BLK, HEAD_SIZE
        )

    def one_sequence(seq, carry):
        for at in range(seq_blocks):
            here = slice(at * BLK, (at + 1) * BLK)
            place = stored[seq * seq_blocks + at]
            key_block = block_rows(place, 1)
            key_rows[here, :] = key_block
            feature = features_t(fold_parts(nt(key_map_t, key_block), 3))
            phi_k[:, here] = feature
            rounded = feature.astype(BF16)
            phi_kb[:, here] = rounded
            phi_kb_rows[here, :] = nt(unit, rounded).astype(BF16)
            query_block = block_rows(place, 0)
            query_rows[here, :] = query_block
            feature = features_t(fold_parts(nt(query_map_t, query_block), 3))
            phi_q[:, here] = feature
            phi_qb[:, here] = feature.astype(BF16)
        for at in range(seq_blocks):
            here = slice(at * BLK, (at + 1) * BLK)
            live = (at + 1) * BLK
            query_block = query_rows[here, :]
            teacher = nt(key_rows[:live, :], query_block)
            student = nn(phi_kb_rows[:live, :], phi_qb[:, here])
            last = slice(at * BLK, live)
            teacher_last = jnp.where(visible, teacher[last], NEG_FLOOR)
            student_last = jnp.where(visible, student[last], 0.0)
            highest = jnp.max(teacher_last, axis=0, keepdims=True)
            linear_sum = jnp.sum(student_last, axis=0, keepdims=True)
            if at:
                highest = jnp.maximum(
                    highest, jnp.max(teacher[: at * BLK], axis=0, keepdims=True)
                )
                linear_sum = linear_sum + jnp.sum(student[: at * BLK], axis=0, keepdims=True)
            exponent_last = jnp.exp2((teacher_last - highest) * exponent_scale)
            denominator = jnp.sum(exponent_last, axis=0, keepdims=True)
            if at:
                exponent = jnp.exp2((teacher[: at * BLK] - highest) * exponent_scale)
                denominator = denominator + jnp.sum(exponent, axis=0, keepdims=True)
            base = 1.0 / (linear_sum * token_count)
            share = 1.0 / (denominator * token_count)
            weights = jnp.where(
                visible, base - (exponent_last * share) / student[last], 0.0
            ).astype(BF16)
            if at:
                weights = jnp.concatenate(
                    [
                        (base - (exponent * share) / student[: at * BLK]).astype(BF16),
                        weights,
                    ],
                    axis=0,
                )
            pair_weights[:live, here] = weights
            query_grad = nn(phi_kb[:, :live], weights)
            logit_grad = feature_grad_t(phi_q[:, here], query_grad)
            acc_q[...] += nn(bf16_parts(logit_grad, 2), query_block)
        for at in range(seq_blocks):
            here = slice(at * BLK, (at + 1) * BLK)
            later = slice(at * BLK, seq_tokens)
            key_grad = nt(phi_qb[:, later], pair_weights[here, later])
            logit_grad = feature_grad_t(phi_k[:, here], key_grad)
            acc_k[...] += nn(bf16_parts(logit_grad, 2), key_rows[here, :])
        return carry

    lax.fori_loop(0, sequences, one_sequence, 0)
    out_ref[:HEAD_SIZE, :] = fold_parts(acc_q[...], 2).T.astype(BF16)
    out_ref[HEAD_SIZE:, :] = bf16_parts(fold_parts(acc_k[...], 2).T, 2)


def send_kernel(seq_count, head_count, key_heads, queries_ref, keys_ref, out_ref):
    rows = queries_ref.shape[0]
    share = seq_count // key_heads
    for head in range(head_count):
        for seq in range(seq_count):
            target = seq * head_count + head
            column = (head * seq_count + seq) * HEAD_SIZE
            out_ref[target, :rows, :] = queries_ref[:, column : column + HEAD_SIZE]
            column = (head * key_heads + seq // share) * HEAD_SIZE
            out_ref[target, rows:, :] = keys_ref[:, column : column + HEAD_SIZE]


def per_device_head(queries, keys, block_pos, query_map, key_map):
    seq_count = lax.axis_size("seq")
    head_count = lax.axis_size("head")
    key_heads = key_map.shape[0]
    rows = queries.shape[0]
    devices = seq_count * head_count
    token_count = rows * devices
    sent = pl.pallas_call(
        functools.partial(send_kernel, seq_count, head_count, key_heads),
        out_shape=jax.ShapeDtypeStruct((devices, 2 * rows, HEAD_SIZE), BF16),
    )(queries, keys)
    arrived = lax.all_to_all(sent, ("seq", "head"), split_axis=0, concat_axis=0, tiled=True)
    mine = lax.axis_index("seq").astype(jnp.int32)
    which = jnp.stack([mine, mine // (seq_count // key_heads)])
    seq_tokens = seq_count * BLK
    whole = lambda *_: (0, 0, 0)
    grads = pl.pallas_call(
        functools.partial(head_kernel, token_count, seq_count),
        out_shape=jax.ShapeDtypeStruct((3 * HEAD_SIZE, HEAD_SIZE), BF16),
        grid_spec=pltpu.PrefetchScalarGridSpec(
            num_scalar_prefetch=2,
            grid=(1,),
            in_specs=[
                pl.BlockSpec(arrived.shape, whole),
                pl.BlockSpec((1, HEAD_SIZE, HEAD_SIZE), lambda _, pos, which: (which[0], 0, 0)),
                pl.BlockSpec((1, HEAD_SIZE, HEAD_SIZE), lambda _, pos, which: (which[1], 0, 0)),
            ],
            out_specs=pl.BlockSpec((3 * HEAD_SIZE, HEAD_SIZE), lambda *_: (0, 0)),
            scratch_shapes=[
                pltpu.SMEM((token_count // BLK,), jnp.int32),
                pltpu.VMEM((seq_tokens, HEAD_SIZE), BF16),
                pltpu.VMEM((seq_tokens, HEAD_SIZE), BF16),
                pltpu.VMEM((2 * HEAD_SIZE, seq_tokens), F32),
                pltpu.VMEM((2 * HEAD_SIZE, seq_tokens), F32),
                pltpu.VMEM((2 * HEAD_SIZE, seq_tokens), BF16),
                pltpu.VMEM((2 * HEAD_SIZE, seq_tokens), BF16),
                pltpu.VMEM((seq_tokens, 2 * HEAD_SIZE), BF16),
                pltpu.VMEM((seq_tokens, seq_tokens), BF16),
                pltpu.VMEM((2 * HEAD_SIZE, HEAD_SIZE), F32),
                pltpu.VMEM((2 * HEAD_SIZE, HEAD_SIZE), F32),
            ],
        ),
    )(block_pos, which, arrived, query_map, key_map)
    everyone = lax.all_gather(grads, "seq", axis=0, tiled=False)
    everyone = everyone.reshape(seq_count, 3, HEAD_SIZE, HEAD_SIZE).astype(F32)
    key_parts = (everyone[:, 1] + everyone[:, 2]).reshape(
        key_heads, seq_count // key_heads, HEAD_SIZE, HEAD_SIZE
    )
    return everyone[:, 0], jnp.sum(key_parts, axis=1)


def per_device(queries, keys, block_pos, query_map, key_map):
    seq_count = lax.axis_size("seq")
    one_head_each = (
        query_map.shape[0] == seq_count
        and seq_count % key_map.shape[0] == 0
        and BLK % queries.shape[0] == 0
    )
    chosen = per_device_head if one_head_each else per_device_general
    return chosen(queries, keys, block_pos, query_map, key_map)


def solution(mesh):
    in_specs = (
        P(("seq", "head"), None),
        P(("seq", "head"), None),
        P(),
        P("head", None, None),
        P("head", None, None),
    )
    out_specs = (P("head", None, None), P("head", None, None))
    return jax.shard_map(
        per_device, mesh=mesh, in_specs=in_specs, out_specs=out_specs, check_vma=False
    )
```

```python
import functools
import math

import jax
import jax.numpy as jnp
from jax import lax
from jax.experimental import pallas as pl
from jax.experimental.pallas import tpu as pltpu
from jax.sharding import PartitionSpec as P

HEAD_SIZE = 128
BLK = 128

HIGHEST = lax.Precision.HIGHEST
NEG_FLOOR = -1e30


def softmax_pair(logits):
    return jnp.concatenate(
        [jax.nn.softmax(logits, axis=-1), jax.nn.softmax(-logits, axis=-1)], axis=-1
    )


def feature_grad(feature, upstream):
    half_width = feature.shape[-1] // 2
    positive, negative = (feature[..., :half_width], feature[..., half_width:])
    grad_positive, grad_negative = (upstream[..., :half_width], upstream[..., half_width:])
    first = positive * (grad_positive - jnp.sum(grad_positive * positive, axis=-1, keepdims=True))
    second = negative * (grad_negative - jnp.sum(grad_negative * negative, axis=-1, keepdims=True))
    return first - second


def row_places(row_index, block_pos, seq_count):
    stored = row_index // BLK
    lookup = stored[:, None] == jnp.arange(block_pos.shape[0], dtype=jnp.int32)[None, :]
    blocks = jnp.sum(jnp.where(lookup, block_pos[None, :], 0), axis=1)
    return (blocks // seq_count, blocks * BLK + row_index % BLK)


def over_blocks(running, portions, step_fn):
    row_count = portions[0].shape[1]
    step_rows = math.gcd(row_count, 512)

    def advance(number, inner_carry):
        slabs = tuple(
            (
                lax.dynamic_slice_in_dim(portion, number * step_rows, step_rows, 1)
                for portion in portions
            )
        )
        return step_fn(inner_carry, slabs, number * step_rows)

    return lax.fori_loop(0, row_count // step_rows, advance, running)


def per_device_general(queries, keys, block_pos, query_map, key_map):
    local_q, local_k = (
        lax.all_to_all(queries, "head", split_axis=1, concat_axis=0, tiled=True),
        lax.all_to_all(keys, "head", split_axis=1, concat_axis=0, tiled=True),
    )
    seq_count = lax.axis_size("seq")
    seq_rank = lax.axis_index("seq")
    rows_local = local_k.shape[0]
    token_count = rows_local * seq_count
    key_heads = key_map.shape[0]
    group_width = query_map.shape[0] // key_heads
    score_scale = HEAD_SIZE ** (-0.5)
    query_index = seq_rank * rows_local + jnp.arange(rows_local, dtype=jnp.int32)
    query_heads = local_q.reshape(rows_local, key_heads, group_width, HEAD_SIZE).transpose(
        1, 2, 0, 3
    )
    query_wide = query_heads.astype(jnp.float32)
    query_logits = jnp.einsum(
        "vgnd,vgde->vgne",
        query_wide,
        query_map.reshape(key_heads, group_width, HEAD_SIZE, HEAD_SIZE),
        precision=HIGHEST,
    )
    rows_all = group_width * rows_local
    phi_query = softmax_pair(query_logits).reshape(key_heads, rows_all, 2 * HEAD_SIZE)
    phi_query_b = phi_query.astype(jnp.bfloat16)
    query_flat = query_heads.reshape(key_heads, rows_all, HEAD_SIZE)
    query_seq, query_at = row_places(query_index, block_pos, seq_count)
    query_seq = jnp.tile(query_seq, group_width)
    query_at = jnp.tile(query_at, group_width)

    def visible_for(offset, slab_rows):
        key_index = offset + jnp.arange(slab_rows, dtype=jnp.int32)
        key_seq, key_at = row_places(key_index, block_pos, seq_count)
        return (key_seq[None, :] == query_seq[:, None]) & (key_at[None, :] <= query_at[:, None])

    def key_features(key_slab):
        logits = jnp.einsum(
            "vwd,vde->vwe", key_slab.astype(jnp.float32), key_map, precision=HIGHEST
        )
        return softmax_pair(logits)

    def teacher(key_slab):
        return (
            jnp.einsum("vrd,vwd->vrw", query_flat, key_slab, preferred_element_type=jnp.float32)
            * score_scale
        )

    def stats_step(running, slabs, offset):
        key_slab = slabs[0]
        visible = visible_for(offset, key_slab.shape[1])

        def stats_compute_live(current):
            highest, denominator, linear_sum = current
            masked = jnp.where(visible[None], teacher(key_slab), NEG_FLOOR)
            new_high = jnp.maximum(highest, jnp.max(masked, axis=-1))
            exponent = jnp.where(visible[None], jnp.exp(masked - new_high[..., None]), 0.0)
            denominator = denominator * jnp.exp(highest - new_high) + jnp.sum(exponent, axis=-1)
            phi_key_b = key_features(key_slab).astype(jnp.bfloat16)
            linear = jnp.einsum(
                "vrf,vwf->vrw", phi_query_b, phi_key_b, preferred_element_type=jnp.float32
            )
            linear_sum = linear_sum + jnp.sum(jnp.where(visible[None], linear, 0.0), axis=-1)
            return (new_high, denominator, linear_sum)

        return lax.cond(jnp.any(visible), stats_compute_live, lambda current: current, running)

    def grads_step(running, slabs, offset):
        key_slab = slabs[0]
        visible = visible_for(offset, key_slab.shape[1])

        def grads_compute_live(current):
            query_grad, key_weight_grad = current
            masked = jnp.where(visible[None], teacher(key_slab), NEG_FLOOR)
            exponent = jnp.where(visible[None], jnp.exp(masked - highest[..., None]), 0.0)
            teacher_prob = exponent / denominator[..., None]
            phi_key = key_features(key_slab)
            phi_key_b = phi_key.astype(jnp.bfloat16)
            linear = jnp.einsum(
                "vrf,vwf->vrw", phi_query_b, phi_key_b, preferred_element_type=jnp.float32
            )
            weights = (
                jnp.where(visible[None], 1.0 / linear_sum[..., None] - teacher_prob / linear, 0.0)
                / token_count
            ).astype(jnp.bfloat16)
            query_grad = query_grad + jnp.einsum(
                "vrw,vwf->vrf", weights, phi_key_b, preferred_element_type=jnp.float32
            )
            key_grad = jnp.einsum(
                "vrw,vrf->vwf", weights, phi_query_b, preferred_element_type=jnp.float32
            )
            key_logit_grad = feature_grad(phi_key, key_grad)
            key_weight_grad = key_weight_grad + jnp.einsum(
                "vwd,vwe->vde", key_slab.astype(jnp.float32), key_logit_grad, precision=HIGHEST
            )
            return (query_grad, key_weight_grad)

        return lax.cond(jnp.any(visible), grads_compute_live, lambda current: current, running)

    def as_heads(pieces):
        return pieces.reshape(pieces.shape[0], key_heads, -1).transpose(1, 0, 2)

    row_zeros = jnp.zeros((key_heads, rows_all), jnp.float32)
    stats_init = (jnp.full((key_heads, rows_all), NEG_FLOOR, jnp.float32), row_zeros, row_zeros)
    grads_init = (
        jnp.zeros((key_heads, rows_all, 2 * HEAD_SIZE), jnp.float32),
        jnp.zeros((key_heads, HEAD_SIZE, HEAD_SIZE), jnp.float32),
    )
    highest, denominator, linear_sum = over_blocks(
        stats_init, (as_heads(lax.all_gather(local_k, "seq", axis=0, tiled=True)),), stats_step
    )
    query_grad, key_weight_grad = over_blocks(
        grads_init, (as_heads(lax.all_gather(local_k, "seq", axis=0, tiled=True)),), grads_step
    )
    query_logit_grad = feature_grad(phi_query, query_grad).reshape(
        key_heads, group_width, rows_local, HEAD_SIZE
    )
    query_weight_grad = jnp.einsum(
        "vgnd,vgne->vgde", query_wide, query_logit_grad, precision=HIGHEST
    ).reshape(key_heads * group_width, HEAD_SIZE, HEAD_SIZE)
    query_map_gradient, key_map_gradient = lax.psum((query_weight_grad, key_weight_grad), "seq")
    return (query_map_gradient, key_map_gradient)


NT = (((1,), (1,)), ((), ()))
F32 = jnp.float32
BF16 = jnp.bfloat16


def nn(left, right):
    return jnp.dot(left, right, preferred_element_type=F32)


def nt(left, right):
    return lax.dot_general(left, right, NT, preferred_element_type=F32)


def bf16_parts(value, count):
    parts = []
    for _ in range(count):
        part = value.astype(BF16)
        parts.append(part)
        value = value - part.astype(F32)
    return jnp.concatenate(parts, axis=0)


def features_t(logits):
    up = jnp.exp(logits - jnp.max(logits, axis=0, keepdims=True))
    down = jnp.exp(jnp.min(logits, axis=0, keepdims=True) - logits)
    up = up * (1.0 / jnp.sum(up, axis=0, keepdims=True))
    down = down * (1.0 / jnp.sum(down, axis=0, keepdims=True))
    return jnp.concatenate([up, down], axis=0)


def feature_grad_t(feature, upstream):
    halves = []
    for half in (slice(0, HEAD_SIZE), slice(HEAD_SIZE, 2 * HEAD_SIZE)):
        value, grad = feature[half], upstream[half]
        halves.append(value * (grad - jnp.sum(grad * value, axis=0, keepdims=True)))
    return halves[0] - halves[1]


def tile_sum(value):
    return jnp.sum(value.reshape(-1, 8, value.shape[-1]), axis=0)


def tile_max(value):
    return jnp.max(value.reshape(-1, 8, value.shape[-1]), axis=0)


def side_parts(value):
    high = value.astype(BF16)
    return jnp.concatenate([high, (value - high.astype(F32)).astype(BF16)], axis=1)


def map_parts(weights):
    rest = weights.T
    parts = []
    for _ in range(3):
        parts.append(rest.astype(BF16))
        rest = rest - parts[-1].astype(F32)
    return jnp.concatenate(parts[::-1], axis=1)


def logits_t(parts, tokens):
    return nt(parts, jnp.concatenate([tokens] * 3, axis=1))


def send_kernel(seq_count, head_count, key_heads, queries_ref, keys_ref, out_ref):
    rows = queries_ref.shape[0]
    share = seq_count // key_heads
    part = rows // share
    for head in range(head_count):
        for seq in range(seq_count):
            target = seq * head_count + head
            column = (head * seq_count + seq) * HEAD_SIZE
            out_ref[target, :rows, :] = queries_ref[:, column : column + HEAD_SIZE]
            column = (head * key_heads + seq // share) * HEAD_SIZE
            first = seq % share * part
            out_ref[target, rows:, :] = keys_ref[
                first : first + part, column : column + HEAD_SIZE
            ]


def query_kernel(rows, mine_ref, arrived_ref, query_map_ref, phi_ref, phi_b_ref):
    per_block = BLK // rows
    parts = map_parts(query_map_ref[mine_ref[0]])

    def block_logits(number):
        tokens = arrived_ref[number * per_block : (number + 1) * per_block, :rows, :]
        return logits_t(parts, tokens.reshape(BLK, HEAD_SIZE))

    blocks = phi_ref.shape[0]
    ahead = block_logits(0)
    for number in range(blocks):
        logits = ahead
        if number + 1 < blocks:
            ahead = block_logits(number + 1)
        feature = features_t(logits)
        phi_ref[number] = feature
        phi_b_ref[number] = feature.astype(BF16)


def pair_kernel(
    token_count,
    seq_blocks,
    rows,
    share,
    pos_ref,
    mine_ref,
    arrived_ref,
    *refs,
):
    key_refs, refs = refs[: share - 1], refs[share - 1 :]
    (
        key_map_ref,
        phi_q,
        phi_qb,
        out_ref,
        stored,
        key_rows,
        phi_k,
        phi_kb,
        phi_kb_rows,
        pair_weights,
        scores,
        linears,
        acc_q,
        acc_k,
    ) = refs
    per_block = BLK // rows
    part = rows // share
    sequences = token_count // (seq_blocks * BLK)
    for number in range(token_count // BLK):
        stored[pos_ref[number]] = number
    acc_q[...] = jnp.zeros_like(acc_q)
    acc_k[...] = jnp.zeros_like(acc_k)
    mine = mine_ref[0] % share
    parts = map_parts(key_map_ref[mine_ref[0] // share])
    lane = lax.broadcasted_iota(jnp.int32, (BLK, BLK), 1)
    sublane = lax.broadcasted_iota(jnp.int32, (BLK, BLK), 0)
    unit = jnp.where(lane == sublane, 1.0, 0.0).astype(BF16)
    visible = sublane <= lane
    exponent_scale = HEAD_SIZE ** (-0.5) * math.log2(math.e)

    def block(at):
        return slice(at * BLK, (at + 1) * BLK)

    def place(seq, at):
        return stored[seq * seq_blocks + at]

    def query_block(seq, at):
        first = place(seq, at) * per_block
        return arrived_ref[pl.ds(first, per_block), :rows, :].reshape(BLK, HEAD_SIZE)

    def key_logits(seq, at):
        first = place(seq, at) * per_block
        for chunk in range(per_block):
            for other in range(share):
                start = pl.multiple_of(
                    at * BLK + chunk * rows + (mine ^ other) * part, part
                )
                if other:
                    piece = key_refs[other - 1][first + chunk]
                else:
                    piece = arrived_ref[first + chunk, rows:, :]
                key_rows[seq, pl.ds(start, part), :] = piece
        return logits_t(parts, key_rows[seq, block(at), :])

    def key_features(seq, at, logits):
        feature = features_t(logits)
        phi_k[seq, :, block(at)] = feature
        rounded = feature.astype(BF16)
        phi_kb[seq, :, block(at)] = rounded
        phi_kb_rows[seq, block(at), :] = nt(unit, rounded).astype(BF16)

    def pair_scores(seq, at):
        live = (at + 1) * BLK
        slot = at % 2
        teacher = nt(key_rows[seq, :live, :], query_block(seq, at))
        student = nn(phi_kb_rows[seq, :live, :], phi_qb[place(seq, at)])
        highest = linear_sum = None
        for number in range(at + 1):
            here = block(number)
            score, linear = teacher[here], student[here]
            linears[seq, slot, here, :] = linear
            if number == at:
                score = jnp.where(visible, score, NEG_FLOOR)
                linear = jnp.where(visible, linear, 0.0)
            scores[seq, slot, here, :] = score
            top, total = tile_max(score), tile_sum(linear)
            highest = top if number == 0 else jnp.maximum(highest, top)
            linear_sum = total if number == 0 else linear_sum + total
        return (
            jnp.max(highest, axis=0, keepdims=True),
            jnp.sum(linear_sum, axis=0, keepdims=True),
        )

    def pair_gradients(seq, at, stats):
        highest, linear_sum = stats
        slot = at % 2
        denominator = None
        for number in range(at + 1):
            here = block(number)
            exponent = jnp.exp2((scores[seq, slot, here, :] - highest) * exponent_scale)
            scores[seq, slot, here, :] = exponent
            total = tile_sum(exponent)
            denominator = total if number == 0 else denominator + total
        denominator = jnp.sum(denominator, axis=0, keepdims=True)
        base = 1.0 / (linear_sum * token_count)
        rate = 1.0 / (denominator * token_count)
        for number in range(at + 1):
            here = block(number)
            weights = base - scores[seq, slot, here, :] * rate / linears[seq, slot, here, :]
            if number == at:
                weights = jnp.where(visible, weights, 0.0)
            pair_weights[seq, here, block(at)] = weights.astype(BF16)

    def query_grads(seq, at):
        live = (at + 1) * BLK
        upstream = nn(phi_kb[seq, :, :live], pair_weights[seq, :live, block(at)])
        change = side_parts(feature_grad_t(phi_q[place(seq, at)], upstream))
        tokens = query_block(seq, at)
        acc_q[...] += nn(change, jnp.concatenate([tokens, tokens], axis=0))

    def key_grads(seq, at):
        later = slice(at * BLK, seq_blocks * BLK)
        phi = jnp.concatenate(
            [phi_qb[place(seq, number)] for number in range(at, seq_blocks)], axis=1
        )
        upstream = nt(phi, pair_weights[seq, block(at), later])
        change = side_parts(feature_grad_t(phi_k[seq, :, block(at)], upstream))
        tokens = key_rows[seq, block(at), :]
        acc_k[...] += nn(change, jnp.concatenate([tokens, tokens], axis=0))

    def feature_steps(seq):
        ahead = key_logits(seq, 0)
        for at in range(seq_blocks):
            logits = ahead
            if at + 1 < seq_blocks:
                ahead = key_logits(seq, at + 1)
            key_features(seq, at, logits)
            yield

    def pair_steps(seq):
        ahead = pair_scores(seq, 0)
        for at in range(seq_blocks):
            stats = ahead
            if at + 1 < seq_blocks:
                ahead = pair_scores(seq, at + 1)
            pair_gradients(seq, at, stats)
            if at:
                query_grads(seq, at - 1)
            yield
        query_grads(seq, seq_blocks - 1)

    def key_steps(seq):
        for at in range(seq_blocks):
            key_grads(seq, at)
            yield

    stages = (feature_steps, pair_steps, key_steps)
    for turn in range(sequences + len(stages) - 1):
        active = [
            stage(turn - number)
            for number, stage in enumerate(stages)
            if 0 <= turn - number < sequences
        ]
        while active:
            for step in list(active):
                if next(step, step) is step:
                    active.remove(step)
    out_ref[:HEAD_SIZE, :] = acc_q[...].T.astype(BF16)
    out_ref[HEAD_SIZE:, :] = bf16_parts(acc_k[...].T, 2)


def per_device_head(queries, keys, block_pos, query_map, key_map):
    seq_count = lax.axis_size("seq")
    head_count = lax.axis_size("head")
    key_heads = key_map.shape[0]
    share = seq_count // key_heads
    rows = queries.shape[0]
    part = rows // share
    devices = seq_count * head_count
    token_count = rows * devices
    blocks = token_count // BLK
    seq_tokens = seq_count * BLK
    sequences = token_count // seq_tokens
    vmem = pl.BlockSpec(memory_space=pltpu.VMEM)
    smem = pl.BlockSpec(memory_space=pltpu.SMEM)
    sent = pl.pallas_call(
        functools.partial(send_kernel, seq_count, head_count, key_heads),
        out_shape=jax.ShapeDtypeStruct((devices, rows + part, HEAD_SIZE), BF16),
        compiler_params=pltpu.CompilerParams(vmem_limit_bytes=8 << 20),
    )(queries, keys)
    arrived = lax.all_to_all(sent, ("seq", "head"), split_axis=0, concat_axis=0, tiled=True)
    mine = lax.axis_index("seq").astype(jnp.int32).reshape(1)

    def swap(piece, bit):
        return lax.ppermute(piece, "seq", [(i, i ^ bit) for i in range(seq_count)])

    pieces = [arrived[:, rows:, :]]
    for other in range(1, share):
        bit = other & -other
        pieces.append(swap(pieces[other - bit], bit))
    phi, phi_b = pl.pallas_call(
        functools.partial(query_kernel, rows),
        out_shape=(
            jax.ShapeDtypeStruct((blocks, 2 * HEAD_SIZE, BLK), F32),
            jax.ShapeDtypeStruct((blocks, 2 * HEAD_SIZE, BLK), BF16),
        ),
        in_specs=[smem, vmem, vmem],
        out_specs=(vmem, vmem),
        compiler_params=pltpu.CompilerParams(vmem_limit_bytes=16 << 20),
        cost_estimate=pl.CostEstimate(
            flops=token_count * HEAD_SIZE * HEAD_SIZE * 6,
            bytes_accessed=token_count * HEAD_SIZE * 20,
            transcendentals=token_count * HEAD_SIZE * 2,
        ),
    )(mine, arrived, query_map)
    grads = pl.pallas_call(
        functools.partial(pair_kernel, token_count, seq_count, rows, share),
        out_shape=jax.ShapeDtypeStruct((3 * HEAD_SIZE, HEAD_SIZE), BF16),
        in_specs=[smem, smem] + [vmem] * (share + 3),
        out_specs=vmem,
        scratch_shapes=[
            pltpu.SMEM((blocks,), jnp.int32),
            pltpu.VMEM((sequences, seq_tokens, HEAD_SIZE), BF16),
            pltpu.VMEM((sequences, 2 * HEAD_SIZE, seq_tokens), F32),
            pltpu.VMEM((sequences, 2 * HEAD_SIZE, seq_tokens), BF16),
            pltpu.VMEM((sequences, seq_tokens, 2 * HEAD_SIZE), BF16),
            pltpu.VMEM((sequences, seq_tokens, seq_tokens), BF16),
            pltpu.VMEM((sequences, 2, seq_tokens, BLK), F32),
            pltpu.VMEM((sequences, 2, seq_tokens, BLK), F32),
            pltpu.VMEM((HEAD_SIZE, HEAD_SIZE), F32),
            pltpu.VMEM((HEAD_SIZE, HEAD_SIZE), F32),
        ],
        compiler_params=pltpu.CompilerParams(vmem_limit_bytes=32 << 20),
    )(block_pos, mine, arrived, *pieces[1:], key_map, phi, phi_b)
    everyone = lax.all_gather(grads, "seq", axis=0, tiled=False)
    everyone = everyone.reshape(seq_count, 3, HEAD_SIZE, HEAD_SIZE).astype(F32)
    key_sums = (everyone[:, 1] + everyone[:, 2]).reshape(
        key_heads, share, HEAD_SIZE, HEAD_SIZE
    )
    return everyone[:, 0], jnp.sum(key_sums, axis=1)


def per_device(queries, keys, block_pos, query_map, key_map):
    seq_count = lax.axis_size("seq")
    share = seq_count // key_map.shape[0]
    one_head_each = (
        query_map.shape[0] == seq_count
        and seq_count == share * key_map.shape[0]
        and share & (share - 1) == 0
        and BLK % queries.shape[0] == 0
        and queries.shape[0] % (16 * share) == 0
    )
    chosen = per_device_head if one_head_each else per_device_general
    return chosen(queries, keys, block_pos, query_map, key_map)


def solution(mesh):
    in_specs = (
        P(("seq", "head"), None),
        P(("seq", "head"), None),
        P(),
        P("head", None, None),
        P("head", None, None),
    )
    out_specs = (P("head", None, None), P("head", None, None))
    return jax.shard_map(
        per_device, mesh=mesh, in_specs=in_specs, out_specs=out_specs, check_vma=False
    )
```

```python
import functools
import math

import jax
import jax.numpy as jnp
from jax import lax
from jax.experimental import pallas as pl
from jax.experimental.pallas import tpu as pltpu
from jax.sharding import PartitionSpec as P

HEAD_SIZE = 128
BLK = 128

HIGHEST = lax.Precision.HIGHEST
NEG_FLOOR = -1e30


def softmax_pair(logits):
    return jnp.concatenate(
        [jax.nn.softmax(logits, axis=-1), jax.nn.softmax(-logits, axis=-1)], axis=-1
    )


def feature_grad(feature, upstream):
    half_width = feature.shape[-1] // 2
    positive, negative = (feature[..., :half_width], feature[..., half_width:])
    grad_positive, grad_negative = (upstream[..., :half_width], upstream[..., half_width:])
    first = positive * (grad_positive - jnp.sum(grad_positive * positive, axis=-1, keepdims=True))
    second = negative * (grad_negative - jnp.sum(grad_negative * negative, axis=-1, keepdims=True))
    return first - second


def row_places(row_index, block_pos, seq_count):
    stored = row_index // BLK
    lookup = stored[:, None] == jnp.arange(block_pos.shape[0], dtype=jnp.int32)[None, :]
    blocks = jnp.sum(jnp.where(lookup, block_pos[None, :], 0), axis=1)
    return (blocks // seq_count, blocks * BLK + row_index % BLK)


def over_blocks(running, portions, step_fn):
    row_count = portions[0].shape[1]
    step_rows = math.gcd(row_count, 512)

    def advance(number, inner_carry):
        slabs = tuple(
            (
                lax.dynamic_slice_in_dim(portion, number * step_rows, step_rows, 1)
                for portion in portions
            )
        )
        return step_fn(inner_carry, slabs, number * step_rows)

    return lax.fori_loop(0, row_count // step_rows, advance, running)


def per_device_general(queries, keys, block_pos, query_map, key_map):
    local_q, local_k = (
        lax.all_to_all(queries, "head", split_axis=1, concat_axis=0, tiled=True),
        lax.all_to_all(keys, "head", split_axis=1, concat_axis=0, tiled=True),
    )
    seq_count = lax.axis_size("seq")
    seq_rank = lax.axis_index("seq")
    rows_local = local_k.shape[0]
    token_count = rows_local * seq_count
    key_heads = key_map.shape[0]
    group_width = query_map.shape[0] // key_heads
    score_scale = HEAD_SIZE ** (-0.5)
    query_index = seq_rank * rows_local + jnp.arange(rows_local, dtype=jnp.int32)
    query_heads = local_q.reshape(rows_local, key_heads, group_width, HEAD_SIZE).transpose(
        1, 2, 0, 3
    )
    query_wide = query_heads.astype(jnp.float32)
    query_logits = jnp.einsum(
        "vgnd,vgde->vgne",
        query_wide,
        query_map.reshape(key_heads, group_width, HEAD_SIZE, HEAD_SIZE),
        precision=HIGHEST,
    )
    rows_all = group_width * rows_local
    phi_query = softmax_pair(query_logits).reshape(key_heads, rows_all, 2 * HEAD_SIZE)
    phi_query_b = phi_query.astype(jnp.bfloat16)
    query_flat = query_heads.reshape(key_heads, rows_all, HEAD_SIZE)
    query_seq, query_at = row_places(query_index, block_pos, seq_count)
    query_seq = jnp.tile(query_seq, group_width)
    query_at = jnp.tile(query_at, group_width)

    def visible_for(offset, slab_rows):
        key_index = offset + jnp.arange(slab_rows, dtype=jnp.int32)
        key_seq, key_at = row_places(key_index, block_pos, seq_count)
        return (key_seq[None, :] == query_seq[:, None]) & (key_at[None, :] <= query_at[:, None])

    def key_features(key_slab):
        logits = jnp.einsum(
            "vwd,vde->vwe", key_slab.astype(jnp.float32), key_map, precision=HIGHEST
        )
        return softmax_pair(logits)

    def teacher(key_slab):
        return (
            jnp.einsum("vrd,vwd->vrw", query_flat, key_slab, preferred_element_type=jnp.float32)
            * score_scale
        )

    def stats_step(running, slabs, offset):
        key_slab = slabs[0]
        visible = visible_for(offset, key_slab.shape[1])

        def stats_compute_live(current):
            highest, denominator, linear_sum = current
            masked = jnp.where(visible[None], teacher(key_slab), NEG_FLOOR)
            new_high = jnp.maximum(highest, jnp.max(masked, axis=-1))
            exponent = jnp.where(visible[None], jnp.exp(masked - new_high[..., None]), 0.0)
            denominator = denominator * jnp.exp(highest - new_high) + jnp.sum(exponent, axis=-1)
            phi_key_b = key_features(key_slab).astype(jnp.bfloat16)
            linear = jnp.einsum(
                "vrf,vwf->vrw", phi_query_b, phi_key_b, preferred_element_type=jnp.float32
            )
            linear_sum = linear_sum + jnp.sum(jnp.where(visible[None], linear, 0.0), axis=-1)
            return (new_high, denominator, linear_sum)

        return lax.cond(jnp.any(visible), stats_compute_live, lambda current: current, running)

    def grads_step(running, slabs, offset):
        key_slab = slabs[0]
        visible = visible_for(offset, key_slab.shape[1])

        def grads_compute_live(current):
            query_grad, key_weight_grad = current
            masked = jnp.where(visible[None], teacher(key_slab), NEG_FLOOR)
            exponent = jnp.where(visible[None], jnp.exp(masked - highest[..., None]), 0.0)
            teacher_prob = exponent / denominator[..., None]
            phi_key = key_features(key_slab)
            phi_key_b = phi_key.astype(jnp.bfloat16)
            linear = jnp.einsum(
                "vrf,vwf->vrw", phi_query_b, phi_key_b, preferred_element_type=jnp.float32
            )
            weights = (
                jnp.where(visible[None], 1.0 / linear_sum[..., None] - teacher_prob / linear, 0.0)
                / token_count
            ).astype(jnp.bfloat16)
            query_grad = query_grad + jnp.einsum(
                "vrw,vwf->vrf", weights, phi_key_b, preferred_element_type=jnp.float32
            )
            key_grad = jnp.einsum(
                "vrw,vrf->vwf", weights, phi_query_b, preferred_element_type=jnp.float32
            )
            key_logit_grad = feature_grad(phi_key, key_grad)
            key_weight_grad = key_weight_grad + jnp.einsum(
                "vwd,vwe->vde", key_slab.astype(jnp.float32), key_logit_grad, precision=HIGHEST
            )
            return (query_grad, key_weight_grad)

        return lax.cond(jnp.any(visible), grads_compute_live, lambda current: current, running)

    def as_heads(pieces):
        return pieces.reshape(pieces.shape[0], key_heads, -1).transpose(1, 0, 2)

    row_zeros = jnp.zeros((key_heads, rows_all), jnp.float32)
    stats_init = (jnp.full((key_heads, rows_all), NEG_FLOOR, jnp.float32), row_zeros, row_zeros)
    grads_init = (
        jnp.zeros((key_heads, rows_all, 2 * HEAD_SIZE), jnp.float32),
        jnp.zeros((key_heads, HEAD_SIZE, HEAD_SIZE), jnp.float32),
    )
    highest, denominator, linear_sum = over_blocks(
        stats_init, (as_heads(lax.all_gather(local_k, "seq", axis=0, tiled=True)),), stats_step
    )
    query_grad, key_weight_grad = over_blocks(
        grads_init, (as_heads(lax.all_gather(local_k, "seq", axis=0, tiled=True)),), grads_step
    )
    query_logit_grad = feature_grad(phi_query, query_grad).reshape(
        key_heads, group_width, rows_local, HEAD_SIZE
    )
    query_weight_grad = jnp.einsum(
        "vgnd,vgne->vgde", query_wide, query_logit_grad, precision=HIGHEST
    ).reshape(key_heads * group_width, HEAD_SIZE, HEAD_SIZE)
    query_map_gradient, key_map_gradient = lax.psum((query_weight_grad, key_weight_grad), "seq")
    return (query_map_gradient, key_map_gradient)


NT = (((1,), (1,)), ((), ()))
F32 = jnp.float32
BF16 = jnp.bfloat16


def nn(left, right):
    return jnp.dot(left, right, preferred_element_type=F32)


def nt(left, right):
    return lax.dot_general(left, right, NT, preferred_element_type=F32)


def bf16_parts(value, count):
    parts = []
    for _ in range(count):
        part = value.astype(BF16)
        parts.append(part)
        value = value - part.astype(F32)
    return jnp.concatenate(parts, axis=0)


def features_t(logits):
    up = jnp.exp(logits - jnp.max(logits, axis=0, keepdims=True))
    down = jnp.exp(jnp.min(logits, axis=0, keepdims=True) - logits)
    up = up * (1.0 / jnp.sum(up, axis=0, keepdims=True))
    down = down * (1.0 / jnp.sum(down, axis=0, keepdims=True))
    return jnp.concatenate([up, down], axis=0)


def feature_grad_t(feature, upstream):
    halves = []
    for half in (slice(0, HEAD_SIZE), slice(HEAD_SIZE, 2 * HEAD_SIZE)):
        value, grad = feature[half], upstream[half]
        halves.append(value * (grad - jnp.sum(grad * value, axis=0, keepdims=True)))
    return halves[0] - halves[1]


def tile_sum(value):
    return jnp.sum(value.reshape(-1, 8, value.shape[-1]), axis=0)


def tile_max(value):
    return jnp.max(value.reshape(-1, 8, value.shape[-1]), axis=0)


def side_parts(value):
    high = value.astype(BF16)
    return jnp.concatenate([high, (value - high.astype(F32)).astype(BF16)], axis=1)


def map_parts(weights):
    rest = weights.T
    parts = []
    for _ in range(3):
        parts.append(rest.astype(BF16))
        rest = rest - parts[-1].astype(F32)
    return jnp.concatenate(parts[::-1], axis=1)


def logits_t(parts, tokens):
    return nt(parts, jnp.concatenate([tokens] * 3, axis=1))


def send_kernel(seq_count, head_count, key_heads, queries_ref, keys_ref, out_ref, sems):
    rows = queries_ref.shape[0]
    share = seq_count // key_heads
    part = rows // share
    copies = []
    for head in range(head_count):
        for seq in range(seq_count):
            target = seq * head_count + head
            column = (head * seq_count + seq) * HEAD_SIZE
            copies.append(
                pltpu.make_async_copy(
                    queries_ref.at[:, column : column + HEAD_SIZE],
                    out_ref.at[target, :rows, :],
                    sems.at[0, target],
                )
            )
            column = (head * key_heads + seq // share) * HEAD_SIZE
            first = seq % share * part
            copies.append(
                pltpu.make_async_copy(
                    keys_ref.at[first : first + part, column : column + HEAD_SIZE],
                    out_ref.at[target, rows:, :],
                    sems.at[1, target],
                )
            )
    for copy in copies:
        copy.start()
    for copy in copies:
        copy.wait()


def query_kernel(rows, mine_ref, arrived_ref, query_map_ref, phi_ref):
    per_block = BLK // rows
    parts = map_parts(query_map_ref[mine_ref[0]])

    def block_logits(number):
        tokens = arrived_ref[number * per_block : (number + 1) * per_block, :rows, :]
        return logits_t(parts, tokens.reshape(BLK, HEAD_SIZE))

    blocks = phi_ref.shape[0]
    ahead = block_logits(0)
    for number in range(blocks):
        logits = ahead
        if number + 1 < blocks:
            ahead = block_logits(number + 1)
        phi_ref[number] = features_t(logits)


def pair_kernel(
    token_count,
    seq_blocks,
    rows,
    share,
    pos_ref,
    mine_ref,
    arrived_ref,
    *refs,
):
    key_refs, refs = refs[: share - 1], refs[share - 1 :]
    (
        key_map_ref,
        phi_q,
        out_ref,
        stored,
        key_rows,
        query_rows,
        phi_qb,
        phi_k,
        phi_kb,
        phi_kb_rows,
        pair_weights,
        scores,
        linears,
        acc_q,
        acc_k,
    ) = refs
    per_block = BLK // rows
    part = rows // share
    sequences = token_count // (seq_blocks * BLK)
    for number in range(token_count // BLK):
        stored[pos_ref[number]] = number
    acc_q[...] = jnp.zeros_like(acc_q)
    acc_k[...] = jnp.zeros_like(acc_k)
    width = 2 if seq_blocks % 2 == 0 else 1
    tiles = seq_blocks // width
    for seq in range(sequences):
        for at in range(0, seq_blocks, width):
            if width > 1:
                pair_weights[seq, (at + 1) * BLK : (at + 2) * BLK, at * BLK : (at + 1) * BLK] = (
                    jnp.zeros((BLK, BLK), BF16)
                )
    mine = mine_ref[0] % share
    parts = map_parts(key_map_ref[mine_ref[0] // share])
    lane = lax.broadcasted_iota(jnp.int32, (BLK, BLK), 1)
    sublane = lax.broadcasted_iota(jnp.int32, (BLK, BLK), 0)
    unit = jnp.where(lane == sublane, 1.0, 0.0).astype(BF16)
    visible = sublane <= lane
    exponent_scale = HEAD_SIZE ** (-0.5) * math.log2(math.e)

    def block(at):
        return slice(at * BLK, (at + 1) * BLK)

    def span(tile):
        return slice(tile * width * BLK, (tile + 1) * width * BLK)

    def place(seq, at):
        return stored[seq * seq_blocks + at]

    def load_queries(seq, at):
        first = place(seq, at) * per_block
        tokens = arrived_ref[pl.ds(first, per_block), :rows, :]
        query_rows[seq, block(at), :] = tokens.reshape(BLK, HEAD_SIZE)
        phi_qb[seq, :, block(at)] = phi_q[place(seq, at)].astype(BF16)

    def load_keys(seq, at):
        first = place(seq, at) * per_block
        for chunk in range(per_block):
            for other in range(share):
                start = pl.multiple_of(
                    at * BLK + chunk * rows + (mine ^ other) * part, part
                )
                if other:
                    piece = key_refs[other - 1][first + chunk]
                else:
                    piece = arrived_ref[first + chunk, rows:, :]
                key_rows[seq, pl.ds(start, part), :] = piece

    def key_logits(seq, at):
        return logits_t(parts, key_rows[seq, block(at), :])

    def key_features(seq, at, logits):
        feature = features_t(logits)
        phi_k[seq, :, block(at)] = feature
        phi_kb[seq, :, block(at)] = feature.astype(BF16)

    def turn_features(seq, at):
        phi_kb_rows[seq, block(at), :] = nt(unit, phi_kb[seq, :, block(at)]).astype(BF16)

    def pair_scores(seq, tile):
        here = span(tile)
        slot = tile % 2
        teacher = nt(key_rows[seq, : here.stop, :], query_rows[seq, here, :])
        student = nn(phi_kb_rows[seq, : here.stop, :], phi_qb[seq, :, here])
        stats = []
        for half in range(width):
            at = tile * width + half
            highest = linear_sum = None
            for number in range(at + 1):
                score = teacher[block(number), block(half)]
                linear = student[block(number), block(half)]
                linears[seq, slot, block(number), block(half)] = linear
                if number == at:
                    score = jnp.where(visible, score, NEG_FLOOR)
                    linear = jnp.where(visible, linear, 0.0)
                scores[seq, slot, block(number), block(half)] = score
                top, total = tile_max(score), tile_sum(linear)
                highest = top if number == 0 else jnp.maximum(highest, top)
                linear_sum = total if number == 0 else linear_sum + total
            stats.append(
                (
                    jnp.max(highest, axis=0, keepdims=True),
                    jnp.sum(linear_sum, axis=0, keepdims=True),
                )
            )
        return stats

    def pair_gradients(seq, tile, half, stats):
        highest, linear_sum = stats
        slot = tile % 2
        at = tile * width + half
        denominator = None
        for number in range(at + 1):
            score = scores[seq, slot, block(number), block(half)]
            exponent = jnp.exp2((score - highest) * exponent_scale)
            scores[seq, slot, block(number), block(half)] = exponent
            total = tile_sum(exponent)
            denominator = total if number == 0 else denominator + total
        denominator = jnp.sum(denominator, axis=0, keepdims=True)
        base = 1.0 / (linear_sum * token_count)
        rate = 1.0 / (denominator * token_count)
        for number in range(at + 1):
            exponent = scores[seq, slot, block(number), block(half)]
            weights = base - exponent * rate / linears[seq, slot, block(number), block(half)]
            if number == at:
                weights = jnp.where(visible, weights, 0.0)
            pair_weights[seq, block(number), block(at)] = weights.astype(BF16)

    def map_change(phis, upstream, tokens):
        changes = [
            side_parts(feature_grad_t(phi, upstream[:, block(half)]))
            for half, phi in enumerate(phis)
        ]
        twice = [tokens[block(half)] for half in range(width) for _ in range(2)]
        return nn(jnp.concatenate(changes, axis=1), jnp.concatenate(twice, axis=0))

    def query_upstream(seq, tile):
        here = span(tile)
        return nn(phi_kb[seq, :, : here.stop], pair_weights[seq, : here.stop, here])

    def query_change(seq, tile, upstream):
        phis = [phi_q[place(seq, tile * width + half)] for half in range(width)]
        acc_q[...] += map_change(phis, upstream, query_rows[seq, span(tile), :])

    def key_upstream(seq, tile):
        later = slice(tile * width * BLK, seq_blocks * BLK)
        return nt(phi_qb[seq, :, later], pair_weights[seq, span(tile), later])

    def key_change(seq, tile, upstream):
        phis = [phi_k[seq, :, block(tile * width + half)] for half in range(width)]
        acc_k[...] += map_change(phis, upstream, key_rows[seq, span(tile), :])

    def feature_steps(seq):
        ahead = [key_logits(seq, at) for at in range(min(3, seq_blocks))]
        for at in range(seq_blocks):
            if at + len(ahead) < seq_blocks:
                ahead.append(key_logits(seq, at + len(ahead)))
            key_features(seq, at, ahead.pop(0))
            if at > 1:
                turn_features(seq, at - 2)
            yield
        for at in range(max(seq_blocks - 2, 0), seq_blocks):
            turn_features(seq, at)

    def pair_steps(seq):
        ahead = pair_scores(seq, 0)
        behind = None
        for tile in range(tiles):
            stats = ahead
            if tile + 1 < tiles:
                ahead = pair_scores(seq, tile + 1)
            for half in range(width):
                pair_gradients(seq, tile, half, stats[half])
                yield
            upstream = query_upstream(seq, tile)
            if tile:
                query_change(seq, tile - 1, behind)
            behind = upstream
        yield
        query_change(seq, tiles - 1, behind)

    def key_steps(seq):
        ahead = key_upstream(seq, 0)
        yield
        for tile in range(tiles):
            upstream = ahead
            if tile + 1 < tiles:
                ahead = key_upstream(seq, tile + 1)
            key_change(seq, tile, upstream)
            yield

    for seq in range(sequences):
        for at in range(seq_blocks):
            load_keys(seq, at)
            load_queries(seq, at)
    stages = (feature_steps, pair_steps, key_steps)
    for turn in range(sequences + len(stages) - 1):
        active = [
            stage(turn - number)
            for number, stage in enumerate(stages)
            if 0 <= turn - number < sequences
        ]
        while active:
            for step in list(active):
                if next(step, step) is step:
                    active.remove(step)
    out_ref[:HEAD_SIZE, :] = acc_q[...].T.astype(BF16)
    out_ref[HEAD_SIZE:, :] = bf16_parts(acc_k[...].T, 2)


def per_device_head(queries, keys, block_pos, query_map, key_map):
    seq_count = lax.axis_size("seq")
    head_count = lax.axis_size("head")
    key_heads = key_map.shape[0]
    share = seq_count // key_heads
    rows = queries.shape[0]
    part = rows // share
    devices = seq_count * head_count
    token_count = rows * devices
    blocks = token_count // BLK
    seq_tokens = seq_count * BLK
    sequences = token_count // seq_tokens
    vmem = pl.BlockSpec(memory_space=pltpu.VMEM)
    smem = pl.BlockSpec(memory_space=pltpu.SMEM)
    sent = pl.pallas_call(
        functools.partial(send_kernel, seq_count, head_count, key_heads),
        out_shape=jax.ShapeDtypeStruct((devices, rows + part, HEAD_SIZE), BF16),
        in_specs=[pl.BlockSpec(memory_space=pltpu.HBM)] * 2,
        out_specs=vmem,
        scratch_shapes=[pltpu.SemaphoreType.DMA((2, devices))],
        compiler_params=pltpu.CompilerParams(vmem_limit_bytes=60 << 20),
    )(queries, keys)
    arrived = lax.all_to_all(sent, ("seq", "head"), split_axis=0, concat_axis=0, tiled=True)
    mine = lax.axis_index("seq").astype(jnp.int32).reshape(1)

    def swap(piece, bit):
        return lax.ppermute(piece, "seq", [(i, i ^ bit) for i in range(seq_count)])

    phi = pl.pallas_call(
        functools.partial(query_kernel, rows),
        out_shape=jax.ShapeDtypeStruct((blocks, 2 * HEAD_SIZE, BLK), F32),
        in_specs=[smem, vmem, vmem],
        out_specs=vmem,
        compiler_params=pltpu.CompilerParams(vmem_limit_bytes=16 << 20),
        cost_estimate=pl.CostEstimate(
            flops=token_count * HEAD_SIZE * HEAD_SIZE * 6,
            bytes_accessed=token_count * HEAD_SIZE * 20,
            transcendentals=token_count * HEAD_SIZE * 2,
        ),
    )(mine, arrived, query_map)
    pieces = {0: arrived[:, rows:, :]}
    for number in range(share.bit_length() - 1):
        bit = share >> (number + 1)
        if number and number == share.bit_length() - 2:
            pieces, phi = lax.optimization_barrier((pieces, phi))
        pieces |= {other + bit: swap(piece, bit) for other, piece in pieces.items()}
    pieces = [pieces[other] for other in range(share)]
    grads = pl.pallas_call(
        functools.partial(pair_kernel, token_count, seq_count, rows, share),
        out_shape=jax.ShapeDtypeStruct((3 * HEAD_SIZE, HEAD_SIZE), BF16),
        in_specs=[smem, smem] + [vmem] * (share + 2),
        out_specs=vmem,
        scratch_shapes=[
            pltpu.SMEM((blocks,), jnp.int32),
            pltpu.VMEM((sequences, seq_tokens, HEAD_SIZE), BF16),
            pltpu.VMEM((sequences, seq_tokens, HEAD_SIZE), BF16),
            pltpu.VMEM((sequences, 2 * HEAD_SIZE, seq_tokens), BF16),
            pltpu.VMEM((sequences, 2 * HEAD_SIZE, seq_tokens), F32),
            pltpu.VMEM((sequences, 2 * HEAD_SIZE, seq_tokens), BF16),
            pltpu.VMEM((sequences, seq_tokens, 2 * HEAD_SIZE), BF16),
            pltpu.VMEM((sequences, seq_tokens, seq_tokens), BF16),
            pltpu.VMEM((sequences, 2, seq_tokens, 2 * BLK), F32),
            pltpu.VMEM((sequences, 2, seq_tokens, 2 * BLK), F32),
            pltpu.VMEM((HEAD_SIZE, HEAD_SIZE), F32),
            pltpu.VMEM((HEAD_SIZE, HEAD_SIZE), F32),
        ],
        compiler_params=pltpu.CompilerParams(vmem_limit_bytes=32 << 20),
    )(block_pos, mine, arrived, *pieces[1:], key_map, phi)
    everyone = lax.all_gather(grads, "seq", axis=0, tiled=False)
    everyone = everyone.reshape(seq_count, 3, HEAD_SIZE, HEAD_SIZE).astype(F32)
    key_sums = (everyone[:, 1] + everyone[:, 2]).reshape(
        key_heads, share, HEAD_SIZE, HEAD_SIZE
    )
    return everyone[:, 0], jnp.sum(key_sums, axis=1)


def per_device(queries, keys, block_pos, query_map, key_map):
    seq_count = lax.axis_size("seq")
    share = seq_count // key_map.shape[0]
    one_head_each = (
        query_map.shape[0] == seq_count
        and seq_count == share * key_map.shape[0]
        and share & (share - 1) == 0
        and BLK % queries.shape[0] == 0
        and queries.shape[0] % (16 * share) == 0
    )
    chosen = per_device_head if one_head_each else per_device_general
    return chosen(queries, keys, block_pos, query_map, key_map)


def solution(mesh):
    in_specs = (
        P(("seq", "head"), None),
        P(("seq", "head"), None),
        P(),
        P("head", None, None),
        P("head", None, None),
    )
    out_specs = (P("head", None, None), P("head", None, None))
    return jax.shard_map(
        per_device, mesh=mesh, in_specs=in_specs, out_specs=out_specs, check_vma=False
    )
```

```python
import functools
import math

import jax
import jax.numpy as jnp
from jax import lax
from jax.experimental import pallas as pl
from jax.experimental.pallas import tpu as pltpu
from jax.sharding import PartitionSpec as P

HEAD_SIZE = 128
BLK = 128

HIGHEST = lax.Precision.HIGHEST
NEG_FLOOR = -1e30


def softmax_pair(logits):
    return jnp.concatenate(
        [jax.nn.softmax(logits, axis=-1), jax.nn.softmax(-logits, axis=-1)], axis=-1
    )


def feature_grad(feature, upstream):
    half_width = feature.shape[-1] // 2
    positive, negative = (feature[..., :half_width], feature[..., half_width:])
    grad_positive, grad_negative = (upstream[..., :half_width], upstream[..., half_width:])
    first = positive * (grad_positive - jnp.sum(grad_positive * positive, axis=-1, keepdims=True))
    second = negative * (grad_negative - jnp.sum(grad_negative * negative, axis=-1, keepdims=True))
    return first - second


def row_places(row_index, block_pos, seq_count):
    stored = row_index // BLK
    lookup = stored[:, None] == jnp.arange(block_pos.shape[0], dtype=jnp.int32)[None, :]
    blocks = jnp.sum(jnp.where(lookup, block_pos[None, :], 0), axis=1)
    return (blocks // seq_count, blocks * BLK + row_index % BLK)


def over_blocks(running, portions, step_fn):
    row_count = portions[0].shape[1]
    step_rows = math.gcd(row_count, 512)

    def advance(number, inner_carry):
        slabs = tuple(
            (
                lax.dynamic_slice_in_dim(portion, number * step_rows, step_rows, 1)
                for portion in portions
            )
        )
        return step_fn(inner_carry, slabs, number * step_rows)

    return lax.fori_loop(0, row_count // step_rows, advance, running)


def per_device_general(queries, keys, block_pos, query_map, key_map):
    local_q, local_k = (
        lax.all_to_all(queries, "head", split_axis=1, concat_axis=0, tiled=True),
        lax.all_to_all(keys, "head", split_axis=1, concat_axis=0, tiled=True),
    )
    seq_count = lax.axis_size("seq")
    seq_rank = lax.axis_index("seq")
    rows_local = local_k.shape[0]
    token_count = rows_local * seq_count
    key_heads = key_map.shape[0]
    group_width = query_map.shape[0] // key_heads
    score_scale = HEAD_SIZE ** (-0.5)
    query_index = seq_rank * rows_local + jnp.arange(rows_local, dtype=jnp.int32)
    query_heads = local_q.reshape(rows_local, key_heads, group_width, HEAD_SIZE).transpose(
        1, 2, 0, 3
    )
    query_wide = query_heads.astype(jnp.float32)
    query_logits = jnp.einsum(
        "vgnd,vgde->vgne",
        query_wide,
        query_map.reshape(key_heads, group_width, HEAD_SIZE, HEAD_SIZE),
        precision=HIGHEST,
    )
    rows_all = group_width * rows_local
    phi_query = softmax_pair(query_logits).reshape(key_heads, rows_all, 2 * HEAD_SIZE)
    phi_query_b = phi_query.astype(jnp.bfloat16)
    query_flat = query_heads.reshape(key_heads, rows_all, HEAD_SIZE)
    query_seq, query_at = row_places(query_index, block_pos, seq_count)
    query_seq = jnp.tile(query_seq, group_width)
    query_at = jnp.tile(query_at, group_width)

    def visible_for(offset, slab_rows):
        key_index = offset + jnp.arange(slab_rows, dtype=jnp.int32)
        key_seq, key_at = row_places(key_index, block_pos, seq_count)
        return (key_seq[None, :] == query_seq[:, None]) & (key_at[None, :] <= query_at[:, None])

    def key_features(key_slab):
        logits = jnp.einsum(
            "vwd,vde->vwe", key_slab.astype(jnp.float32), key_map, precision=HIGHEST
        )
        return softmax_pair(logits)

    def teacher(key_slab):
        return (
            jnp.einsum("vrd,vwd->vrw", query_flat, key_slab, preferred_element_type=jnp.float32)
            * score_scale
        )

    def stats_step(running, slabs, offset):
        key_slab = slabs[0]
        visible = visible_for(offset, key_slab.shape[1])

        def stats_compute_live(current):
            highest, denominator, linear_sum = current
            masked = jnp.where(visible[None], teacher(key_slab), NEG_FLOOR)
            new_high = jnp.maximum(highest, jnp.max(masked, axis=-1))
            exponent = jnp.where(visible[None], jnp.exp(masked - new_high[..., None]), 0.0)
            denominator = denominator * jnp.exp(highest - new_high) + jnp.sum(exponent, axis=-1)
            phi_key_b = key_features(key_slab).astype(jnp.bfloat16)
            linear = jnp.einsum(
                "vrf,vwf->vrw", phi_query_b, phi_key_b, preferred_element_type=jnp.float32
            )
            linear_sum = linear_sum + jnp.sum(jnp.where(visible[None], linear, 0.0), axis=-1)
            return (new_high, denominator, linear_sum)

        return lax.cond(jnp.any(visible), stats_compute_live, lambda current: current, running)

    def grads_step(running, slabs, offset):
        key_slab = slabs[0]
        visible = visible_for(offset, key_slab.shape[1])

        def grads_compute_live(current):
            query_grad, key_weight_grad = current
            masked = jnp.where(visible[None], teacher(key_slab), NEG_FLOOR)
            exponent = jnp.where(visible[None], jnp.exp(masked - highest[..., None]), 0.0)
            teacher_prob = exponent / denominator[..., None]
            phi_key = key_features(key_slab)
            phi_key_b = phi_key.astype(jnp.bfloat16)
            linear = jnp.einsum(
                "vrf,vwf->vrw", phi_query_b, phi_key_b, preferred_element_type=jnp.float32
            )
            weights = (
                jnp.where(visible[None], 1.0 / linear_sum[..., None] - teacher_prob / linear, 0.0)
                / token_count
            ).astype(jnp.bfloat16)
            query_grad = query_grad + jnp.einsum(
                "vrw,vwf->vrf", weights, phi_key_b, preferred_element_type=jnp.float32
            )
            key_grad = jnp.einsum(
                "vrw,vrf->vwf", weights, phi_query_b, preferred_element_type=jnp.float32
            )
            key_logit_grad = feature_grad(phi_key, key_grad)
            key_weight_grad = key_weight_grad + jnp.einsum(
                "vwd,vwe->vde", key_slab.astype(jnp.float32), key_logit_grad, precision=HIGHEST
            )
            return (query_grad, key_weight_grad)

        return lax.cond(jnp.any(visible), grads_compute_live, lambda current: current, running)

    def as_heads(pieces):
        return pieces.reshape(pieces.shape[0], key_heads, -1).transpose(1, 0, 2)

    row_zeros = jnp.zeros((key_heads, rows_all), jnp.float32)
    stats_init = (jnp.full((key_heads, rows_all), NEG_FLOOR, jnp.float32), row_zeros, row_zeros)
    grads_init = (
        jnp.zeros((key_heads, rows_all, 2 * HEAD_SIZE), jnp.float32),
        jnp.zeros((key_heads, HEAD_SIZE, HEAD_SIZE), jnp.float32),
    )
    highest, denominator, linear_sum = over_blocks(
        stats_init, (as_heads(lax.all_gather(local_k, "seq", axis=0, tiled=True)),), stats_step
    )
    query_grad, key_weight_grad = over_blocks(
        grads_init, (as_heads(lax.all_gather(local_k, "seq", axis=0, tiled=True)),), grads_step
    )
    query_logit_grad = feature_grad(phi_query, query_grad).reshape(
        key_heads, group_width, rows_local, HEAD_SIZE
    )
    query_weight_grad = jnp.einsum(
        "vgnd,vgne->vgde", query_wide, query_logit_grad, precision=HIGHEST
    ).reshape(key_heads * group_width, HEAD_SIZE, HEAD_SIZE)
    query_map_gradient, key_map_gradient = lax.psum((query_weight_grad, key_weight_grad), "seq")
    return (query_map_gradient, key_map_gradient)


NT = (((1,), (1,)), ((), ()))
F32 = jnp.float32
BF16 = jnp.bfloat16


def nn(left, right):
    return jnp.dot(left, right, preferred_element_type=F32)


def nt(left, right):
    return lax.dot_general(left, right, NT, preferred_element_type=F32)


def bf16_parts(value, count):
    parts = []
    for _ in range(count):
        part = value.astype(BF16)
        parts.append(part)
        value = value - part.astype(F32)
    return jnp.concatenate(parts, axis=0)


def features_t(logits):
    up = jnp.exp(logits - jnp.max(logits, axis=0, keepdims=True))
    down = jnp.exp(jnp.min(logits, axis=0, keepdims=True) - logits)
    up = up * (1.0 / jnp.sum(up, axis=0, keepdims=True))
    down = down * (1.0 / jnp.sum(down, axis=0, keepdims=True))
    return jnp.concatenate([up, down], axis=0)


def feature_grad_t(feature, upstream):
    halves = []
    for half in (slice(0, HEAD_SIZE), slice(HEAD_SIZE, 2 * HEAD_SIZE)):
        value, grad = feature[half], upstream[half]
        halves.append(value * (grad - jnp.sum(grad * value, axis=0, keepdims=True)))
    return halves[0] - halves[1]


def tile_sum(value):
    return jnp.sum(value.reshape(-1, 8, value.shape[-1]), axis=0)


def tile_max(value):
    return jnp.max(value.reshape(-1, 8, value.shape[-1]), axis=0)


def side_parts(value):
    high = value.astype(BF16)
    return jnp.concatenate([high, (value - high.astype(F32)).astype(BF16)], axis=1)


def map_parts(weights):
    rest = weights.T
    parts = []
    for _ in range(3):
        parts.append(rest.astype(BF16))
        rest = rest - parts[-1].astype(F32)
    return jnp.concatenate(parts[::-1], axis=1)


def logits_t(parts, tokens):
    return nt(parts, jnp.concatenate([tokens] * 3, axis=1))


def send_kernel(
    seq_count, head_count, key_heads, spread, queries_ref, keys_ref, out_ref, buffer, sems
):
    rows = queries_ref.shape[0]
    share = seq_count // key_heads
    part = rows // spread
    arriving, leaving = [], []
    for head in range(head_count):
        for seq in range(seq_count):
            target = seq * head_count + head
            column = (head * seq_count + seq) * HEAD_SIZE
            query_copy = pltpu.make_async_copy(
                queries_ref.at[:, column : column + HEAD_SIZE],
                buffer.at[target, :rows, :],
                sems.at[0, target],
            )
            column = (head * key_heads + seq // share) * HEAD_SIZE
            first = seq % spread * part
            key_copy = pltpu.make_async_copy(
                keys_ref.at[first : first + part, column : column + HEAD_SIZE],
                buffer.at[target, rows:, :],
                sems.at[1, target],
            )
            query_copy.start()
            key_copy.start()
            arriving.append((query_copy, key_copy))
            leaving.append(
                pltpu.make_async_copy(buffer.at[target], out_ref.at[target], sems.at[2, target])
            )
    for copies, copy in zip(arriving, leaving):
        for earlier in copies:
            earlier.wait()
        copy.start()
    for copy in leaving:
        copy.wait()


def query_kernel(rows, arrived_ref, query_map_ref, phi_ref):
    per_block = BLK // rows
    parts = map_parts(query_map_ref[lax.axis_index("seq")])

    def block_logits(number):
        tokens = arrived_ref[number * per_block : (number + 1) * per_block, :rows, :]
        return logits_t(parts, tokens.reshape(BLK, HEAD_SIZE))

    blocks = phi_ref.shape[0]
    ahead = block_logits(0)
    for number in range(blocks):
        logits = ahead
        if number + 1 < blocks:
            ahead = block_logits(number + 1)
        phi_ref[number] = features_t(logits)


def pair_kernel(
    token_count,
    seq_blocks,
    rows,
    share,
    spread,
    pos_ref,
    arrived_ref,
    *refs,
):
    key_refs, refs = refs[: spread - 1], refs[spread - 1 :]
    (
        key_map_ref,
        phi_q,
        out_ref,
        stored,
        key_rows,
        query_rows,
        phi_qb,
        phi_k,
        phi_kb,
        phi_kb_rows,
        pair_weights,
        scores,
        linears,
        acc_q,
        acc_k,
    ) = refs
    per_block = BLK // rows
    part = rows // spread
    sequences = token_count // (seq_blocks * BLK)
    for number in range(token_count // BLK):
        stored[pos_ref[number]] = number
    acc_q[...] = jnp.zeros_like(acc_q)
    acc_k[...] = jnp.zeros_like(acc_k)
    width = 2 if seq_blocks % 2 == 0 else 1
    tiles = seq_blocks // width
    for seq in range(sequences):
        for at in range(0, seq_blocks, width):
            if width > 1:
                pair_weights[seq, (at + 1) * BLK : (at + 2) * BLK, at * BLK : (at + 1) * BLK] = (
                    jnp.zeros((BLK, BLK), BF16)
                )
    mine = lax.axis_index("seq")
    parts = map_parts(key_map_ref[lax.div(mine, share)])
    mine = lax.rem(mine, spread)
    lane = lax.broadcasted_iota(jnp.int32, (BLK, BLK), 1)
    sublane = lax.broadcasted_iota(jnp.int32, (BLK, BLK), 0)
    unit = jnp.where(lane == sublane, 1.0, 0.0).astype(BF16)
    visible = sublane <= lane
    exponent_scale = HEAD_SIZE ** (-0.5) * math.log2(math.e)

    def block(at):
        return slice(at * BLK, (at + 1) * BLK)

    def span(tile):
        return slice(tile * width * BLK, (tile + 1) * width * BLK)

    def place(seq, at):
        return stored[seq * seq_blocks + at]

    def load_queries(seq, at):
        first = place(seq, at) * per_block
        tokens = arrived_ref[pl.ds(first, per_block), :rows, :]
        query_rows[seq, block(at), :] = tokens.reshape(BLK, HEAD_SIZE)
        phi_qb[seq, :, block(at)] = phi_q[place(seq, at)].astype(BF16)

    def load_keys(seq, at):
        first = place(seq, at) * per_block
        for chunk in range(per_block):
            for other in range(spread):
                start = pl.multiple_of(
                    at * BLK + chunk * rows + (mine ^ other) * part, part
                )
                if other:
                    piece = key_refs[other - 1][first + chunk]
                else:
                    piece = arrived_ref[first + chunk, rows:, :]
                key_rows[seq, pl.ds(start, part), :] = piece

    def key_logits(seq, at):
        return logits_t(parts, key_rows[seq, block(at), :])

    def key_features(seq, at, logits):
        feature = features_t(logits)
        phi_k[seq, :, block(at)] = feature
        phi_kb[seq, :, block(at)] = feature.astype(BF16)

    def turn_features(seq, at):
        phi_kb_rows[seq, block(at), :] = nt(unit, phi_kb[seq, :, block(at)]).astype(BF16)

    def pair_scores(seq, tile):
        here = span(tile)
        slot = tile % 2
        teacher = nt(key_rows[seq, : here.stop, :], query_rows[seq, here, :])
        student = nn(phi_kb_rows[seq, : here.stop, :], phi_qb[seq, :, here])
        stats = []
        for half in range(width):
            at = tile * width + half
            highest = linear_sum = None
            for number in range(at + 1):
                score = teacher[block(number), block(half)]
                linear = student[block(number), block(half)]
                linears[seq, slot, block(number), block(half)] = linear
                if number == at:
                    score = jnp.where(visible, score, NEG_FLOOR)
                    linear = jnp.where(visible, linear, 0.0)
                scores[seq, slot, block(number), block(half)] = score
                top, total = tile_max(score), tile_sum(linear)
                highest = top if number == 0 else jnp.maximum(highest, top)
                linear_sum = total if number == 0 else linear_sum + total
            stats.append(
                (
                    jnp.max(highest, axis=0, keepdims=True),
                    jnp.sum(linear_sum, axis=0, keepdims=True),
                )
            )
        return stats

    def pair_gradients(seq, tile, half, stats):
        highest, linear_sum = stats
        slot = tile % 2
        at = tile * width + half
        denominator = None
        for number in range(at + 1):
            score = scores[seq, slot, block(number), block(half)]
            exponent = jnp.exp2((score - highest) * exponent_scale)
            scores[seq, slot, block(number), block(half)] = exponent
            total = tile_sum(exponent)
            denominator = total if number == 0 else denominator + total
        denominator = jnp.sum(denominator, axis=0, keepdims=True)
        base = 1.0 / (linear_sum * token_count)
        rate = 1.0 / (denominator * token_count)
        for number in range(at + 1):
            exponent = scores[seq, slot, block(number), block(half)]
            weights = base - exponent * rate / linears[seq, slot, block(number), block(half)]
            if number == at:
                weights = jnp.where(visible, weights, 0.0)
            pair_weights[seq, block(number), block(at)] = weights.astype(BF16)

    def map_change(phis, upstream, tokens):
        changes = [
            side_parts(feature_grad_t(phi, upstream[:, block(half)]))
            for half, phi in enumerate(phis)
        ]
        twice = [tokens[block(half)] for half in range(width) for _ in range(2)]
        return nn(jnp.concatenate(changes, axis=1), jnp.concatenate(twice, axis=0))

    def query_upstream(seq, tile):
        here = span(tile)
        return nn(phi_kb[seq, :, : here.stop], pair_weights[seq, : here.stop, here])

    def query_change(seq, tile, upstream):
        phis = [phi_q[place(seq, tile * width + half)] for half in range(width)]
        acc_q[...] += map_change(phis, upstream, query_rows[seq, span(tile), :])

    def key_upstream(seq, tile):
        later = slice(tile * width * BLK, seq_blocks * BLK)
        return nt(phi_qb[seq, :, later], pair_weights[seq, span(tile), later])

    def key_change(seq, tile, upstream):
        phis = [phi_k[seq, :, block(tile * width + half)] for half in range(width)]
        acc_k[...] += map_change(phis, upstream, key_rows[seq, span(tile), :])

    def feature_steps(seq):
        ahead = [key_logits(seq, at) for at in range(min(3, seq_blocks))]
        for at in range(seq_blocks):
            if at + len(ahead) < seq_blocks:
                ahead.append(key_logits(seq, at + len(ahead)))
            key_features(seq, at, ahead.pop(0))
            if at > 1:
                turn_features(seq, at - 2)
            yield
        for at in range(max(seq_blocks - 2, 0), seq_blocks):
            turn_features(seq, at)

    def pair_steps(seq):
        ahead = pair_scores(seq, 0)
        behind = None
        for tile in range(tiles):
            stats = ahead
            if tile + 1 < tiles:
                ahead = pair_scores(seq, tile + 1)
            for half in range(width):
                pair_gradients(seq, tile, half, stats[half])
                yield
            upstream = query_upstream(seq, tile)
            if tile:
                query_change(seq, tile - 1, behind)
            behind = upstream
        yield
        query_change(seq, tiles - 1, behind)

    def key_steps(seq):
        ahead = key_upstream(seq, 0)
        yield
        for tile in range(tiles):
            upstream = ahead
            if tile + 1 < tiles:
                ahead = key_upstream(seq, tile + 1)
            key_change(seq, tile, upstream)
            yield

    for seq in range(sequences):
        for at in range(seq_blocks):
            load_keys(seq, at)
            load_queries(seq, at)
    stages = (feature_steps, pair_steps, key_steps)
    for turn in range(sequences + len(stages) - 1):
        active = [
            stage(turn - number)
            for number, stage in enumerate(stages)
            if 0 <= turn - number < sequences
        ]
        while active:
            for step in list(active):
                if next(step, step) is step:
                    active.remove(step)
    out_ref[:HEAD_SIZE, :] = acc_q[...].T.astype(BF16)
    out_ref[HEAD_SIZE:, :] = bf16_parts(acc_k[...].T, 2)


def per_device_head(queries, keys, block_pos, query_map, key_map):
    seq_count = lax.axis_size("seq")
    head_count = lax.axis_size("head")
    key_heads = key_map.shape[0]
    share = seq_count // key_heads
    rows = queries.shape[0]
    spread = math.gcd(share, 2)
    part = rows // spread
    devices = seq_count * head_count
    token_count = rows * devices
    blocks = token_count // BLK
    seq_tokens = seq_count * BLK
    sequences = token_count // seq_tokens
    vmem = pl.BlockSpec(memory_space=pltpu.VMEM)
    smem = pl.BlockSpec(memory_space=pltpu.SMEM)
    sent_shape = (devices, rows + part, HEAD_SIZE)
    sent = pl.pallas_call(
        functools.partial(send_kernel, seq_count, head_count, key_heads, spread),
        out_shape=jax.ShapeDtypeStruct(sent_shape, BF16),
        in_specs=[pl.BlockSpec(memory_space=pl.ANY)] * 2,
        out_specs=pl.BlockSpec(memory_space=pl.ANY),
        scratch_shapes=[
            pltpu.VMEM(sent_shape, BF16),
            pltpu.SemaphoreType.DMA((3, devices)),
        ],
        compiler_params=pltpu.CompilerParams(vmem_limit_bytes=60 << 20),
    )(queries, keys)
    arrived = lax.all_to_all(sent, ("seq", "head"), split_axis=0, concat_axis=0, tiled=True)
    def swap(piece, bit):
        return lax.ppermute(piece, "seq", [(i, i ^ bit) for i in range(seq_count)])

    phi = pl.pallas_call(
        functools.partial(query_kernel, rows),
        out_shape=jax.ShapeDtypeStruct((blocks, 2 * HEAD_SIZE, BLK), F32),
        in_specs=[vmem, vmem],
        out_specs=vmem,
        compiler_params=pltpu.CompilerParams(vmem_limit_bytes=16 << 20),
        cost_estimate=pl.CostEstimate(
            flops=token_count * HEAD_SIZE * HEAD_SIZE * 6,
            bytes_accessed=token_count * HEAD_SIZE * 20,
            transcendentals=token_count * HEAD_SIZE * 2,
        ),
    )(arrived, query_map)
    pieces = [arrived[:, rows:, :]]
    for other in range(1, spread):
        pieces.append(swap(pieces[0], other))
    grads = pl.pallas_call(
        functools.partial(pair_kernel, token_count, seq_count, rows, share, spread),
        out_shape=jax.ShapeDtypeStruct((3 * HEAD_SIZE, HEAD_SIZE), BF16),
        in_specs=[smem] + [vmem] * (spread + 2),
        out_specs=vmem,
        scratch_shapes=[
            pltpu.SMEM((blocks,), jnp.int32),
            pltpu.VMEM((sequences, seq_tokens, HEAD_SIZE), BF16),
            pltpu.VMEM((sequences, seq_tokens, HEAD_SIZE), BF16),
            pltpu.VMEM((sequences, 2 * HEAD_SIZE, seq_tokens), BF16),
            pltpu.VMEM((sequences, 2 * HEAD_SIZE, seq_tokens), F32),
            pltpu.VMEM((sequences, 2 * HEAD_SIZE, seq_tokens), BF16),
            pltpu.VMEM((sequences, seq_tokens, 2 * HEAD_SIZE), BF16),
            pltpu.VMEM((sequences, seq_tokens, seq_tokens), BF16),
            pltpu.VMEM((sequences, 2, seq_tokens, 2 * BLK), F32),
            pltpu.VMEM((sequences, 2, seq_tokens, 2 * BLK), F32),
            pltpu.VMEM((HEAD_SIZE, HEAD_SIZE), F32),
            pltpu.VMEM((HEAD_SIZE, HEAD_SIZE), F32),
        ],
        compiler_params=pltpu.CompilerParams(vmem_limit_bytes=32 << 20),
    )(block_pos, arrived, *pieces[1:], key_map, phi)
    everyone = lax.all_gather(grads, "seq", axis=0, tiled=False)
    everyone = everyone.reshape(seq_count, 3, HEAD_SIZE, HEAD_SIZE).astype(F32)
    key_sums = (everyone[:, 1] + everyone[:, 2]).reshape(
        key_heads, share, HEAD_SIZE, HEAD_SIZE
    )
    return everyone[:, 0], jnp.sum(key_sums, axis=1)


def per_device(queries, keys, block_pos, query_map, key_map):
    seq_count = lax.axis_size("seq")
    share = seq_count // key_map.shape[0]
    one_head_each = (
        query_map.shape[0] == seq_count
        and seq_count == share * key_map.shape[0]
        and BLK % queries.shape[0] == 0
        and queries.shape[0] % 32 == 0
    )
    chosen = per_device_head if one_head_each else per_device_general
    return chosen(queries, keys, block_pos, query_map, key_map)


def solution(mesh):
    in_specs = (
        P(("seq", "head"), None),
        P(("seq", "head"), None),
        P(),
        P("head", None, None),
        P("head", None, None),
    )
    out_specs = (P("head", None, None), P("head", None, None))
    return jax.shard_map(
        per_device, mesh=mesh, in_specs=in_specs, out_specs=out_specs, check_vma=False
    )
```

```python
import functools
import math

import jax
import jax.numpy as jnp
from jax import lax
from jax.experimental import pallas as pl
from jax.experimental.pallas import tpu as pltpu
from jax.sharding import PartitionSpec as P


HEAD_SIZE = 128
BLK = 128

HIGHEST = lax.Precision.HIGHEST
NEG_FLOOR = -1e30


def softmax_pair(logits):
    return jnp.concatenate(
        [jax.nn.softmax(logits, axis=-1), jax.nn.softmax(-logits, axis=-1)], axis=-1
    )


def feature_grad(feature, upstream):
    half_width = feature.shape[-1] // 2
    positive, negative = (feature[..., :half_width], feature[..., half_width:])
    grad_positive, grad_negative = (upstream[..., :half_width], upstream[..., half_width:])
    first = positive * (grad_positive - jnp.sum(grad_positive * positive, axis=-1, keepdims=True))
    second = negative * (grad_negative - jnp.sum(grad_negative * negative, axis=-1, keepdims=True))
    return first - second


def row_places(row_index, block_pos, seq_count):
    stored = row_index // BLK
    lookup = stored[:, None] == jnp.arange(block_pos.shape[0], dtype=jnp.int32)[None, :]
    blocks = jnp.sum(jnp.where(lookup, block_pos[None, :], 0), axis=1)
    return (blocks // seq_count, blocks * BLK + row_index % BLK)


def over_blocks(running, portions, step_fn):
    row_count = portions[0].shape[1]
    step_rows = math.gcd(row_count, 512)

    def advance(number, inner_carry):
        slabs = tuple(
            (
                lax.dynamic_slice_in_dim(portion, number * step_rows, step_rows, 1)
                for portion in portions
            )
        )
        return step_fn(inner_carry, slabs, number * step_rows)

    return lax.fori_loop(0, row_count // step_rows, advance, running)


def per_device_general(queries, keys, block_pos, query_map, key_map):
    local_q, local_k = (
        lax.all_to_all(queries, "head", split_axis=1, concat_axis=0, tiled=True),
        lax.all_to_all(keys, "head", split_axis=1, concat_axis=0, tiled=True),
    )
    seq_count = lax.axis_size("seq")
    seq_rank = lax.axis_index("seq")
    rows_local = local_k.shape[0]
    token_count = rows_local * seq_count
    key_heads = key_map.shape[0]
    group_width = query_map.shape[0] // key_heads
    score_scale = HEAD_SIZE ** (-0.5)
    query_index = seq_rank * rows_local + jnp.arange(rows_local, dtype=jnp.int32)
    query_heads = local_q.reshape(rows_local, key_heads, group_width, HEAD_SIZE).transpose(
        1, 2, 0, 3
    )
    query_wide = query_heads.astype(jnp.float32)
    query_logits = jnp.einsum(
        "vgnd,vgde->vgne",
        query_wide,
        query_map.reshape(key_heads, group_width, HEAD_SIZE, HEAD_SIZE),
        precision=HIGHEST,
    )
    rows_all = group_width * rows_local
    phi_query = softmax_pair(query_logits).reshape(key_heads, rows_all, 2 * HEAD_SIZE)
    phi_query_b = phi_query.astype(jnp.bfloat16)
    query_flat = query_heads.reshape(key_heads, rows_all, HEAD_SIZE)
    query_seq, query_at = row_places(query_index, block_pos, seq_count)
    query_seq = jnp.tile(query_seq, group_width)
    query_at = jnp.tile(query_at, group_width)

    def visible_for(offset, slab_rows):
        key_index = offset + jnp.arange(slab_rows, dtype=jnp.int32)
        key_seq, key_at = row_places(key_index, block_pos, seq_count)
        return (key_seq[None, :] == query_seq[:, None]) & (key_at[None, :] <= query_at[:, None])

    def key_features(key_slab):
        logits = jnp.einsum(
            "vwd,vde->vwe", key_slab.astype(jnp.float32), key_map, precision=HIGHEST
        )
        return softmax_pair(logits)

    def teacher(key_slab):
        return (
            jnp.einsum("vrd,vwd->vrw", query_flat, key_slab, preferred_element_type=jnp.float32)
            * score_scale
        )

    def stats_step(running, slabs, offset):
        key_slab = slabs[0]
        visible = visible_for(offset, key_slab.shape[1])

        def stats_compute_live(current):
            highest, denominator, linear_sum = current
            masked = jnp.where(visible[None], teacher(key_slab), NEG_FLOOR)
            new_high = jnp.maximum(highest, jnp.max(masked, axis=-1))
            exponent = jnp.where(visible[None], jnp.exp(masked - new_high[..., None]), 0.0)
            denominator = denominator * jnp.exp(highest - new_high) + jnp.sum(exponent, axis=-1)
            phi_key_b = key_features(key_slab).astype(jnp.bfloat16)
            linear = jnp.einsum(
                "vrf,vwf->vrw", phi_query_b, phi_key_b, preferred_element_type=jnp.float32
            )
            linear_sum = linear_sum + jnp.sum(jnp.where(visible[None], linear, 0.0), axis=-1)
            return (new_high, denominator, linear_sum)

        return lax.cond(jnp.any(visible), stats_compute_live, lambda current: current, running)

    def grads_step(running, slabs, offset):
        key_slab = slabs[0]
        visible = visible_for(offset, key_slab.shape[1])

        def grads_compute_live(current):
            query_grad, key_weight_grad = current
            masked = jnp.where(visible[None], teacher(key_slab), NEG_FLOOR)
            exponent = jnp.where(visible[None], jnp.exp(masked - highest[..., None]), 0.0)
            teacher_prob = exponent / denominator[..., None]
            phi_key = key_features(key_slab)
            phi_key_b = phi_key.astype(jnp.bfloat16)
            linear = jnp.einsum(
                "vrf,vwf->vrw", phi_query_b, phi_key_b, preferred_element_type=jnp.float32
            )
            weights = (
                jnp.where(visible[None], 1.0 / linear_sum[..., None] - teacher_prob / linear, 0.0)
                / token_count
            ).astype(jnp.bfloat16)
            query_grad = query_grad + jnp.einsum(
                "vrw,vwf->vrf", weights, phi_key_b, preferred_element_type=jnp.float32
            )
            key_grad = jnp.einsum(
                "vrw,vrf->vwf", weights, phi_query_b, preferred_element_type=jnp.float32
            )
            key_logit_grad = feature_grad(phi_key, key_grad)
            key_weight_grad = key_weight_grad + jnp.einsum(
                "vwd,vwe->vde", key_slab.astype(jnp.float32), key_logit_grad, precision=HIGHEST
            )
            return (query_grad, key_weight_grad)

        return lax.cond(jnp.any(visible), grads_compute_live, lambda current: current, running)

    def as_heads(pieces):
        return pieces.reshape(pieces.shape[0], key_heads, -1).transpose(1, 0, 2)

    row_zeros = jnp.zeros((key_heads, rows_all), jnp.float32)
    stats_init = (jnp.full((key_heads, rows_all), NEG_FLOOR, jnp.float32), row_zeros, row_zeros)
    grads_init = (
        jnp.zeros((key_heads, rows_all, 2 * HEAD_SIZE), jnp.float32),
        jnp.zeros((key_heads, HEAD_SIZE, HEAD_SIZE), jnp.float32),
    )
    highest, denominator, linear_sum = over_blocks(
        stats_init, (as_heads(lax.all_gather(local_k, "seq", axis=0, tiled=True)),), stats_step
    )
    query_grad, key_weight_grad = over_blocks(
        grads_init, (as_heads(lax.all_gather(local_k, "seq", axis=0, tiled=True)),), grads_step
    )
    query_logit_grad = feature_grad(phi_query, query_grad).reshape(
        key_heads, group_width, rows_local, HEAD_SIZE
    )
    query_weight_grad = jnp.einsum(
        "vgnd,vgne->vgde", query_wide, query_logit_grad, precision=HIGHEST
    ).reshape(key_heads * group_width, HEAD_SIZE, HEAD_SIZE)
    query_map_gradient, key_map_gradient = lax.psum((query_weight_grad, key_weight_grad), "seq")
    return (query_map_gradient, key_map_gradient)


NT = (((1,), (1,)), ((), ()))
F32 = jnp.float32
BF16 = jnp.bfloat16


def nn(left, right):
    return jnp.dot(left, right, preferred_element_type=F32)


def nt(left, right):
    return lax.dot_general(left, right, NT, preferred_element_type=F32)


def bf16_parts(value, count):
    parts = []
    for _ in range(count):
        part = value.astype(BF16)
        parts.append(part)
        value = value - part.astype(F32)
    return jnp.concatenate(parts, axis=0)


def features_t(logits):
    up = jnp.exp(logits - jnp.max(logits, axis=0, keepdims=True))
    down = jnp.exp(jnp.min(logits, axis=0, keepdims=True) - logits)
    up = up * (1.0 / jnp.sum(up, axis=0, keepdims=True))
    down = down * (1.0 / jnp.sum(down, axis=0, keepdims=True))
    return jnp.concatenate([up, down], axis=0)


def feature_grad_t(feature, upstream):
    halves = []
    for half in (slice(0, HEAD_SIZE), slice(HEAD_SIZE, 2 * HEAD_SIZE)):
        value, grad = feature[half], upstream[half]
        halves.append(value * (grad - jnp.sum(grad * value, axis=0, keepdims=True)))
    return halves[0] - halves[1]


def tile_sum(value):
    return jnp.sum(value.reshape(-1, 8, value.shape[-1]), axis=0)


def tile_max(value):
    return jnp.max(value.reshape(-1, 8, value.shape[-1]), axis=0)


def side_parts(value):
    high = value.astype(BF16)
    return jnp.concatenate([high, (value - high.astype(F32)).astype(BF16)], axis=1)


def map_parts(weights):
    rest = weights.T
    parts = []
    for _ in range(3):
        parts.append(rest.astype(BF16))
        rest = rest - parts[-1].astype(F32)
    return jnp.concatenate(parts[::-1], axis=1)


def logits_t(parts, tokens):
    return nt(parts, jnp.concatenate([tokens] * 3, axis=1))


def key_send_kernel(keys_ref, *out_refs):
    head = lax.axis_index("head")
    key_heads = out_refs[0].shape[0]
    for other, out_ref in enumerate(out_refs):
        for number in range(key_heads):
            column = ((head ^ other) * key_heads + number) * HEAD_SIZE
            column = pl.multiple_of(column, HEAD_SIZE)
            out_ref[number] = keys_ref[:, pl.ds(column, HEAD_SIZE)]


def query_send_kernel(seq_count, head_count, queries_ref, out_ref):
    for head in range(head_count):
        for seq in range(seq_count):
            column = (head * seq_count + seq) * HEAD_SIZE
            out_ref[seq * head_count + head] = queries_ref[:, column : column + HEAD_SIZE]


def key_turn_kernel(share, *refs):
    key_heads = refs[0].shape[0]
    in_refs, out_refs = refs[:-key_heads], refs[-key_heads:]
    mine = lax.div(lax.axis_index("seq"), share)
    for other, out_ref in enumerate(out_refs):
        for number, in_ref in enumerate(in_refs):
            out_ref[number] = in_ref[mine ^ other]


def query_kernel(rows, arrived_ref, query_map_ref, phi_ref):
    per_block = BLK // rows
    parts = map_parts(query_map_ref[lax.axis_index("seq")])

    def block_logits(number):
        tokens = arrived_ref[number * per_block : (number + 1) * per_block]
        return logits_t(parts, tokens.reshape(BLK, HEAD_SIZE))

    blocks = phi_ref.shape[0]
    ahead = block_logits(0)
    for number in range(blocks):
        logits = ahead
        if number + 1 < blocks:
            ahead = block_logits(number + 1)
        phi_ref[number] = features_t(logits)


def pair_kernel(
    token_count,
    seq_blocks,
    rows,
    share,
    pos_ref,
    arrived_ref,
    *refs,
):
    seq_count, head_count = lax.axis_size("seq"), lax.axis_size("head")
    key_refs, refs = refs[:seq_count], refs[seq_count:]
    (
        key_map_ref,
        phi_q,
        out_ref,
        stored,
        key_rows,
        query_rows,
        phi_qb,
        phi_k,
        phi_kb,
        phi_kb_rows,
        pair_weights,
        scores,
        linears,
        acc_q,
        acc_k,
    ) = refs
    per_block = BLK // rows
    seq_tokens = seq_blocks * BLK
    sequences = token_count // (seq_blocks * BLK)
    for number in range(token_count // BLK):
        stored[pos_ref[number]] = number
    acc_q[...] = jnp.zeros_like(acc_q)
    acc_k[...] = jnp.zeros_like(acc_k)
    width = 2 if seq_blocks % 2 == 0 else 1
    tiles = seq_blocks // width
    for seq in range(sequences):
        for at in range(0, seq_blocks, width):
            if width > 1:
                pair_weights[seq, (at + 1) * BLK : (at + 2) * BLK, at * BLK : (at + 1) * BLK] = (
                    jnp.zeros((BLK, BLK), BF16)
                )
    mine, plane = lax.axis_index("seq"), lax.axis_index("head")
    parts = map_parts(key_map_ref[lax.div(mine, share)])
    lane = lax.broadcasted_iota(jnp.int32, (BLK, BLK), 1)
    sublane = lax.broadcasted_iota(jnp.int32, (BLK, BLK), 0)
    unit = jnp.where(lane == sublane, 1.0, 0.0).astype(BF16)
    visible = sublane <= lane
    exponent_scale = HEAD_SIZE ** (-0.5) * math.log2(math.e)

    def block(at):
        return slice(at * BLK, (at + 1) * BLK)

    def span(tile):
        return slice(tile * width * BLK, (tile + 1) * width * BLK)

    def place(seq, at):
        return stored[seq * seq_blocks + at]

    def flat(seq, here):
        return slice(seq * seq_tokens + here.start, seq * seq_tokens + here.stop)

    def sorted_rows(chunk):
        first = pos_ref[lax.div(chunk, per_block)] * BLK + lax.rem(chunk, per_block) * rows
        return pl.ds(pl.multiple_of(first, rows), rows)

    def load_features(seq, at):
        phi_qb[seq, :, block(at)] = phi_q[place(seq, at)].astype(BF16)

    def key_logits(seq, at):
        return logits_t(parts, key_rows[flat(seq, block(at)), :])

    def key_features(seq, at, logits):
        feature = features_t(logits)
        phi_k[seq, :, block(at)] = feature
        phi_kb[seq, :, block(at)] = feature.astype(BF16)

    def turn_features(seq, at):
        phi_kb_rows[seq, block(at), :] = nt(unit, phi_kb[seq, :, block(at)]).astype(BF16)

    def pair_scores(seq, tile):
        here = span(tile)
        slot = tile % 2
        teacher = nt(key_rows[flat(seq, slice(0, here.stop)), :], query_rows[flat(seq, here), :])
        student = nn(phi_kb_rows[seq, : here.stop, :], phi_qb[seq, :, here])
        stats = []
        for half in range(width):
            at = tile * width + half
            highest = linear_sum = None
            for number in range(at + 1):
                score = teacher[block(number), block(half)]
                linear = student[block(number), block(half)]
                linears[seq, slot, block(number), block(half)] = linear
                if number == at:
                    score = jnp.where(visible, score, NEG_FLOOR)
                    linear = jnp.where(visible, linear, 0.0)
                scores[seq, slot, block(number), block(half)] = score
                top, total = tile_max(score), tile_sum(linear)
                highest = top if number == 0 else jnp.maximum(highest, top)
                linear_sum = total if number == 0 else linear_sum + total
            stats.append(
                (
                    jnp.max(highest, axis=0, keepdims=True),
                    jnp.sum(linear_sum, axis=0, keepdims=True),
                )
            )
        return stats

    def pair_gradients(seq, tile, half, stats):
        highest, linear_sum = stats
        slot = tile % 2
        at = tile * width + half
        denominator = None
        for number in range(at + 1):
            score = scores[seq, slot, block(number), block(half)]
            exponent = jnp.exp2((score - highest) * exponent_scale)
            scores[seq, slot, block(number), block(half)] = exponent
            total = tile_sum(exponent)
            denominator = total if number == 0 else denominator + total
        denominator = jnp.sum(denominator, axis=0, keepdims=True)
        base = 1.0 / (linear_sum * token_count)
        rate = 1.0 / (denominator * token_count)
        for number in range(at + 1):
            exponent = scores[seq, slot, block(number), block(half)]
            weights = base - exponent * rate / linears[seq, slot, block(number), block(half)]
            if number == at:
                weights = jnp.where(visible, weights, 0.0)
            pair_weights[seq, block(number), block(at)] = weights.astype(BF16)

    def map_change(phis, upstream, tokens):
        changes = [
            side_parts(feature_grad_t(phi, upstream[:, block(half)]))
            for half, phi in enumerate(phis)
        ]
        twice = [tokens[block(half)] for half in range(width) for _ in range(2)]
        return nn(jnp.concatenate(changes, axis=1), jnp.concatenate(twice, axis=0))

    def query_upstream(seq, tile):
        here = span(tile)
        return nn(phi_kb[seq, :, : here.stop], pair_weights[seq, : here.stop, here])

    def query_change(seq, tile, upstream):
        phis = [phi_q[place(seq, tile * width + half)] for half in range(width)]
        acc_q[...] += map_change(phis, upstream, query_rows[flat(seq, span(tile)), :])

    def key_upstream(seq, tile):
        later = slice(tile * width * BLK, seq_blocks * BLK)
        return nt(phi_qb[seq, :, later], pair_weights[seq, span(tile), later])

    def key_change(seq, tile, upstream):
        phis = [phi_k[seq, :, block(tile * width + half)] for half in range(width)]
        acc_k[...] += map_change(phis, upstream, key_rows[flat(seq, span(tile)), :])

    def feature_steps(seq):
        ahead = [key_logits(seq, at) for at in range(min(3, seq_blocks))]
        for at in range(seq_blocks):
            if at + len(ahead) < seq_blocks:
                ahead.append(key_logits(seq, at + len(ahead)))
            key_features(seq, at, ahead.pop(0))
            if at > 1:
                turn_features(seq, at - 2)
            yield
        for at in range(max(seq_blocks - 2, 0), seq_blocks):
            turn_features(seq, at)

    def pair_steps(seq):
        ahead = pair_scores(seq, 0)
        behind = None
        for tile in range(tiles):
            stats = ahead
            if tile + 1 < tiles:
                ahead = pair_scores(seq, tile + 1)
            for half in range(width):
                pair_gradients(seq, tile, half, stats[half])
                yield
            upstream = query_upstream(seq, tile)
            if tile:
                query_change(seq, tile - 1, behind)
            behind = upstream
        yield
        query_change(seq, tiles - 1, behind)

    def key_steps(seq):
        ahead = key_upstream(seq, 0)
        yield
        for tile in range(tiles):
            upstream = ahead
            if tile + 1 < tiles:
                ahead = key_upstream(seq, tile + 1)
            key_change(seq, tile, upstream)
            yield

    for other in range(seq_count):
        for number in range(head_count):
            chunk = (mine ^ other) * head_count + (plane ^ number)
            key_rows[sorted_rows(chunk), :] = key_refs[other][number]
    for chunk in range(token_count // rows):
        query_rows[sorted_rows(chunk), :] = arrived_ref[chunk]
    for seq in range(sequences):
        for at in range(seq_blocks):
            load_features(seq, at)
    stages = (feature_steps, pair_steps, key_steps)
    for turn in range(sequences + len(stages) - 1):
        active = [
            stage(turn - number)
            for number, stage in enumerate(stages)
            if 0 <= turn - number < sequences
        ]
        while active:
            for step in list(active):
                if next(step, step) is step:
                    active.remove(step)
    out_ref[:HEAD_SIZE, :] = acc_q[...].T.astype(BF16)
    out_ref[HEAD_SIZE:, :] = bf16_parts(acc_k[...].T, 2)


def collect_kernel(everyone_ref, queries_out_ref, keys_out_ref, buffer, sems):
    seq_count = queries_out_ref.shape[0]
    key_heads = keys_out_ref.shape[0]
    share = seq_count // key_heads
    copies = []

    def leave(number, value, out_ref):
        buffer[number] = value
        copies.append(pltpu.make_async_copy(buffer.at[number], out_ref, sems.at[number]))
        copies[-1].start()

    for number in range(seq_count):
        leave(number, everyone_ref[number, :HEAD_SIZE, :].astype(F32), queries_out_ref.at[number])
    for number in range(key_heads):
        total = None
        for seq in range(number * share, (number + 1) * share):
            for half in (1, 2):
                rows = slice(half * HEAD_SIZE, (half + 1) * HEAD_SIZE)
                value = everyone_ref[seq, rows, :].astype(F32)
                total = value if total is None else total + value
        leave(seq_count + number, total, keys_out_ref.at[number])
    for copy in copies:
        copy.wait()


def per_device_head(queries, keys, block_pos, query_map, key_map):
    seq_count = lax.axis_size("seq")
    head_count = lax.axis_size("head")
    key_heads = key_map.shape[0]
    share = seq_count // key_heads
    rows = queries.shape[0]
    devices = seq_count * head_count
    token_count = rows * devices
    blocks = token_count // BLK
    seq_tokens = seq_count * BLK
    sequences = token_count // seq_tokens
    vmem = pl.BlockSpec(memory_space=pltpu.VMEM)
    smem = pl.BlockSpec(memory_space=pltpu.SMEM)

    def swap(piece, axis, bits):
        size = lax.axis_size(axis)
        return lax.ppermute(piece, axis, [(i, i ^ bits) for i in range(size)])

    small = pltpu.CompilerParams(vmem_limit_bytes=4 << 20)
    by_plane = pl.pallas_call(
        key_send_kernel,
        out_shape=[jax.ShapeDtypeStruct((key_heads, rows, HEAD_SIZE), BF16)] * head_count,
        in_specs=[vmem],
        out_specs=[vmem] * head_count,
        compiler_params=small,
    )(keys)
    by_plane = list(by_plane)
    for other in range(1, head_count):
        by_plane[other] = swap(by_plane[other], "head", other)
    sent = pl.pallas_call(
        functools.partial(query_send_kernel, seq_count, head_count),
        out_shape=jax.ShapeDtypeStruct((devices, rows, HEAD_SIZE), BF16),
        in_specs=[vmem],
        out_specs=vmem,
        compiler_params=small,
    )(queries)
    arrived = lax.all_to_all(sent, ("seq", "head"), split_axis=0, concat_axis=0, tiled=True)
    by_key_head = pl.pallas_call(
        functools.partial(key_turn_kernel, share),
        out_shape=[jax.ShapeDtypeStruct((head_count, rows, HEAD_SIZE), BF16)] * key_heads,
        in_specs=[vmem] * head_count,
        out_specs=[vmem] * key_heads,
        compiler_params=small,
    )(*by_plane)
    pieces = [None] * seq_count
    for other in range(0, seq_count, 2):
        piece = by_key_head[other // share]
        pieces[other] = swap(piece, "seq", other) if other else piece
    for other in range(0, seq_count, 2):
        pieces[other + 1] = swap(pieces[other], "seq", 1)
    phi = pl.pallas_call(
        functools.partial(query_kernel, rows),
        out_shape=jax.ShapeDtypeStruct((blocks, 2 * HEAD_SIZE, BLK), F32),
        in_specs=[vmem, vmem],
        out_specs=vmem,
        compiler_params=pltpu.CompilerParams(vmem_limit_bytes=16 << 20),
        cost_estimate=pl.CostEstimate(
            flops=token_count * HEAD_SIZE * HEAD_SIZE * 6,
            bytes_accessed=token_count * HEAD_SIZE * 20,
            transcendentals=token_count * HEAD_SIZE * 2,
        ),
    )(arrived, query_map)
    grads = pl.pallas_call(
        functools.partial(pair_kernel, token_count, seq_count, rows, share),
        out_shape=jax.ShapeDtypeStruct((3 * HEAD_SIZE, HEAD_SIZE), BF16),
        in_specs=[smem] + [vmem] * (seq_count + 3),
        out_specs=vmem,
        scratch_shapes=[
            pltpu.SMEM((blocks,), jnp.int32),
            pltpu.VMEM((token_count, HEAD_SIZE), BF16),
            pltpu.VMEM((token_count, HEAD_SIZE), BF16),
            pltpu.VMEM((sequences, 2 * HEAD_SIZE, seq_tokens), BF16),
            pltpu.VMEM((sequences, 2 * HEAD_SIZE, seq_tokens), F32),
            pltpu.VMEM((sequences, 2 * HEAD_SIZE, seq_tokens), BF16),
            pltpu.VMEM((sequences, seq_tokens, 2 * HEAD_SIZE), BF16),
            pltpu.VMEM((sequences, seq_tokens, seq_tokens), BF16),
            pltpu.VMEM((sequences, 2, seq_tokens, 2 * BLK), F32),
            pltpu.VMEM((sequences, 2, seq_tokens, 2 * BLK), F32),
            pltpu.VMEM((HEAD_SIZE, HEAD_SIZE), F32),
            pltpu.VMEM((HEAD_SIZE, HEAD_SIZE), F32),
        ],
        compiler_params=pltpu.CompilerParams(vmem_limit_bytes=32 << 20),
    )(block_pos, arrived, *pieces, key_map, phi)
    everyone = lax.all_gather(grads, "seq", axis=0, tiled=False)
    return pl.pallas_call(
        collect_kernel,
        out_shape=(
            jax.ShapeDtypeStruct((seq_count, HEAD_SIZE, HEAD_SIZE), F32),
            jax.ShapeDtypeStruct((key_heads, HEAD_SIZE, HEAD_SIZE), F32),
        ),
        in_specs=[vmem],
        out_specs=(pl.BlockSpec(memory_space=pl.ANY),) * 2,
        scratch_shapes=[
            pltpu.VMEM((seq_count + key_heads, HEAD_SIZE, HEAD_SIZE), F32),
            pltpu.SemaphoreType.DMA((seq_count + key_heads,)),
        ],
        compiler_params=small,
    )(everyone)


def one_head_each(mesh, queries, keys, block_pos, query_map, key_map):
    del keys, block_pos
    seq_count, head_count = mesh.shape["seq"], mesh.shape["head"]
    rows = queries.shape[0] // (seq_count * head_count)
    key_heads = key_map.shape[0] // head_count
    return (
        query_map.shape[0] == seq_count * head_count
        and seq_count % (2 * key_heads) == 0
        and seq_count & (seq_count - 1) == 0
        and head_count & (head_count - 1) == 0
        and BLK % rows == 0
        and rows % 16 == 0
    )


def solution(mesh):
    in_specs = (
        P(("seq", "head"), None),
        P(("seq", "head"), None),
        P(),
        P("head", None, None),
        P("head", None, None),
    )
    out_specs = (P("head", None, None), P("head", None, None))

    def sharded(function):
        return jax.shard_map(
            function, mesh=mesh, in_specs=in_specs, out_specs=out_specs, check_vma=False
        )

    def step(*args):
        if one_head_each(mesh, *args):
            return sharded(per_device_head)(*args)
        return sharded(per_device_general)(*args)

    return step
```

```python
import functools
import math

import jax
import jax.numpy as jnp
from jax import lax
from jax.experimental import pallas as pl
from jax.experimental.pallas import tpu as pltpu
from jax.sharding import PartitionSpec as P


HEAD_SIZE = 128
BLK = 128

HIGHEST = lax.Precision.HIGHEST
NEG_FLOOR = -1e30


def softmax_pair(logits):
    return jnp.concatenate(
        [jax.nn.softmax(logits, axis=-1), jax.nn.softmax(-logits, axis=-1)], axis=-1
    )


def feature_grad(feature, upstream):
    half_width = feature.shape[-1] // 2
    positive, negative = (feature[..., :half_width], feature[..., half_width:])
    grad_positive, grad_negative = (upstream[..., :half_width], upstream[..., half_width:])
    first = positive * (grad_positive - jnp.sum(grad_positive * positive, axis=-1, keepdims=True))
    second = negative * (grad_negative - jnp.sum(grad_negative * negative, axis=-1, keepdims=True))
    return first - second


def row_places(row_index, block_pos, seq_count):
    stored = row_index // BLK
    lookup = stored[:, None] == jnp.arange(block_pos.shape[0], dtype=jnp.int32)[None, :]
    blocks = jnp.sum(jnp.where(lookup, block_pos[None, :], 0), axis=1)
    return (blocks // seq_count, blocks * BLK + row_index % BLK)


def over_blocks(running, portions, step_fn):
    row_count = portions[0].shape[1]
    step_rows = math.gcd(row_count, 512)

    def advance(number, inner_carry):
        slabs = tuple(
            (
                lax.dynamic_slice_in_dim(portion, number * step_rows, step_rows, 1)
                for portion in portions
            )
        )
        return step_fn(inner_carry, slabs, number * step_rows)

    return lax.fori_loop(0, row_count // step_rows, advance, running)


def per_device_general(queries, keys, block_pos, query_map, key_map):
    local_q, local_k = (
        lax.all_to_all(queries, "head", split_axis=1, concat_axis=0, tiled=True),
        lax.all_to_all(keys, "head", split_axis=1, concat_axis=0, tiled=True),
    )
    seq_count = lax.axis_size("seq")
    seq_rank = lax.axis_index("seq")
    rows_local = local_k.shape[0]
    token_count = rows_local * seq_count
    key_heads = key_map.shape[0]
    group_width = query_map.shape[0] // key_heads
    score_scale = HEAD_SIZE ** (-0.5)
    query_index = seq_rank * rows_local + jnp.arange(rows_local, dtype=jnp.int32)
    query_heads = local_q.reshape(rows_local, key_heads, group_width, HEAD_SIZE).transpose(
        1, 2, 0, 3
    )
    query_wide = query_heads.astype(jnp.float32)
    query_logits = jnp.einsum(
        "vgnd,vgde->vgne",
        query_wide,
        query_map.reshape(key_heads, group_width, HEAD_SIZE, HEAD_SIZE),
        precision=HIGHEST,
    )
    rows_all = group_width * rows_local
    phi_query = softmax_pair(query_logits).reshape(key_heads, rows_all, 2 * HEAD_SIZE)
    phi_query_b = phi_query.astype(jnp.bfloat16)
    query_flat = query_heads.reshape(key_heads, rows_all, HEAD_SIZE)
    query_seq, query_at = row_places(query_index, block_pos, seq_count)
    query_seq = jnp.tile(query_seq, group_width)
    query_at = jnp.tile(query_at, group_width)

    def visible_for(offset, slab_rows):
        key_index = offset + jnp.arange(slab_rows, dtype=jnp.int32)
        key_seq, key_at = row_places(key_index, block_pos, seq_count)
        return (key_seq[None, :] == query_seq[:, None]) & (key_at[None, :] <= query_at[:, None])

    def key_features(key_slab):
        logits = jnp.einsum(
            "vwd,vde->vwe", key_slab.astype(jnp.float32), key_map, precision=HIGHEST
        )
        return softmax_pair(logits)

    def teacher(key_slab):
        return (
            jnp.einsum("vrd,vwd->vrw", query_flat, key_slab, preferred_element_type=jnp.float32)
            * score_scale
        )

    def stats_step(running, slabs, offset):
        key_slab = slabs[0]
        visible = visible_for(offset, key_slab.shape[1])

        def stats_compute_live(current):
            highest, denominator, linear_sum = current
            masked = jnp.where(visible[None], teacher(key_slab), NEG_FLOOR)
            new_high = jnp.maximum(highest, jnp.max(masked, axis=-1))
            exponent = jnp.where(visible[None], jnp.exp(masked - new_high[..., None]), 0.0)
            denominator = denominator * jnp.exp(highest - new_high) + jnp.sum(exponent, axis=-1)
            phi_key_b = key_features(key_slab).astype(jnp.bfloat16)
            linear = jnp.einsum(
                "vrf,vwf->vrw", phi_query_b, phi_key_b, preferred_element_type=jnp.float32
            )
            linear_sum = linear_sum + jnp.sum(jnp.where(visible[None], linear, 0.0), axis=-1)
            return (new_high, denominator, linear_sum)

        return lax.cond(jnp.any(visible), stats_compute_live, lambda current: current, running)

    def grads_step(running, slabs, offset):
        key_slab = slabs[0]
        visible = visible_for(offset, key_slab.shape[1])

        def grads_compute_live(current):
            query_grad, key_weight_grad = current
            masked = jnp.where(visible[None], teacher(key_slab), NEG_FLOOR)
            exponent = jnp.where(visible[None], jnp.exp(masked - highest[..., None]), 0.0)
            teacher_prob = exponent / denominator[..., None]
            phi_key = key_features(key_slab)
            phi_key_b = phi_key.astype(jnp.bfloat16)
            linear = jnp.einsum(
                "vrf,vwf->vrw", phi_query_b, phi_key_b, preferred_element_type=jnp.float32
            )
            weights = (
                jnp.where(visible[None], 1.0 / linear_sum[..., None] - teacher_prob / linear, 0.0)
                / token_count
            ).astype(jnp.bfloat16)
            query_grad = query_grad + jnp.einsum(
                "vrw,vwf->vrf", weights, phi_key_b, preferred_element_type=jnp.float32
            )
            key_grad = jnp.einsum(
                "vrw,vrf->vwf", weights, phi_query_b, preferred_element_type=jnp.float32
            )
            key_logit_grad = feature_grad(phi_key, key_grad)
            key_weight_grad = key_weight_grad + jnp.einsum(
                "vwd,vwe->vde", key_slab.astype(jnp.float32), key_logit_grad, precision=HIGHEST
            )
            return (query_grad, key_weight_grad)

        return lax.cond(jnp.any(visible), grads_compute_live, lambda current: current, running)

    def as_heads(pieces):
        return pieces.reshape(pieces.shape[0], key_heads, -1).transpose(1, 0, 2)

    row_zeros = jnp.zeros((key_heads, rows_all), jnp.float32)
    stats_init = (jnp.full((key_heads, rows_all), NEG_FLOOR, jnp.float32), row_zeros, row_zeros)
    grads_init = (
        jnp.zeros((key_heads, rows_all, 2 * HEAD_SIZE), jnp.float32),
        jnp.zeros((key_heads, HEAD_SIZE, HEAD_SIZE), jnp.float32),
    )
    highest, denominator, linear_sum = over_blocks(
        stats_init, (as_heads(lax.all_gather(local_k, "seq", axis=0, tiled=True)),), stats_step
    )
    query_grad, key_weight_grad = over_blocks(
        grads_init, (as_heads(lax.all_gather(local_k, "seq", axis=0, tiled=True)),), grads_step
    )
    query_logit_grad = feature_grad(phi_query, query_grad).reshape(
        key_heads, group_width, rows_local, HEAD_SIZE
    )
    query_weight_grad = jnp.einsum(
        "vgnd,vgne->vgde", query_wide, query_logit_grad, precision=HIGHEST
    ).reshape(key_heads * group_width, HEAD_SIZE, HEAD_SIZE)
    query_map_gradient, key_map_gradient = lax.psum((query_weight_grad, key_weight_grad), "seq")
    return (query_map_gradient, key_map_gradient)


NT = (((1,), (1,)), ((), ()))
F32 = jnp.float32
BF16 = jnp.bfloat16


def nn(left, right):
    return jnp.dot(left, right, preferred_element_type=F32)


def nt(left, right):
    return lax.dot_general(left, right, NT, preferred_element_type=F32)


def bf16_parts(value, count):
    parts = []
    for _ in range(count):
        part = value.astype(BF16)
        parts.append(part)
        value = value - part.astype(F32)
    return jnp.concatenate(parts, axis=0)


def features_t(logits):
    up = jnp.exp(logits - jnp.max(logits, axis=0, keepdims=True))
    down = jnp.exp(jnp.min(logits, axis=0, keepdims=True) - logits)
    up = up * (1.0 / jnp.sum(up, axis=0, keepdims=True))
    down = down * (1.0 / jnp.sum(down, axis=0, keepdims=True))
    return jnp.concatenate([up, down], axis=0)


def feature_grad_t(feature, upstream):
    halves = []
    for half in (slice(0, HEAD_SIZE), slice(HEAD_SIZE, 2 * HEAD_SIZE)):
        value, grad = feature[half], upstream[half]
        halves.append(value * (grad - jnp.sum(grad * value, axis=0, keepdims=True)))
    return halves[0] - halves[1]


def tile_sum(value):
    return jnp.sum(value.reshape(-1, 8, value.shape[-1]), axis=0)


def tile_max(value):
    return jnp.max(value.reshape(-1, 8, value.shape[-1]), axis=0)


def side_parts(value):
    high = value.astype(BF16)
    return jnp.concatenate([high, (value - high.astype(F32)).astype(BF16)], axis=1)


def map_parts(weights):
    rest = weights.T
    parts = []
    for _ in range(3):
        parts.append(rest.astype(BF16))
        rest = rest - parts[-1].astype(F32)
    return jnp.concatenate(parts[::-1], axis=1)


def logits_t(parts, tokens):
    return nt(parts, jnp.concatenate([tokens] * 3, axis=1))


def key_send_kernel(keys_ref, *out_refs):
    head = lax.axis_index("head")
    key_heads = out_refs[0].shape[0]
    for other, out_ref in enumerate(out_refs):
        for number in range(key_heads):
            column = ((head ^ other) * key_heads + number) * HEAD_SIZE
            column = pl.multiple_of(column, HEAD_SIZE)
            out_ref[number] = keys_ref[:, pl.ds(column, HEAD_SIZE)]


def query_send_kernel(seq_count, head_count, queries_ref, out_ref):
    for head in range(head_count):
        for seq in range(seq_count):
            column = (head * seq_count + seq) * HEAD_SIZE
            out_ref[seq * head_count + head] = queries_ref[:, column : column + HEAD_SIZE]


def key_turn_kernel(share, *refs):
    key_heads = refs[0].shape[0]
    in_refs, out_refs = refs[:-key_heads], refs[-key_heads:]
    mine = lax.div(lax.axis_index("seq"), share)
    for other, out_ref in enumerate(out_refs):
        for number, in_ref in enumerate(in_refs):
            out_ref[number] = in_ref[mine ^ other]


def sorted_rows(pos_ref, chunk, rows):
    per_block = BLK // rows
    first = pos_ref[lax.div(chunk, per_block)] * BLK + lax.rem(chunk, per_block) * rows
    return pl.ds(pl.multiple_of(first, rows), rows)


def block(at):
    return slice(at * BLK, (at + 1) * BLK)


def key_kernel(share, pos_ref, key_map_ref, query_map_ref, *refs):
    seq_count, head_count = lax.axis_size("seq"), lax.axis_size("head")
    piece_refs, refs = refs[:seq_count], refs[seq_count:]
    key_rows, phi, query_weights_ref, key_weights_ref = refs
    rows = piece_refs[0].shape[1]
    seq_blocks = phi.shape[2] // BLK
    blocks = phi.shape[0] * seq_blocks
    mine, plane = lax.axis_index("seq"), lax.axis_index("head")
    query_weights_ref[...] = query_map_ref[mine]
    for other in range(seq_count):
        for number in range(head_count):
            chunk = (mine ^ other) * head_count + (plane ^ number)
            key_rows[sorted_rows(pos_ref, chunk, rows), :] = piece_refs[other][number]
    key_weights_ref[...] = key_map_ref[lax.div(mine, share)]
    parts = map_parts(key_weights_ref[...])
    ahead = []
    for number in range(blocks):
        while number + len(ahead) < min(number + 3, blocks):
            ahead.append(logits_t(parts, key_rows[block(number + len(ahead)), :]))
        seq, at = divmod(number, seq_blocks)
        phi[seq, :, block(at)] = features_t(ahead.pop(0))


def pair_kernel(
    token_count,
    seq_blocks,
    pos_ref,
    arrived_ref,
    query_weights_ref,
    key_weights_ref,
    key_rows,
    phi_k_early,
    out_ref,
    query_rows,
    phi_q,
    phi_qb,
    phi_k_late,
    phi_kb,
    phi_kb_rows,
    pair_weights,
    scores,
    linears,
    acc_q,
    acc_k,
):
    rows = arrived_ref.shape[1]
    seq_tokens = seq_blocks * BLK
    sequences = token_count // seq_tokens
    acc_q[...] = jnp.zeros_like(acc_q)
    acc_k[...] = jnp.zeros_like(acc_k)
    width = 2 if seq_blocks % 2 == 0 else 1
    tiles = seq_blocks // width
    for seq in range(sequences):
        for at in range(0, seq_blocks, width):
            if width > 1:
                pair_weights[seq, block(at + 1), block(at)] = jnp.zeros((BLK, BLK), BF16)
    parts = map_parts(query_weights_ref[...])
    key_parts = map_parts(key_weights_ref[...])
    early = phi_k_early.shape[0]
    lane = lax.broadcasted_iota(jnp.int32, (BLK, BLK), 1)
    sublane = lax.broadcasted_iota(jnp.int32, (BLK, BLK), 0)
    unit = jnp.where(lane == sublane, 1.0, 0.0).astype(BF16)
    visible = sublane <= lane
    exponent_scale = HEAD_SIZE ** (-0.5) * math.log2(math.e)

    def span(tile):
        return slice(tile * width * BLK, (tile + 1) * width * BLK)

    def flat(seq, here):
        return slice(seq * seq_tokens + here.start, seq * seq_tokens + here.stop)

    def query_logits(seq, at):
        return logits_t(parts, query_rows[flat(seq, block(at)), :])

    def query_features(seq, at, logits):
        feature = features_t(logits)
        phi_q[seq, :, block(at)] = feature
        phi_qb[seq, :, block(at)] = feature.astype(BF16)

    def phi_k(seq, at):
        if seq < early:
            return phi_k_early[seq, :, block(at)]
        return phi_k_late[seq - early, :, block(at)]

    def key_logits(seq, at):
        if seq < early:
            return None
        return logits_t(key_parts, key_rows[flat(seq, block(at)), :])

    def key_features(seq, at, logits):
        if seq >= early:
            phi_k_late[seq - early, :, block(at)] = features_t(logits)

    def turn_features(seq, at):
        rounded = phi_k(seq, at).astype(BF16)
        phi_kb[seq, :, block(at)] = rounded
        phi_kb_rows[seq, block(at), :] = nt(unit, rounded).astype(BF16)

    def pair_scores(seq, tile):
        here = span(tile)
        slot = tile % 2
        teacher = nt(key_rows[flat(seq, slice(0, here.stop)), :], query_rows[flat(seq, here), :])
        student = nn(phi_kb_rows[seq, : here.stop, :], phi_qb[seq, :, here])
        stats = []
        for half in range(width):
            at = tile * width + half
            highest = linear_sum = None
            for number in range(at + 1):
                score = teacher[block(number), block(half)]
                linear = student[block(number), block(half)]
                linears[seq, slot, block(number), block(half)] = linear
                if number == at:
                    score = jnp.where(visible, score, NEG_FLOOR)
                    linear = jnp.where(visible, linear, 0.0)
                scores[seq, slot, block(number), block(half)] = score
                top, total = tile_max(score), tile_sum(linear)
                highest = top if number == 0 else jnp.maximum(highest, top)
                linear_sum = total if number == 0 else linear_sum + total
            stats.append(
                (
                    jnp.max(highest, axis=0, keepdims=True),
                    jnp.sum(linear_sum, axis=0, keepdims=True),
                )
            )
        return stats

    def pair_gradients(seq, tile, half, stats):
        highest, linear_sum = stats
        slot = tile % 2
        at = tile * width + half
        denominator = None
        for number in range(at + 1):
            score = scores[seq, slot, block(number), block(half)]
            exponent = jnp.exp2((score - highest) * exponent_scale)
            scores[seq, slot, block(number), block(half)] = exponent
            total = tile_sum(exponent)
            denominator = total if number == 0 else denominator + total
        denominator = jnp.sum(denominator, axis=0, keepdims=True)
        base = 1.0 / (linear_sum * token_count)
        rate = 1.0 / (denominator * token_count)
        for number in range(at + 1):
            exponent = scores[seq, slot, block(number), block(half)]
            weights = base - exponent * rate / linears[seq, slot, block(number), block(half)]
            if number == at:
                weights = jnp.where(visible, weights, 0.0)
            pair_weights[seq, block(number), block(at)] = weights.astype(BF16)

    def map_change(phis, upstream, tokens):
        changes = [
            side_parts(feature_grad_t(phi, upstream[:, block(half)]))
            for half, phi in enumerate(phis)
        ]
        twice = [tokens[block(half)] for half in range(width) for _ in range(2)]
        return nn(jnp.concatenate(changes, axis=1), jnp.concatenate(twice, axis=0))

    def query_upstream(seq, tile):
        here = span(tile)
        return nn(phi_kb[seq, :, : here.stop], pair_weights[seq, : here.stop, here])

    def query_change(seq, tile, upstream):
        phis = [phi_q[seq, :, block(tile * width + half)] for half in range(width)]
        acc_q[...] += map_change(phis, upstream, query_rows[flat(seq, span(tile)), :])

    def key_upstream(seq, tile):
        later = slice(tile * width * BLK, seq_blocks * BLK)
        return nt(phi_qb[seq, :, later], pair_weights[seq, span(tile), later])

    def key_change(seq, tile, upstream):
        phis = [phi_k(seq, tile * width + half) for half in range(width)]
        acc_k[...] += map_change(phis, upstream, key_rows[flat(seq, span(tile)), :])

    def feature_steps(seq):
        ahead = [key_logits(seq, at) for at in range(min(3, seq_blocks))]
        for at in range(seq_blocks):
            if at + len(ahead) < seq_blocks:
                ahead.append(key_logits(seq, at + len(ahead)))
            key_features(seq, at, ahead.pop(0))
            if at > 1:
                turn_features(seq, at - 2)
            yield
        for at in range(max(seq_blocks - 2, 0), seq_blocks):
            turn_features(seq, at)

    def feature_steps(seq):
        ahead = []
        for at in range(seq_blocks):
            while at + len(ahead) < min(at + 3, seq_blocks):
                later = at + len(ahead)
                ahead.append((key_logits(seq, later), query_logits(seq, later)))
            from_keys, from_queries = ahead.pop(0)
            key_features(seq, at, from_keys)
            query_features(seq, at, from_queries)
            if at:
                turn_features(seq, at - 1)
            yield
        turn_features(seq, seq_blocks - 1)

    def pair_steps(seq):
        ahead = pair_scores(seq, 0)
        behind = None
        for tile in range(tiles):
            stats = ahead
            if tile + 1 < tiles:
                ahead = pair_scores(seq, tile + 1)
            for half in range(width):
                pair_gradients(seq, tile, half, stats[half])
                yield
            upstream = query_upstream(seq, tile)
            if tile:
                query_change(seq, tile - 1, behind)
            behind = upstream
        yield
        query_change(seq, tiles - 1, behind)

    def key_steps(seq):
        ahead = key_upstream(seq, 0)
        yield
        for tile in range(tiles):
            upstream = ahead
            if tile + 1 < tiles:
                ahead = key_upstream(seq, tile + 1)
            key_change(seq, tile, upstream)
            yield

    for chunk in range(token_count // rows):
        query_rows[sorted_rows(pos_ref, chunk, rows), :] = arrived_ref[chunk]
    stages = (feature_steps, pair_steps, key_steps)
    for turn in range(sequences + len(stages) - 1):
        active = [
            stage(turn - number)
            for number, stage in enumerate(stages)
            if 0 <= turn - number < sequences
        ]
        while active:
            for step in list(active):
                if next(step, step) is step:
                    active.remove(step)
    out_ref[:HEAD_SIZE, :] = acc_q[...].T.astype(BF16)
    out_ref[HEAD_SIZE:, :] = bf16_parts(acc_k[...].T, 2)


def collect_kernel(everyone_ref, queries_out_ref, keys_out_ref, buffer, sems):
    seq_count = queries_out_ref.shape[0]
    key_heads = keys_out_ref.shape[0]
    share = seq_count // key_heads
    copies = []

    def leave(number, value, out_ref):
        buffer[number] = value
        copies.append(pltpu.make_async_copy(buffer.at[number], out_ref, sems.at[number]))
        copies[-1].start()

    for number in range(seq_count):
        leave(number, everyone_ref[number, :HEAD_SIZE, :].astype(F32), queries_out_ref.at[number])
    for number in range(key_heads):
        total = None
        for seq in range(number * share, (number + 1) * share):
            for half in (1, 2):
                rows = slice(half * HEAD_SIZE, (half + 1) * HEAD_SIZE)
                value = everyone_ref[seq, rows, :].astype(F32)
                total = value if total is None else total + value
        leave(seq_count + number, total, keys_out_ref.at[number])
    for copy in copies:
        copy.wait()


def per_device_head(queries, keys, block_pos, query_map, key_map):
    seq_count = lax.axis_size("seq")
    head_count = lax.axis_size("head")
    key_heads = key_map.shape[0]
    share = seq_count // key_heads
    rows = queries.shape[0]
    devices = seq_count * head_count
    token_count = rows * devices
    seq_tokens = seq_count * BLK
    sequences = token_count // seq_tokens
    vmem = pl.BlockSpec(memory_space=pltpu.VMEM)
    smem = pl.BlockSpec(memory_space=pltpu.SMEM)

    def swap(piece, axis, bits):
        size = lax.axis_size(axis)
        return lax.ppermute(piece, axis, [(i, i ^ bits) for i in range(size)])

    small = pltpu.CompilerParams(vmem_limit_bytes=4 << 20)
    by_plane = pl.pallas_call(
        key_send_kernel,
        out_shape=[jax.ShapeDtypeStruct((key_heads, rows, HEAD_SIZE), BF16)] * head_count,
        in_specs=[vmem],
        out_specs=[vmem] * head_count,
        compiler_params=small,
    )(keys)
    by_plane = list(by_plane)
    for other in range(1, head_count):
        by_plane[other] = swap(by_plane[other], "head", other)
    sent = pl.pallas_call(
        functools.partial(query_send_kernel, seq_count, head_count),
        out_shape=jax.ShapeDtypeStruct((devices, rows, HEAD_SIZE), BF16),
        in_specs=[vmem],
        out_specs=vmem,
        compiler_params=small,
    )(queries)
    arrived = lax.all_to_all(sent, ("seq", "head"), split_axis=0, concat_axis=0, tiled=True)
    by_key_head = pl.pallas_call(
        functools.partial(key_turn_kernel, share),
        out_shape=[jax.ShapeDtypeStruct((head_count, rows, HEAD_SIZE), BF16)] * key_heads,
        in_specs=[vmem] * head_count,
        out_specs=[vmem] * key_heads,
        compiler_params=small,
    )(*by_plane)
    pieces = [None] * seq_count
    for other in range(0, seq_count, 2):
        piece = by_key_head[other // share]
        pieces[other] = swap(piece, "seq", other) if other else piece
    for other in range(0, seq_count, 2):
        pieces[other + 1] = swap(pieces[other], "seq", 1)
    early = max(sequences // 2, 1)
    weights_shape = jax.ShapeDtypeStruct((HEAD_SIZE, HEAD_SIZE), F32)
    key_rows, phi_k, query_weights, key_weights = pl.pallas_call(
        functools.partial(key_kernel, share),
        out_shape=(
            jax.ShapeDtypeStruct((token_count, HEAD_SIZE), BF16),
            jax.ShapeDtypeStruct((early, 2 * HEAD_SIZE, seq_tokens), F32),
            weights_shape,
            weights_shape,
        ),
        in_specs=[smem] + [vmem] * (seq_count + 2),
        out_specs=(vmem,) * 4,
        compiler_params=pltpu.CompilerParams(vmem_limit_bytes=8 << 20),
        cost_estimate=pl.CostEstimate(
            flops=token_count * HEAD_SIZE * HEAD_SIZE * 6,
            bytes_accessed=token_count * HEAD_SIZE * 12,
            transcendentals=token_count * HEAD_SIZE * 2,
        ),
    )(block_pos, key_map, query_map, *pieces)
    grads = pl.pallas_call(
        functools.partial(pair_kernel, token_count, seq_count),
        out_shape=jax.ShapeDtypeStruct((3 * HEAD_SIZE, HEAD_SIZE), BF16),
        in_specs=[smem] + [vmem] * 5,
        out_specs=vmem,
        scratch_shapes=[
            pltpu.VMEM((token_count, HEAD_SIZE), BF16),
            pltpu.VMEM((sequences, 2 * HEAD_SIZE, seq_tokens), F32),
            pltpu.VMEM((sequences, 2 * HEAD_SIZE, seq_tokens), BF16),
            pltpu.VMEM((max(sequences - early, 1), 2 * HEAD_SIZE, seq_tokens), F32),
            pltpu.VMEM((sequences, 2 * HEAD_SIZE, seq_tokens), BF16),
            pltpu.VMEM((sequences, seq_tokens, 2 * HEAD_SIZE), BF16),
            pltpu.VMEM((sequences, seq_tokens, seq_tokens), BF16),
            pltpu.VMEM((sequences, 2, seq_tokens, 2 * BLK), F32),
            pltpu.VMEM((sequences, 2, seq_tokens, 2 * BLK), F32),
            pltpu.VMEM((HEAD_SIZE, HEAD_SIZE), F32),
            pltpu.VMEM((HEAD_SIZE, HEAD_SIZE), F32),
        ],
        compiler_params=pltpu.CompilerParams(vmem_limit_bytes=32 << 20),
    )(block_pos, arrived, query_weights, key_weights, key_rows, phi_k)
    everyone = lax.all_gather(grads, "seq", axis=0, tiled=False)
    return pl.pallas_call(
        collect_kernel,
        out_shape=(
            jax.ShapeDtypeStruct((seq_count, HEAD_SIZE, HEAD_SIZE), F32),
            jax.ShapeDtypeStruct((key_heads, HEAD_SIZE, HEAD_SIZE), F32),
        ),
        in_specs=[vmem],
        out_specs=(pl.BlockSpec(memory_space=pl.ANY),) * 2,
        scratch_shapes=[
            pltpu.VMEM((seq_count + key_heads, HEAD_SIZE, HEAD_SIZE), F32),
            pltpu.SemaphoreType.DMA((seq_count + key_heads,)),
        ],
        compiler_params=small,
    )(everyone)


def one_head_each(mesh, queries, keys, block_pos, query_map, key_map):
    del keys, block_pos
    seq_count, head_count = mesh.shape["seq"], mesh.shape["head"]
    rows = queries.shape[0] // (seq_count * head_count)
    key_heads = key_map.shape[0] // head_count
    return (
        query_map.shape[0] == seq_count * head_count
        and seq_count % (2 * key_heads) == 0
        and seq_count & (seq_count - 1) == 0
        and head_count & (head_count - 1) == 0
        and BLK % rows == 0
        and rows % 16 == 0
    )


def solution(mesh):
    in_specs = (
        P(("seq", "head"), None),
        P(("seq", "head"), None),
        P(),
        P("head", None, None),
        P("head", None, None),
    )
    out_specs = (P("head", None, None), P("head", None, None))

    def sharded(function):
        return jax.shard_map(
            function, mesh=mesh, in_specs=in_specs, out_specs=out_specs, check_vma=False
        )

    def step(*args):
        if one_head_each(mesh, *args):
            return sharded(per_device_head)(*args)
        return sharded(per_device_general)(*args)

    return step
```

```python
import functools
import math

import jax
import jax.numpy as jnp
from jax import lax
from jax.experimental import pallas as pl
from jax.experimental.pallas import tpu as pltpu
from jax.sharding import PartitionSpec as P


HEAD_SIZE = 128
BLK = 128

HIGHEST = lax.Precision.HIGHEST
NEG_FLOOR = -1e30


def softmax_pair(logits):
    return jnp.concatenate(
        [jax.nn.softmax(logits, axis=-1), jax.nn.softmax(-logits, axis=-1)], axis=-1
    )


def feature_grad(feature, upstream):
    half_width = feature.shape[-1] // 2
    positive, negative = (feature[..., :half_width], feature[..., half_width:])
    grad_positive, grad_negative = (upstream[..., :half_width], upstream[..., half_width:])
    first = positive * (grad_positive - jnp.sum(grad_positive * positive, axis=-1, keepdims=True))
    second = negative * (grad_negative - jnp.sum(grad_negative * negative, axis=-1, keepdims=True))
    return first - second


def row_places(row_index, block_pos, seq_count):
    stored = row_index // BLK
    lookup = stored[:, None] == jnp.arange(block_pos.shape[0], dtype=jnp.int32)[None, :]
    blocks = jnp.sum(jnp.where(lookup, block_pos[None, :], 0), axis=1)
    return (blocks // seq_count, blocks * BLK + row_index % BLK)


def over_blocks(running, portions, step_fn):
    row_count = portions[0].shape[1]
    step_rows = math.gcd(row_count, 512)

    def advance(number, inner_carry):
        slabs = tuple(
            (
                lax.dynamic_slice_in_dim(portion, number * step_rows, step_rows, 1)
                for portion in portions
            )
        )
        return step_fn(inner_carry, slabs, number * step_rows)

    return lax.fori_loop(0, row_count // step_rows, advance, running)


def per_device_general(queries, keys, block_pos, query_map, key_map):
    local_q, local_k = (
        lax.all_to_all(queries, "head", split_axis=1, concat_axis=0, tiled=True),
        lax.all_to_all(keys, "head", split_axis=1, concat_axis=0, tiled=True),
    )
    seq_count = lax.axis_size("seq")
    seq_rank = lax.axis_index("seq")
    rows_local = local_k.shape[0]
    token_count = rows_local * seq_count
    key_heads = key_map.shape[0]
    group_width = query_map.shape[0] // key_heads
    score_scale = HEAD_SIZE ** (-0.5)
    query_index = seq_rank * rows_local + jnp.arange(rows_local, dtype=jnp.int32)
    query_heads = local_q.reshape(rows_local, key_heads, group_width, HEAD_SIZE).transpose(
        1, 2, 0, 3
    )
    query_wide = query_heads.astype(jnp.float32)
    query_logits = jnp.einsum(
        "vgnd,vgde->vgne",
        query_wide,
        query_map.reshape(key_heads, group_width, HEAD_SIZE, HEAD_SIZE),
        precision=HIGHEST,
    )
    rows_all = group_width * rows_local
    phi_query = softmax_pair(query_logits).reshape(key_heads, rows_all, 2 * HEAD_SIZE)
    phi_query_b = phi_query.astype(jnp.bfloat16)
    query_flat = query_heads.reshape(key_heads, rows_all, HEAD_SIZE)
    query_seq, query_at = row_places(query_index, block_pos, seq_count)
    query_seq = jnp.tile(query_seq, group_width)
    query_at = jnp.tile(query_at, group_width)

    def visible_for(offset, slab_rows):
        key_index = offset + jnp.arange(slab_rows, dtype=jnp.int32)
        key_seq, key_at = row_places(key_index, block_pos, seq_count)
        return (key_seq[None, :] == query_seq[:, None]) & (key_at[None, :] <= query_at[:, None])

    def key_features(key_slab):
        logits = jnp.einsum(
            "vwd,vde->vwe", key_slab.astype(jnp.float32), key_map, precision=HIGHEST
        )
        return softmax_pair(logits)

    def teacher(key_slab):
        return (
            jnp.einsum("vrd,vwd->vrw", query_flat, key_slab, preferred_element_type=jnp.float32)
            * score_scale
        )

    def stats_step(running, slabs, offset):
        key_slab = slabs[0]
        visible = visible_for(offset, key_slab.shape[1])

        def stats_compute_live(current):
            highest, denominator, linear_sum = current
            masked = jnp.where(visible[None], teacher(key_slab), NEG_FLOOR)
            new_high = jnp.maximum(highest, jnp.max(masked, axis=-1))
            exponent = jnp.where(visible[None], jnp.exp(masked - new_high[..., None]), 0.0)
            denominator = denominator * jnp.exp(highest - new_high) + jnp.sum(exponent, axis=-1)
            phi_key_b = key_features(key_slab).astype(jnp.bfloat16)
            linear = jnp.einsum(
                "vrf,vwf->vrw", phi_query_b, phi_key_b, preferred_element_type=jnp.float32
            )
            linear_sum = linear_sum + jnp.sum(jnp.where(visible[None], linear, 0.0), axis=-1)
            return (new_high, denominator, linear_sum)

        return lax.cond(jnp.any(visible), stats_compute_live, lambda current: current, running)

    def grads_step(running, slabs, offset):
        key_slab = slabs[0]
        visible = visible_for(offset, key_slab.shape[1])

        def grads_compute_live(current):
            query_grad, key_weight_grad = current
            masked = jnp.where(visible[None], teacher(key_slab), NEG_FLOOR)
            exponent = jnp.where(visible[None], jnp.exp(masked - highest[..., None]), 0.0)
            teacher_prob = exponent / denominator[..., None]
            phi_key = key_features(key_slab)
            phi_key_b = phi_key.astype(jnp.bfloat16)
            linear = jnp.einsum(
                "vrf,vwf->vrw", phi_query_b, phi_key_b, preferred_element_type=jnp.float32
            )
            weights = (
                jnp.where(visible[None], 1.0 / linear_sum[..., None] - teacher_prob / linear, 0.0)
                / token_count
            ).astype(jnp.bfloat16)
            query_grad = query_grad + jnp.einsum(
                "vrw,vwf->vrf", weights, phi_key_b, preferred_element_type=jnp.float32
            )
            key_grad = jnp.einsum(
                "vrw,vrf->vwf", weights, phi_query_b, preferred_element_type=jnp.float32
            )
            key_logit_grad = feature_grad(phi_key, key_grad)
            key_weight_grad = key_weight_grad + jnp.einsum(
                "vwd,vwe->vde", key_slab.astype(jnp.float32), key_logit_grad, precision=HIGHEST
            )
            return (query_grad, key_weight_grad)

        return lax.cond(jnp.any(visible), grads_compute_live, lambda current: current, running)

    def as_heads(pieces):
        return pieces.reshape(pieces.shape[0], key_heads, -1).transpose(1, 0, 2)

    row_zeros = jnp.zeros((key_heads, rows_all), jnp.float32)
    stats_init = (jnp.full((key_heads, rows_all), NEG_FLOOR, jnp.float32), row_zeros, row_zeros)
    grads_init = (
        jnp.zeros((key_heads, rows_all, 2 * HEAD_SIZE), jnp.float32),
        jnp.zeros((key_heads, HEAD_SIZE, HEAD_SIZE), jnp.float32),
    )
    highest, denominator, linear_sum = over_blocks(
        stats_init, (as_heads(lax.all_gather(local_k, "seq", axis=0, tiled=True)),), stats_step
    )
    query_grad, key_weight_grad = over_blocks(
        grads_init, (as_heads(lax.all_gather(local_k, "seq", axis=0, tiled=True)),), grads_step
    )
    query_logit_grad = feature_grad(phi_query, query_grad).reshape(
        key_heads, group_width, rows_local, HEAD_SIZE
    )
    query_weight_grad = jnp.einsum(
        "vgnd,vgne->vgde", query_wide, query_logit_grad, precision=HIGHEST
    ).reshape(key_heads * group_width, HEAD_SIZE, HEAD_SIZE)
    query_map_gradient, key_map_gradient = lax.psum((query_weight_grad, key_weight_grad), "seq")
    return (query_map_gradient, key_map_gradient)


NT = (((1,), (1,)), ((), ()))
F32 = jnp.float32
BF16 = jnp.bfloat16


def nn(left, right):
    return jnp.dot(left, right, preferred_element_type=F32)


def nt(left, right):
    return lax.dot_general(left, right, NT, preferred_element_type=F32)


def bf16_parts(value, count):
    parts = []
    for _ in range(count):
        part = value.astype(BF16)
        parts.append(part)
        value = value - part.astype(F32)
    return jnp.concatenate(parts, axis=0)


def features_t(logits):
    up = jnp.exp(logits - jnp.max(logits, axis=0, keepdims=True))
    down = jnp.exp(jnp.min(logits, axis=0, keepdims=True) - logits)
    up = up * (1.0 / jnp.sum(up, axis=0, keepdims=True))
    down = down * (1.0 / jnp.sum(down, axis=0, keepdims=True))
    return jnp.concatenate([up, down], axis=0)


def feature_grad_t(feature, upstream):
    halves = []
    for half in (slice(0, HEAD_SIZE), slice(HEAD_SIZE, 2 * HEAD_SIZE)):
        value, grad = feature[half], upstream[half]
        halves.append(value * (grad - jnp.sum(grad * value, axis=0, keepdims=True)))
    return halves[0] - halves[1]


def tile_sum(value):
    return jnp.sum(value.reshape(-1, 8, value.shape[-1]), axis=0)


def tile_max(value):
    return jnp.max(value.reshape(-1, 8, value.shape[-1]), axis=0)


def side_parts(value):
    high = value.astype(BF16)
    return jnp.concatenate([high, (value - high.astype(F32)).astype(BF16)], axis=1)


def map_parts(weights):
    rest = weights.T
    parts = []
    for _ in range(3):
        parts.append(rest.astype(BF16))
        rest = rest - parts[-1].astype(F32)
    return jnp.concatenate(parts[::-1], axis=1)


def logits_t(parts, tokens):
    return nt(parts, jnp.concatenate([tokens] * 3, axis=1))


def send_kernel(seq_count, queries_ref, keys_ref, *refs):
    queries_out_ref, *keys_out_refs, query_buffer, key_buffer, sems, query_sems, key_sems = refs
    head_count = len(keys_out_refs)
    key_heads = keys_out_refs[0].shape[0]
    keys_in = pltpu.make_async_copy(keys_ref, key_buffer, sems.at[0])
    queries_in = pltpu.make_async_copy(queries_ref, query_buffer, sems.at[1])
    keys_in.start()
    queries_in.start()
    leaving = []
    keys_in.wait()
    for other, out_ref in enumerate(keys_out_refs):
        for number in range(key_heads):
            column = ((lax.axis_index("head") ^ other) * key_heads + number) * HEAD_SIZE
            column = pl.multiple_of(column, HEAD_SIZE)
            leaving.append(
                pltpu.make_async_copy(
                    key_buffer.at[:, pl.ds(column, HEAD_SIZE)],
                    out_ref.at[number],
                    key_sems.at[other, number],
                )
            )
            leaving[-1].start()
    queries_in.wait()
    for head in range(head_count):
        for seq in range(seq_count):
            column = (head * seq_count + seq) * HEAD_SIZE
            target = seq * head_count + head
            leaving.append(
                pltpu.make_async_copy(
                    query_buffer.at[:, column : column + HEAD_SIZE],
                    queries_out_ref.at[target],
                    query_sems.at[target],
                )
            )
            leaving[-1].start()
    for copy in leaving:
        copy.wait()


def key_turn_kernel(share, *refs):
    key_heads = refs[0].shape[0]
    in_refs, out_refs = refs[:-key_heads], refs[-key_heads:]
    mine = lax.div(lax.axis_index("seq"), share)
    for other, out_ref in enumerate(out_refs):
        for number, in_ref in enumerate(in_refs):
            out_ref[number] = in_ref[mine ^ other]


def sorted_rows(pos_ref, chunk, rows):
    per_block = BLK // rows
    first = pos_ref[lax.div(chunk, per_block)] * BLK + lax.rem(chunk, per_block) * rows
    return pl.ds(pl.multiple_of(first, rows), rows)


def block(at):
    return slice(at * BLK, (at + 1) * BLK)


def key_kernel(share, pos_ref, key_map_ref, query_map_ref, *refs):
    seq_count, head_count = lax.axis_size("seq"), lax.axis_size("head")
    piece_refs, refs = refs[:seq_count], refs[seq_count:]
    key_rows, phi, query_weights_ref, key_weights_ref = refs
    rows = piece_refs[0].shape[1]
    seq_blocks = phi.shape[2] // BLK
    blocks = phi.shape[0] * seq_blocks
    mine, plane = lax.axis_index("seq"), lax.axis_index("head")
    query_weights_ref[...] = query_map_ref[mine]
    for other in range(seq_count):
        for number in range(head_count):
            chunk = (mine ^ other) * head_count + (plane ^ number)
            key_rows[sorted_rows(pos_ref, chunk, rows), :] = piece_refs[other][number]
    key_weights_ref[...] = key_map_ref[lax.div(mine, share)]
    parts = map_parts(key_weights_ref[...])
    ahead = []
    for number in range(blocks):
        while number + len(ahead) < min(number + 3, blocks):
            ahead.append(logits_t(parts, key_rows[block(number + len(ahead)), :]))
        seq, at = divmod(number, seq_blocks)
        phi[seq, :, block(at)] = features_t(ahead.pop(0))


def pair_kernel(
    token_count,
    seq_blocks,
    pos_ref,
    arrived_ref,
    query_weights_ref,
    key_weights_ref,
    key_rows,
    phi_k_early,
    out_ref,
    query_rows,
    phi_q,
    phi_qb,
    phi_k_late,
    phi_kb,
    phi_kb_rows,
    pair_weights,
    scores,
    linears,
    acc_q,
    acc_k,
):
    rows = arrived_ref.shape[1]
    seq_tokens = seq_blocks * BLK
    sequences = token_count // seq_tokens
    acc_q[...] = jnp.zeros_like(acc_q)
    acc_k[...] = jnp.zeros_like(acc_k)
    width = 2 if seq_blocks % 2 == 0 else 1
    tiles = seq_blocks // width
    for seq in range(sequences):
        for at in range(0, seq_blocks, width):
            if width > 1:
                pair_weights[seq, block(at + 1), block(at)] = jnp.zeros((BLK, BLK), BF16)
    parts = map_parts(query_weights_ref[...])
    key_parts = map_parts(key_weights_ref[...])
    early = phi_k_early.shape[0]
    lane = lax.broadcasted_iota(jnp.int32, (BLK, BLK), 1)
    sublane = lax.broadcasted_iota(jnp.int32, (BLK, BLK), 0)
    unit = jnp.where(lane == sublane, 1.0, 0.0).astype(BF16)
    visible = sublane <= lane
    exponent_scale = HEAD_SIZE ** (-0.5) * math.log2(math.e)

    def span(tile):
        return slice(tile * width * BLK, (tile + 1) * width * BLK)

    def flat(seq, here):
        return slice(seq * seq_tokens + here.start, seq * seq_tokens + here.stop)

    def query_logits(seq, at):
        return logits_t(parts, query_rows[flat(seq, block(at)), :])

    def query_features(seq, at, logits):
        feature = features_t(logits)
        phi_q[seq, :, block(at)] = feature
        phi_qb[seq, :, block(at)] = feature.astype(BF16)

    def phi_k(seq, at):
        if seq < early:
            return phi_k_early[seq, :, block(at)]
        return phi_k_late[seq - early, :, block(at)]

    def key_logits(seq, at):
        if seq < early:
            return None
        return logits_t(key_parts, key_rows[flat(seq, block(at)), :])

    def key_features(seq, at, logits):
        if seq >= early:
            phi_k_late[seq - early, :, block(at)] = features_t(logits)

    def turn_features(seq, at):
        rounded = phi_k(seq, at).astype(BF16)
        phi_kb[seq, :, block(at)] = rounded
        phi_kb_rows[seq, block(at), :] = nt(unit, rounded).astype(BF16)

    def pair_scores(seq, tile):
        here = span(tile)
        slot = tile % 2
        teacher = nt(key_rows[flat(seq, slice(0, here.stop)), :], query_rows[flat(seq, here), :])
        student = nn(phi_kb_rows[seq, : here.stop, :], phi_qb[seq, :, here])
        stats = []
        for half in range(width):
            at = tile * width + half
            highest = linear_sum = None
            for number in range(at + 1):
                score = teacher[block(number), block(half)]
                linear = student[block(number), block(half)]
                linears[seq, slot, block(number), block(half)] = linear
                if number == at:
                    score = jnp.where(visible, score, NEG_FLOOR)
                    linear = jnp.where(visible, linear, 0.0)
                scores[seq, slot, block(number), block(half)] = score
                top, total = tile_max(score), tile_sum(linear)
                highest = top if number == 0 else jnp.maximum(highest, top)
                linear_sum = total if number == 0 else linear_sum + total
            stats.append(
                (
                    jnp.max(highest, axis=0, keepdims=True),
                    jnp.sum(linear_sum, axis=0, keepdims=True),
                )
            )
        return stats

    def pair_gradients(seq, tile, half, stats):
        highest, linear_sum = stats
        slot = tile % 2
        at = tile * width + half
        denominator = None
        for number in range(at + 1):
            score = scores[seq, slot, block(number), block(half)]
            exponent = jnp.exp2((score - highest) * exponent_scale)
            scores[seq, slot, block(number), block(half)] = exponent
            total = tile_sum(exponent)
            denominator = total if number == 0 else denominator + total
        denominator = jnp.sum(denominator, axis=0, keepdims=True)
        base = 1.0 / (linear_sum * token_count)
        rate = 1.0 / (denominator * token_count)
        for number in range(at + 1):
            exponent = scores[seq, slot, block(number), block(half)]
            weights = base - exponent * rate / linears[seq, slot, block(number), block(half)]
            if number == at:
                weights = jnp.where(visible, weights, 0.0)
            pair_weights[seq, block(number), block(at)] = weights.astype(BF16)

    def map_change(phis, upstream, tokens):
        changes = [
            side_parts(feature_grad_t(phi, upstream[:, block(half)]))
            for half, phi in enumerate(phis)
        ]
        twice = [tokens[block(half)] for half in range(width) for _ in range(2)]
        return nn(jnp.concatenate(changes, axis=1), jnp.concatenate(twice, axis=0))

    def query_upstream(seq, tile):
        here = span(tile)
        return nn(phi_kb[seq, :, : here.stop], pair_weights[seq, : here.stop, here])

    def query_change(seq, tile, upstream):
        phis = [phi_q[seq, :, block(tile * width + half)] for half in range(width)]
        acc_q[...] += map_change(phis, upstream, query_rows[flat(seq, span(tile)), :])

    def key_upstream(seq, tile):
        later = slice(tile * width * BLK, seq_blocks * BLK)
        return nt(phi_qb[seq, :, later], pair_weights[seq, span(tile), later])

    def key_change(seq, tile, upstream):
        phis = [phi_k(seq, tile * width + half) for half in range(width)]
        acc_k[...] += map_change(phis, upstream, key_rows[flat(seq, span(tile)), :])

    def feature_steps(seq):
        ahead = [key_logits(seq, at) for at in range(min(3, seq_blocks))]
        for at in range(seq_blocks):
            if at + len(ahead) < seq_blocks:
                ahead.append(key_logits(seq, at + len(ahead)))
            key_features(seq, at, ahead.pop(0))
            if at > 1:
                turn_features(seq, at - 2)
            yield
        for at in range(max(seq_blocks - 2, 0), seq_blocks):
            turn_features(seq, at)

    def feature_steps(seq):
        ahead = []
        for at in range(seq_blocks):
            while at + len(ahead) < min(at + 3, seq_blocks):
                later = at + len(ahead)
                ahead.append((key_logits(seq, later), query_logits(seq, later)))
            from_keys, from_queries = ahead.pop(0)
            key_features(seq, at, from_keys)
            query_features(seq, at, from_queries)
            if at:
                turn_features(seq, at - 1)
            yield
        turn_features(seq, seq_blocks - 1)

    def pair_steps(seq):
        order = list(reversed(range(tiles)))
        ahead = pair_scores(seq, order[0])
        behind = None
        for number, tile in enumerate(order):
            stats = ahead
            if number + 1 < tiles:
                ahead = pair_scores(seq, order[number + 1])
            for half in range(width):
                pair_gradients(seq, tile, half, stats[half])
                yield
            upstreams = query_upstream(seq, tile), key_upstream(seq, tile)
            if behind:
                query_change(seq, order[number - 1], behind[0])
                key_change(seq, order[number - 1], behind[1])
            behind = upstreams
        yield
        query_change(seq, order[-1], behind[0])
        key_change(seq, order[-1], behind[1])

    for chunk in range(token_count // rows):
        query_rows[sorted_rows(pos_ref, chunk, rows), :] = arrived_ref[chunk]
    stages = (feature_steps, pair_steps)
    for turn in range(sequences + len(stages) - 1):
        active = [
            stage(turn - number)
            for number, stage in enumerate(stages)
            if 0 <= turn - number < sequences
        ]
        while active:
            for step in list(active):
                if next(step, step) is step:
                    active.remove(step)
    out_ref[:HEAD_SIZE, :] = acc_q[...].T.astype(BF16)
    out_ref[HEAD_SIZE:, :] = bf16_parts(acc_k[...].T, 2)


def collect_kernel(everyone_ref, queries_out_ref, keys_out_ref, buffer, sems):
    seq_count = queries_out_ref.shape[0]
    key_heads = keys_out_ref.shape[0]
    share = seq_count // key_heads
    copies = []

    def leave(number, value, out_ref):
        buffer[number] = value
        copies.append(pltpu.make_async_copy(buffer.at[number], out_ref, sems.at[number]))
        copies[-1].start()

    for number in range(seq_count):
        leave(number, everyone_ref[number, :HEAD_SIZE, :].astype(F32), queries_out_ref.at[number])
    for number in range(key_heads):
        total = None
        for seq in range(number * share, (number + 1) * share):
            for half in (1, 2):
                rows = slice(half * HEAD_SIZE, (half + 1) * HEAD_SIZE)
                value = everyone_ref[seq, rows, :].astype(F32)
                total = value if total is None else total + value
        leave(seq_count + number, total, keys_out_ref.at[number])
    for copy in copies:
        copy.wait()


def per_device_head(queries, keys, block_pos, query_map, key_map):
    seq_count = lax.axis_size("seq")
    head_count = lax.axis_size("head")
    key_heads = key_map.shape[0]
    share = seq_count // key_heads
    rows = queries.shape[0]
    devices = seq_count * head_count
    token_count = rows * devices
    seq_tokens = seq_count * BLK
    sequences = token_count // seq_tokens
    vmem = pl.BlockSpec(memory_space=pltpu.VMEM)
    smem = pl.BlockSpec(memory_space=pltpu.SMEM)

    def swap(piece, axis, bits):
        size = lax.axis_size(axis)
        return lax.ppermute(piece, axis, [(i, i ^ bits) for i in range(size)])

    small = pltpu.CompilerParams(vmem_limit_bytes=4 << 20)
    anywhere = pl.BlockSpec(memory_space=pl.ANY)
    sent, *by_plane = pl.pallas_call(
        functools.partial(send_kernel, seq_count),
        out_shape=[jax.ShapeDtypeStruct((devices, rows, HEAD_SIZE), BF16)]
        + [jax.ShapeDtypeStruct((key_heads, rows, HEAD_SIZE), BF16)] * head_count,
        in_specs=[anywhere] * 2,
        out_specs=[anywhere] * (head_count + 1),
        scratch_shapes=[
            pltpu.VMEM(queries.shape, BF16),
            pltpu.VMEM(keys.shape, BF16),
            pltpu.SemaphoreType.DMA((2,)),
            pltpu.SemaphoreType.DMA((devices,)),
            pltpu.SemaphoreType.DMA((head_count, key_heads)),
        ],
        compiler_params=pltpu.CompilerParams(vmem_limit_bytes=60 << 20),
    )(queries, keys)
    for other in range(1, head_count):
        by_plane[other] = swap(by_plane[other], "head", other)
    arrived = lax.all_to_all(sent, ("seq", "head"), split_axis=0, concat_axis=0, tiled=True)
    by_key_head = pl.pallas_call(
        functools.partial(key_turn_kernel, share),
        out_shape=[jax.ShapeDtypeStruct((head_count, rows, HEAD_SIZE), BF16)] * key_heads,
        in_specs=[vmem] * head_count,
        out_specs=[vmem] * key_heads,
        compiler_params=small,
    )(*by_plane)
    pieces = [None] * seq_count
    for other in range(0, seq_count, 2):
        piece = by_key_head[other // share]
        pieces[other] = swap(piece, "seq", other) if other else piece
    for other in range(0, seq_count, 2):
        pieces[other + 1] = swap(pieces[other], "seq", 1)
    early = max(sequences // 2, 1)
    weights_shape = jax.ShapeDtypeStruct((HEAD_SIZE, HEAD_SIZE), F32)
    key_rows, phi_k, query_weights, key_weights = pl.pallas_call(
        functools.partial(key_kernel, share),
        out_shape=(
            jax.ShapeDtypeStruct((token_count, HEAD_SIZE), BF16),
            jax.ShapeDtypeStruct((early, 2 * HEAD_SIZE, seq_tokens), F32),
            weights_shape,
            weights_shape,
        ),
        in_specs=[smem] + [vmem] * (seq_count + 2),
        out_specs=(vmem,) * 4,
        compiler_params=pltpu.CompilerParams(vmem_limit_bytes=8 << 20),
        cost_estimate=pl.CostEstimate(
            flops=token_count * HEAD_SIZE * HEAD_SIZE * 6,
            bytes_accessed=token_count * HEAD_SIZE * 12,
            transcendentals=token_count * HEAD_SIZE * 2,
        ),
    )(block_pos, key_map, query_map, *pieces)
    grads = pl.pallas_call(
        functools.partial(pair_kernel, token_count, seq_count),
        out_shape=jax.ShapeDtypeStruct((3 * HEAD_SIZE, HEAD_SIZE), BF16),
        in_specs=[smem] + [vmem] * 5,
        out_specs=vmem,
        scratch_shapes=[
            pltpu.VMEM((token_count, HEAD_SIZE), BF16),
            pltpu.VMEM((sequences, 2 * HEAD_SIZE, seq_tokens), F32),
            pltpu.VMEM((sequences, 2 * HEAD_SIZE, seq_tokens), BF16),
            pltpu.VMEM((max(sequences - early, 1), 2 * HEAD_SIZE, seq_tokens), F32),
            pltpu.VMEM((sequences, 2 * HEAD_SIZE, seq_tokens), BF16),
            pltpu.VMEM((sequences, seq_tokens, 2 * HEAD_SIZE), BF16),
            pltpu.VMEM((sequences, seq_tokens, seq_tokens), BF16),
            pltpu.VMEM((sequences, 2, seq_tokens, 2 * BLK), F32),
            pltpu.VMEM((sequences, 2, seq_tokens, 2 * BLK), F32),
            pltpu.VMEM((HEAD_SIZE, HEAD_SIZE), F32),
            pltpu.VMEM((HEAD_SIZE, HEAD_SIZE), F32),
        ],
        compiler_params=pltpu.CompilerParams(vmem_limit_bytes=32 << 20),
    )(block_pos, arrived, query_weights, key_weights, key_rows, phi_k)
    everyone = lax.all_gather(grads, "seq", axis=0, tiled=False)
    return pl.pallas_call(
        collect_kernel,
        out_shape=(
            jax.ShapeDtypeStruct((seq_count, HEAD_SIZE, HEAD_SIZE), F32),
            jax.ShapeDtypeStruct((key_heads, HEAD_SIZE, HEAD_SIZE), F32),
        ),
        in_specs=[vmem],
        out_specs=(pl.BlockSpec(memory_space=pl.ANY),) * 2,
        scratch_shapes=[
            pltpu.VMEM((seq_count + key_heads, HEAD_SIZE, HEAD_SIZE), F32),
            pltpu.SemaphoreType.DMA((seq_count + key_heads,)),
        ],
        compiler_params=small,
    )(everyone)


def one_head_each(mesh, queries, keys, block_pos, query_map, key_map):
    del keys, block_pos
    seq_count, head_count = mesh.shape["seq"], mesh.shape["head"]
    rows = queries.shape[0] // (seq_count * head_count)
    key_heads = key_map.shape[0] // head_count
    return (
        query_map.shape[0] == seq_count * head_count
        and seq_count % (2 * key_heads) == 0
        and seq_count & (seq_count - 1) == 0
        and head_count & (head_count - 1) == 0
        and BLK % rows == 0
        and rows % 16 == 0
    )


def solution(mesh):
    in_specs = (
        P(("seq", "head"), None),
        P(("seq", "head"), None),
        P(),
        P("head", None, None),
        P("head", None, None),
    )
    out_specs = (P("head", None, None), P("head", None, None))

    def sharded(function):
        return jax.shard_map(
            function, mesh=mesh, in_specs=in_specs, out_specs=out_specs, check_vma=False
        )

    def step(*args):
        if one_head_each(mesh, *args):
            return sharded(per_device_head)(*args)
        return sharded(per_device_general)(*args)

    return step
```

```python
import functools
import math

import jax
import jax.numpy as jnp
from jax import lax
from jax.experimental import pallas as pl
from jax.experimental.pallas import tpu as pltpu
from jax.sharding import PartitionSpec as P


HEAD_SIZE = 128
BLK = 128

HIGHEST = lax.Precision.HIGHEST
NEG_FLOOR = -1e30


def softmax_pair(logits):
    return jnp.concatenate(
        [jax.nn.softmax(logits, axis=-1), jax.nn.softmax(-logits, axis=-1)], axis=-1
    )


def feature_grad(feature, upstream):
    half_width = feature.shape[-1] // 2
    positive, negative = (feature[..., :half_width], feature[..., half_width:])
    grad_positive, grad_negative = (upstream[..., :half_width], upstream[..., half_width:])
    first = positive * (grad_positive - jnp.sum(grad_positive * positive, axis=-1, keepdims=True))
    second = negative * (grad_negative - jnp.sum(grad_negative * negative, axis=-1, keepdims=True))
    return first - second


def row_places(row_index, block_pos, seq_count):
    stored = row_index // BLK
    lookup = stored[:, None] == jnp.arange(block_pos.shape[0], dtype=jnp.int32)[None, :]
    blocks = jnp.sum(jnp.where(lookup, block_pos[None, :], 0), axis=1)
    return (blocks // seq_count, blocks * BLK + row_index % BLK)


def over_blocks(running, portions, step_fn):
    row_count = portions[0].shape[1]
    step_rows = math.gcd(row_count, 512)

    def advance(number, inner_carry):
        slabs = tuple(
            (
                lax.dynamic_slice_in_dim(portion, number * step_rows, step_rows, 1)
                for portion in portions
            )
        )
        return step_fn(inner_carry, slabs, number * step_rows)

    return lax.fori_loop(0, row_count // step_rows, advance, running)


def per_device_general(queries, keys, block_pos, query_map, key_map):
    local_q, local_k = (
        lax.all_to_all(queries, "head", split_axis=1, concat_axis=0, tiled=True),
        lax.all_to_all(keys, "head", split_axis=1, concat_axis=0, tiled=True),
    )
    seq_count = lax.axis_size("seq")
    seq_rank = lax.axis_index("seq")
    rows_local = local_k.shape[0]
    token_count = rows_local * seq_count
    key_heads = key_map.shape[0]
    group_width = query_map.shape[0] // key_heads
    score_scale = HEAD_SIZE ** (-0.5)
    query_index = seq_rank * rows_local + jnp.arange(rows_local, dtype=jnp.int32)
    query_heads = local_q.reshape(rows_local, key_heads, group_width, HEAD_SIZE).transpose(
        1, 2, 0, 3
    )
    query_wide = query_heads.astype(jnp.float32)
    query_logits = jnp.einsum(
        "vgnd,vgde->vgne",
        query_wide,
        query_map.reshape(key_heads, group_width, HEAD_SIZE, HEAD_SIZE),
        precision=HIGHEST,
    )
    rows_all = group_width * rows_local
    phi_query = softmax_pair(query_logits).reshape(key_heads, rows_all, 2 * HEAD_SIZE)
    phi_query_b = phi_query.astype(jnp.bfloat16)
    query_flat = query_heads.reshape(key_heads, rows_all, HEAD_SIZE)
    query_seq, query_at = row_places(query_index, block_pos, seq_count)
    query_seq = jnp.tile(query_seq, group_width)
    query_at = jnp.tile(query_at, group_width)

    def visible_for(offset, slab_rows):
        key_index = offset + jnp.arange(slab_rows, dtype=jnp.int32)
        key_seq, key_at = row_places(key_index, block_pos, seq_count)
        return (key_seq[None, :] == query_seq[:, None]) & (key_at[None, :] <= query_at[:, None])

    def key_features(key_slab):
        logits = jnp.einsum(
            "vwd,vde->vwe", key_slab.astype(jnp.float32), key_map, precision=HIGHEST
        )
        return softmax_pair(logits)

    def teacher(key_slab):
        return (
            jnp.einsum("vrd,vwd->vrw", query_flat, key_slab, preferred_element_type=jnp.float32)
            * score_scale
        )

    def stats_step(running, slabs, offset):
        key_slab = slabs[0]
        visible = visible_for(offset, key_slab.shape[1])

        def stats_compute_live(current):
            highest, denominator, linear_sum = current
            masked = jnp.where(visible[None], teacher(key_slab), NEG_FLOOR)
            new_high = jnp.maximum(highest, jnp.max(masked, axis=-1))
            exponent = jnp.where(visible[None], jnp.exp(masked - new_high[..., None]), 0.0)
            denominator = denominator * jnp.exp(highest - new_high) + jnp.sum(exponent, axis=-1)
            phi_key_b = key_features(key_slab).astype(jnp.bfloat16)
            linear = jnp.einsum(
                "vrf,vwf->vrw", phi_query_b, phi_key_b, preferred_element_type=jnp.float32
            )
            linear_sum = linear_sum + jnp.sum(jnp.where(visible[None], linear, 0.0), axis=-1)
            return (new_high, denominator, linear_sum)

        return lax.cond(jnp.any(visible), stats_compute_live, lambda current: current, running)

    def grads_step(running, slabs, offset):
        key_slab = slabs[0]
        visible = visible_for(offset, key_slab.shape[1])

        def grads_compute_live(current):
            query_grad, key_weight_grad = current
            masked = jnp.where(visible[None], teacher(key_slab), NEG_FLOOR)
            exponent = jnp.where(visible[None], jnp.exp(masked - highest[..., None]), 0.0)
            teacher_prob = exponent / denominator[..., None]
            phi_key = key_features(key_slab)
            phi_key_b = phi_key.astype(jnp.bfloat16)
            linear = jnp.einsum(
                "vrf,vwf->vrw", phi_query_b, phi_key_b, preferred_element_type=jnp.float32
            )
            weights = (
                jnp.where(visible[None], 1.0 / linear_sum[..., None] - teacher_prob / linear, 0.0)
                / token_count
            ).astype(jnp.bfloat16)
            query_grad = query_grad + jnp.einsum(
                "vrw,vwf->vrf", weights, phi_key_b, preferred_element_type=jnp.float32
            )
            key_grad = jnp.einsum(
                "vrw,vrf->vwf", weights, phi_query_b, preferred_element_type=jnp.float32
            )
            key_logit_grad = feature_grad(phi_key, key_grad)
            key_weight_grad = key_weight_grad + jnp.einsum(
                "vwd,vwe->vde", key_slab.astype(jnp.float32), key_logit_grad, precision=HIGHEST
            )
            return (query_grad, key_weight_grad)

        return lax.cond(jnp.any(visible), grads_compute_live, lambda current: current, running)

    def as_heads(pieces):
        return pieces.reshape(pieces.shape[0], key_heads, -1).transpose(1, 0, 2)

    row_zeros = jnp.zeros((key_heads, rows_all), jnp.float32)
    stats_init = (jnp.full((key_heads, rows_all), NEG_FLOOR, jnp.float32), row_zeros, row_zeros)
    grads_init = (
        jnp.zeros((key_heads, rows_all, 2 * HEAD_SIZE), jnp.float32),
        jnp.zeros((key_heads, HEAD_SIZE, HEAD_SIZE), jnp.float32),
    )
    highest, denominator, linear_sum = over_blocks(
        stats_init, (as_heads(lax.all_gather(local_k, "seq", axis=0, tiled=True)),), stats_step
    )
    query_grad, key_weight_grad = over_blocks(
        grads_init, (as_heads(lax.all_gather(local_k, "seq", axis=0, tiled=True)),), grads_step
    )
    query_logit_grad = feature_grad(phi_query, query_grad).reshape(
        key_heads, group_width, rows_local, HEAD_SIZE
    )
    query_weight_grad = jnp.einsum(
        "vgnd,vgne->vgde", query_wide, query_logit_grad, precision=HIGHEST
    ).reshape(key_heads * group_width, HEAD_SIZE, HEAD_SIZE)
    query_map_gradient, key_map_gradient = lax.psum((query_weight_grad, key_weight_grad), "seq")
    return (query_map_gradient, key_map_gradient)


NT = (((1,), (1,)), ((), ()))
F32 = jnp.float32
BF16 = jnp.bfloat16


def nn(left, right):
    return jnp.dot(left, right, preferred_element_type=F32)


def nt(left, right):
    return lax.dot_general(left, right, NT, preferred_element_type=F32)


def bf16_parts(value, count):
    parts = []
    for _ in range(count):
        part = value.astype(BF16)
        parts.append(part)
        value = value - part.astype(F32)
    return jnp.concatenate(parts, axis=0)


def features_t(logits):
    up = jnp.exp2(logits - jnp.max(logits, axis=0, keepdims=True))
    down = jnp.exp2(jnp.min(logits, axis=0, keepdims=True) - logits)
    up = up * (1.0 / jnp.sum(up, axis=0, keepdims=True))
    down = down * (1.0 / jnp.sum(down, axis=0, keepdims=True))
    return jnp.concatenate([up, down], axis=0)


def feature_grad_t(feature, upstream):
    halves = []
    for half in (slice(0, HEAD_SIZE), slice(HEAD_SIZE, 2 * HEAD_SIZE)):
        value, grad = feature[half], upstream[half]
        halves.append(value * (grad - jnp.sum(grad * value, axis=0, keepdims=True)))
    return halves[0] - halves[1]


def tile_sum(value):
    return jnp.sum(value.reshape(-1, 8, value.shape[-1]), axis=0)


def tile_max(value):
    return jnp.max(value.reshape(-1, 8, value.shape[-1]), axis=0)


def side_parts(value):
    high = value.astype(BF16)
    return jnp.concatenate([high, (value - high.astype(F32)).astype(BF16)], axis=1)


def map_parts(weights):
    rest = weights.T * math.log2(math.e)
    parts = []
    for _ in range(3):
        parts.append(rest.astype(BF16))
        rest = rest - parts[-1].astype(F32)
    return jnp.concatenate(parts[::-1], axis=1)


def logits_t(parts, tokens):
    return nt(parts, jnp.concatenate([tokens] * 3, axis=1))


def send_kernel(seq_count, queries_ref, keys_ref, *refs):
    queries_out_ref, *keys_out_refs, query_buffer, key_buffer, sems, query_sems, key_sems = refs
    head_count = len(keys_out_refs)
    key_heads = keys_out_refs[0].shape[0]
    keys_in = pltpu.make_async_copy(keys_ref, key_buffer, sems.at[0])
    queries_in = pltpu.make_async_copy(queries_ref, query_buffer, sems.at[1])
    keys_in.start()
    queries_in.start()
    leaving = []
    keys_in.wait()
    for other, out_ref in enumerate(keys_out_refs):
        for number in range(key_heads):
            column = ((lax.axis_index("head") ^ other) * key_heads + number) * HEAD_SIZE
            column = pl.multiple_of(column, HEAD_SIZE)
            leaving.append(
                pltpu.make_async_copy(
                    key_buffer.at[:, pl.ds(column, HEAD_SIZE)],
                    out_ref.at[number],
                    key_sems.at[other, number],
                )
            )
            leaving[-1].start()
    queries_in.wait()
    for head in range(head_count):
        for seq in range(seq_count):
            column = (head * seq_count + seq) * HEAD_SIZE
            target = seq * head_count + head
            leaving.append(
                pltpu.make_async_copy(
                    query_buffer.at[:, column : column + HEAD_SIZE],
                    queries_out_ref.at[target],
                    query_sems.at[target],
                )
            )
            leaving[-1].start()
    for copy in leaving:
        copy.wait()


def key_turn_kernel(share, *refs):
    key_heads = refs[0].shape[0]
    in_refs, out_refs = refs[:-key_heads], refs[-key_heads:]
    mine = lax.div(lax.axis_index("seq"), share)
    for other, out_ref in enumerate(out_refs):
        for number, in_ref in enumerate(in_refs):
            out_ref[number] = in_ref[mine ^ other]


def sorted_rows(pos_ref, chunk, rows):
    per_block = BLK // rows
    first = pos_ref[lax.div(chunk, per_block)] * BLK + lax.rem(chunk, per_block) * rows
    return pl.ds(pl.multiple_of(first, rows), rows)


def block(at):
    return slice(at * BLK, (at + 1) * BLK)


def key_kernel(share, pos_ref, key_map_ref, query_map_ref, *refs):
    seq_count, head_count = lax.axis_size("seq"), lax.axis_size("head")
    piece_refs, refs = refs[:seq_count], refs[seq_count:]
    key_rows, phi, query_weights_ref, key_weights_ref = refs
    rows = piece_refs[0].shape[1]
    seq_blocks = phi.shape[2] // BLK
    blocks = phi.shape[0] * seq_blocks
    mine, plane = lax.axis_index("seq"), lax.axis_index("head")
    query_weights_ref[...] = query_map_ref[mine]
    for other in range(seq_count):
        for number in range(head_count):
            chunk = (mine ^ other) * head_count + (plane ^ number)
            key_rows[sorted_rows(pos_ref, chunk, rows), :] = piece_refs[other][number]
    key_weights_ref[...] = key_map_ref[lax.div(mine, share)]
    parts = map_parts(key_weights_ref[...])
    ahead = []
    for number in range(blocks):
        while number + len(ahead) < min(number + 3, blocks):
            ahead.append(logits_t(parts, key_rows[block(number + len(ahead)), :]))
        seq, at = divmod(number, seq_blocks)
        phi[seq, :, block(at)] = features_t(ahead.pop(0))


def pair_kernel(
    token_count,
    seq_blocks,
    pos_ref,
    arrived_ref,
    query_weights_ref,
    key_weights_ref,
    key_rows,
    phi_k_early,
    out_ref,
    query_rows,
    phi_q,
    phi_qb,
    phi_k_late,
    phi_kb,
    phi_kb_rows,
    pair_weights,
    scores,
    linears,
    acc_q,
    acc_k,
):
    rows = arrived_ref.shape[1]
    seq_tokens = seq_blocks * BLK
    sequences = token_count // seq_tokens
    acc_q[...] = jnp.zeros_like(acc_q)
    acc_k[...] = jnp.zeros_like(acc_k)
    width = 2 if seq_blocks % 2 == 0 else 1
    tiles = seq_blocks // width
    for seq in range(sequences):
        for at in range(0, seq_blocks, width):
            if width > 1:
                pair_weights[seq, at, block(at + 1), :] = jnp.zeros((BLK, BLK), BF16)
    parts = map_parts(query_weights_ref[...])
    key_parts = map_parts(key_weights_ref[...])
    early = phi_k_early.shape[0]
    lane = lax.broadcasted_iota(jnp.int32, (BLK, BLK), 1)
    sublane = lax.broadcasted_iota(jnp.int32, (BLK, BLK), 0)
    visible = sublane <= lane
    exponent_scale = HEAD_SIZE ** (-0.5) * math.log2(math.e)

    def side_by_side(pieces):
        return jnp.concatenate(list(pieces), axis=1)

    def blocks_of(here):
        return range(here.start // BLK, here.stop // BLK)

    def span(tile):
        return slice(tile * width * BLK, (tile + 1) * width * BLK)

    def flat(seq, here):
        return slice(seq * seq_tokens + here.start, seq * seq_tokens + here.stop)

    def query_logits(seq, at):
        return logits_t(parts, query_rows[flat(seq, block(at)), :])

    def query_features(seq, at, logits):
        feature = features_t(logits)
        phi_q[seq, :, block(at)] = feature
        phi_qb[seq, at] = feature.astype(BF16)

    def phi_k(seq, at):
        if seq < early:
            return phi_k_early[seq, :, block(at)]
        return phi_k_late[seq - early, :, block(at)]

    def key_logits(seq, at):
        if seq < early:
            return None
        return logits_t(key_parts, key_rows[flat(seq, block(at)), :])

    def key_features(seq, at, logits):
        if seq >= early:
            phi_k_late[seq - early, :, block(at)] = features_t(logits)

    def turn_features(seq, at):
        feature = phi_k(seq, at)
        phi_kb[seq, at] = feature.astype(BF16)
        for half in range(2):
            turned = feature[half * HEAD_SIZE : (half + 1) * HEAD_SIZE].T
            phi_kb_rows[seq, half, block(at), :] = turned.astype(BF16)

    def pair_scores(seq, tile):
        here = span(tile)
        slot = tile % 2
        teacher = nt(key_rows[flat(seq, slice(0, here.stop)), :], query_rows[flat(seq, here), :])
        student = nn(
            side_by_side(phi_kb_rows[seq, half, : here.stop, :] for half in range(2)),
            side_by_side(phi_qb[seq, at] for at in blocks_of(here)),
        )
        stats = []
        for half in range(width):
            at = tile * width + half
            highest = linear_sum = None
            for number in range(at + 1):
                score = teacher[block(number), block(half)]
                linear = student[block(number), block(half)]
                linears[seq, slot, block(number), block(half)] = linear
                if number == at:
                    score = jnp.where(visible, score, NEG_FLOOR)
                    linear = jnp.where(visible, linear, 0.0)
                scores[seq, slot, block(number), block(half)] = score
                top, total = tile_max(score), tile_sum(linear)
                highest = top if number == 0 else jnp.maximum(highest, top)
                linear_sum = total if number == 0 else linear_sum + total
            stats.append(
                (
                    jnp.max(highest, axis=0, keepdims=True),
                    jnp.sum(linear_sum, axis=0, keepdims=True),
                )
            )
        return stats

    def pair_gradients(seq, tile, half, stats):
        highest, linear_sum = stats
        slot = tile % 2
        at = tile * width + half
        denominator = None
        for number in range(at + 1):
            score = scores[seq, slot, block(number), block(half)]
            exponent = jnp.exp2((score - highest) * exponent_scale)
            scores[seq, slot, block(number), block(half)] = exponent
            total = tile_sum(exponent)
            denominator = total if number == 0 else denominator + total
        denominator = jnp.sum(denominator, axis=0, keepdims=True)
        base = 1.0 / (linear_sum * token_count)
        rate = 1.0 / (denominator * token_count)
        for number in range(at + 1):
            exponent = scores[seq, slot, block(number), block(half)]
            weights = base - exponent * rate / linears[seq, slot, block(number), block(half)]
            if number == at:
                weights = jnp.where(visible, weights, 0.0)
            pair_weights[seq, at, block(number), :] = weights.astype(BF16)

    def map_change(phis, upstream, tokens):
        changes = [
            side_parts(feature_grad_t(phi, upstream[:, block(half)]))
            for half, phi in enumerate(phis)
        ]
        twice = [tokens[block(half)] for half in range(width) for _ in range(2)]
        return nn(jnp.concatenate(changes, axis=1), jnp.concatenate(twice, axis=0))

    def query_upstream(seq, tile):
        here = span(tile)
        return nn(
            side_by_side(phi_kb[seq, at] for at in range(here.stop // BLK)),
            side_by_side(pair_weights[seq, at, : here.stop, :] for at in blocks_of(here)),
        )

    def query_change(seq, tile, upstream):
        phis = [phi_q[seq, :, block(tile * width + half)] for half in range(width)]
        acc_q[...] += map_change(phis, upstream, query_rows[flat(seq, span(tile)), :])

    def key_upstream(seq, tile):
        later = range(tile * width, seq_blocks)
        return nt(
            side_by_side(phi_qb[seq, at] for at in later),
            side_by_side(pair_weights[seq, at, span(tile), :] for at in later),
        )

    def key_change(seq, tile, upstream):
        phis = [phi_k(seq, tile * width + half) for half in range(width)]
        acc_k[...] += map_change(phis, upstream, key_rows[flat(seq, span(tile)), :])

    def feature_steps(seq):
        ahead = [key_logits(seq, at) for at in range(min(3, seq_blocks))]
        for at in range(seq_blocks):
            if at + len(ahead) < seq_blocks:
                ahead.append(key_logits(seq, at + len(ahead)))
            key_features(seq, at, ahead.pop(0))
            if at > 1:
                turn_features(seq, at - 2)
            yield
        for at in range(max(seq_blocks - 2, 0), seq_blocks):
            turn_features(seq, at)

    def feature_steps(seq):
        ahead = []
        for at in range(seq_blocks):
            while at + len(ahead) < min(at + 3, seq_blocks):
                later = at + len(ahead)
                ahead.append((key_logits(seq, later), query_logits(seq, later)))
            from_keys, from_queries = ahead.pop(0)
            key_features(seq, at, from_keys)
            query_features(seq, at, from_queries)
            if at:
                turn_features(seq, at - 1)
            yield
        turn_features(seq, seq_blocks - 1)

    def pair_steps(seq):
        order = list(reversed(range(tiles)))
        ahead = pair_scores(seq, order[0])
        behind = None
        for number, tile in enumerate(order):
            stats = ahead
            if number + 1 < tiles:
                ahead = pair_scores(seq, order[number + 1])
            for half in range(width):
                pair_gradients(seq, tile, half, stats[half])
                yield
            upstreams = query_upstream(seq, tile), key_upstream(seq, tile)
            if behind:
                query_change(seq, order[number - 1], behind[0])
                key_change(seq, order[number - 1], behind[1])
            behind = upstreams
        yield
        query_change(seq, order[-1], behind[0])
        key_change(seq, order[-1], behind[1])

    for chunk in range(token_count // rows):
        query_rows[sorted_rows(pos_ref, chunk, rows), :] = arrived_ref[chunk]
    stages = (feature_steps, pair_steps)
    for turn in range(sequences + len(stages) - 1):
        active = [
            stage(turn - number)
            for number, stage in enumerate(stages)
            if 0 <= turn - number < sequences
        ]
        while active:
            for step in list(active):
                if next(step, step) is step:
                    active.remove(step)
    out_ref[:HEAD_SIZE, :] = acc_q[...].T.astype(BF16)
    out_ref[HEAD_SIZE:, :] = bf16_parts(acc_k[...].T, 2)


def collect_kernel(everyone_ref, queries_out_ref, keys_out_ref, buffer, sems):
    seq_count = queries_out_ref.shape[0]
    key_heads = keys_out_ref.shape[0]
    share = seq_count // key_heads
    copies = []

    def leave(number, value, out_ref):
        buffer[number] = value
        copies.append(pltpu.make_async_copy(buffer.at[number], out_ref, sems.at[number]))
        copies[-1].start()

    for number in range(seq_count):
        leave(number, everyone_ref[number, :HEAD_SIZE, :].astype(F32), queries_out_ref.at[number])
    for number in range(key_heads):
        total = None
        for seq in range(number * share, (number + 1) * share):
            for half in (1, 2):
                rows = slice(half * HEAD_SIZE, (half + 1) * HEAD_SIZE)
                value = everyone_ref[seq, rows, :].astype(F32)
                total = value if total is None else total + value
        leave(seq_count + number, total, keys_out_ref.at[number])
    for copy in copies:
        copy.wait()


def per_device_head(queries, keys, block_pos, query_map, key_map):
    seq_count = lax.axis_size("seq")
    head_count = lax.axis_size("head")
    key_heads = key_map.shape[0]
    share = seq_count // key_heads
    rows = queries.shape[0]
    devices = seq_count * head_count
    token_count = rows * devices
    seq_tokens = seq_count * BLK
    sequences = token_count // seq_tokens
    vmem = pl.BlockSpec(memory_space=pltpu.VMEM)
    smem = pl.BlockSpec(memory_space=pltpu.SMEM)

    def swap(piece, axis, bits):
        size = lax.axis_size(axis)
        return lax.ppermute(piece, axis, [(i, i ^ bits) for i in range(size)])

    small = pltpu.CompilerParams(vmem_limit_bytes=4 << 20)
    anywhere = pl.BlockSpec(memory_space=pl.ANY)
    sent, *by_plane = pl.pallas_call(
        functools.partial(send_kernel, seq_count),
        out_shape=[jax.ShapeDtypeStruct((devices, rows, HEAD_SIZE), BF16)]
        + [jax.ShapeDtypeStruct((key_heads, rows, HEAD_SIZE), BF16)] * head_count,
        in_specs=[anywhere] * 2,
        out_specs=[anywhere] * (head_count + 1),
        scratch_shapes=[
            pltpu.VMEM(queries.shape, BF16),
            pltpu.VMEM(keys.shape, BF16),
            pltpu.SemaphoreType.DMA((2,)),
            pltpu.SemaphoreType.DMA((devices,)),
            pltpu.SemaphoreType.DMA((head_count, key_heads)),
        ],
        compiler_params=pltpu.CompilerParams(vmem_limit_bytes=60 << 20),
    )(queries, keys)
    for other in range(1, head_count):
        by_plane[other] = swap(by_plane[other], "head", other)
    arrived = lax.all_to_all(sent, ("seq", "head"), split_axis=0, concat_axis=0, tiled=True)
    by_key_head = pl.pallas_call(
        functools.partial(key_turn_kernel, share),
        out_shape=[jax.ShapeDtypeStruct((head_count, rows, HEAD_SIZE), BF16)] * key_heads,
        in_specs=[vmem] * head_count,
        out_specs=[vmem] * key_heads,
        compiler_params=small,
    )(*by_plane)
    pieces = [None] * seq_count
    for other in range(0, seq_count, 2):
        piece = by_key_head[other // share]
        pieces[other] = swap(piece, "seq", other) if other else piece
    for other in range(0, seq_count, 2):
        pieces[other + 1] = swap(pieces[other], "seq", 1)
    early = max(sequences // 2, 1)
    weights_shape = jax.ShapeDtypeStruct((HEAD_SIZE, HEAD_SIZE), F32)
    key_rows, phi_k, query_weights, key_weights = pl.pallas_call(
        functools.partial(key_kernel, share),
        out_shape=(
            jax.ShapeDtypeStruct((token_count, HEAD_SIZE), BF16),
            jax.ShapeDtypeStruct((early, 2 * HEAD_SIZE, seq_tokens), F32),
            weights_shape,
            weights_shape,
        ),
        in_specs=[smem] + [vmem] * (seq_count + 2),
        out_specs=(vmem,) * 4,
        compiler_params=pltpu.CompilerParams(vmem_limit_bytes=8 << 20),
        cost_estimate=pl.CostEstimate(
            flops=token_count * HEAD_SIZE * HEAD_SIZE * 6,
            bytes_accessed=token_count * HEAD_SIZE * 12,
            transcendentals=token_count * HEAD_SIZE * 2,
        ),
    )(block_pos, key_map, query_map, *pieces)
    grads = pl.pallas_call(
        functools.partial(pair_kernel, token_count, seq_count),
        out_shape=jax.ShapeDtypeStruct((3 * HEAD_SIZE, HEAD_SIZE), BF16),
        in_specs=[smem] + [vmem] * 5,
        out_specs=vmem,
        scratch_shapes=[
            pltpu.VMEM((token_count, HEAD_SIZE), BF16),
            pltpu.VMEM((sequences, 2 * HEAD_SIZE, seq_tokens), F32),
            pltpu.VMEM((sequences, seq_count, 2 * HEAD_SIZE, BLK), BF16),
            pltpu.VMEM((max(sequences - early, 1), 2 * HEAD_SIZE, seq_tokens), F32),
            pltpu.VMEM((sequences, seq_count, 2 * HEAD_SIZE, BLK), BF16),
            pltpu.VMEM((sequences, 2, seq_tokens, HEAD_SIZE), BF16),
            pltpu.VMEM((sequences, seq_count, seq_tokens, BLK), BF16),
            pltpu.VMEM((sequences, 2, seq_tokens, 2 * BLK), F32),
            pltpu.VMEM((sequences, 2, seq_tokens, 2 * BLK), F32),
            pltpu.VMEM((HEAD_SIZE, HEAD_SIZE), F32),
            pltpu.VMEM((HEAD_SIZE, HEAD_SIZE), F32),
        ],
        compiler_params=pltpu.CompilerParams(vmem_limit_bytes=32 << 20),
    )(block_pos, arrived, query_weights, key_weights, key_rows, phi_k)
    everyone = lax.all_gather(grads, "seq", axis=0, tiled=False)
    return pl.pallas_call(
        collect_kernel,
        out_shape=(
            jax.ShapeDtypeStruct((seq_count, HEAD_SIZE, HEAD_SIZE), F32),
            jax.ShapeDtypeStruct((key_heads, HEAD_SIZE, HEAD_SIZE), F32),
        ),
        in_specs=[vmem],
        out_specs=(pl.BlockSpec(memory_space=pl.ANY),) * 2,
        scratch_shapes=[
            pltpu.VMEM((seq_count + key_heads, HEAD_SIZE, HEAD_SIZE), F32),
            pltpu.SemaphoreType.DMA((seq_count + key_heads,)),
        ],
        compiler_params=small,
    )(everyone)


def one_head_each(mesh, queries, keys, block_pos, query_map, key_map):
    del keys, block_pos
    seq_count, head_count = mesh.shape["seq"], mesh.shape["head"]
    rows = queries.shape[0] // (seq_count * head_count)
    key_heads = key_map.shape[0] // head_count
    return (
        query_map.shape[0] == seq_count * head_count
        and seq_count % (2 * key_heads) == 0
        and seq_count & (seq_count - 1) == 0
        and head_count & (head_count - 1) == 0
        and BLK % rows == 0
        and rows % 16 == 0
    )


def solution(mesh):
    in_specs = (
        P(("seq", "head"), None),
        P(("seq", "head"), None),
        P(),
        P("head", None, None),
        P("head", None, None),
    )
    out_specs = (P("head", None, None), P("head", None, None))

    def sharded(function):
        return jax.shard_map(
            function, mesh=mesh, in_specs=in_specs, out_specs=out_specs, check_vma=False
        )

    def step(*args):
        if one_head_each(mesh, *args):
            return sharded(per_device_head)(*args)
        return sharded(per_device_general)(*args)

    return step
```

```python
import functools
import math

import jax
import jax.numpy as jnp
from jax import lax
from jax.experimental import pallas as pl
from jax.experimental.pallas import tpu as pltpu
from jax.sharding import PartitionSpec as P


HEAD_SIZE = 128
BLK = 128

HIGHEST = lax.Precision.HIGHEST
NEG_FLOOR = -1e30


def softmax_pair(logits):
    return jnp.concatenate(
        [jax.nn.softmax(logits, axis=-1), jax.nn.softmax(-logits, axis=-1)], axis=-1
    )


def feature_grad(feature, upstream):
    half_width = feature.shape[-1] // 2
    positive, negative = (feature[..., :half_width], feature[..., half_width:])
    grad_positive, grad_negative = (upstream[..., :half_width], upstream[..., half_width:])
    first = positive * (grad_positive - jnp.sum(grad_positive * positive, axis=-1, keepdims=True))
    second = negative * (grad_negative - jnp.sum(grad_negative * negative, axis=-1, keepdims=True))
    return first - second


def row_places(row_index, block_pos, seq_count):
    stored = row_index // BLK
    lookup = stored[:, None] == jnp.arange(block_pos.shape[0], dtype=jnp.int32)[None, :]
    blocks = jnp.sum(jnp.where(lookup, block_pos[None, :], 0), axis=1)
    return (blocks // seq_count, blocks * BLK + row_index % BLK)


def over_blocks(running, portions, step_fn):
    row_count = portions[0].shape[1]
    step_rows = math.gcd(row_count, 512)

    def advance(number, inner_carry):
        slabs = tuple(
            (
                lax.dynamic_slice_in_dim(portion, number * step_rows, step_rows, 1)
                for portion in portions
            )
        )
        return step_fn(inner_carry, slabs, number * step_rows)

    return lax.fori_loop(0, row_count // step_rows, advance, running)


def per_device_general(queries, keys, block_pos, query_map, key_map):
    local_q, local_k = (
        lax.all_to_all(queries, "head", split_axis=1, concat_axis=0, tiled=True),
        lax.all_to_all(keys, "head", split_axis=1, concat_axis=0, tiled=True),
    )
    seq_count = lax.axis_size("seq")
    seq_rank = lax.axis_index("seq")
    rows_local = local_k.shape[0]
    token_count = rows_local * seq_count
    key_heads = key_map.shape[0]
    group_width = query_map.shape[0] // key_heads
    score_scale = HEAD_SIZE ** (-0.5)
    query_index = seq_rank * rows_local + jnp.arange(rows_local, dtype=jnp.int32)
    query_heads = local_q.reshape(rows_local, key_heads, group_width, HEAD_SIZE).transpose(
        1, 2, 0, 3
    )
    query_wide = query_heads.astype(jnp.float32)
    query_logits = jnp.einsum(
        "vgnd,vgde->vgne",
        query_wide,
        query_map.reshape(key_heads, group_width, HEAD_SIZE, HEAD_SIZE),
        precision=HIGHEST,
    )
    rows_all = group_width * rows_local
    phi_query = softmax_pair(query_logits).reshape(key_heads, rows_all, 2 * HEAD_SIZE)
    phi_query_b = phi_query.astype(jnp.bfloat16)
    query_flat = query_heads.reshape(key_heads, rows_all, HEAD_SIZE)
    query_seq, query_at = row_places(query_index, block_pos, seq_count)
    query_seq = jnp.tile(query_seq, group_width)
    query_at = jnp.tile(query_at, group_width)

    def visible_for(offset, slab_rows):
        key_index = offset + jnp.arange(slab_rows, dtype=jnp.int32)
        key_seq, key_at = row_places(key_index, block_pos, seq_count)
        return (key_seq[None, :] == query_seq[:, None]) & (key_at[None, :] <= query_at[:, None])

    def key_features(key_slab):
        logits = jnp.einsum(
            "vwd,vde->vwe", key_slab.astype(jnp.float32), key_map, precision=HIGHEST
        )
        return softmax_pair(logits)

    def teacher(key_slab):
        return (
            jnp.einsum("vrd,vwd->vrw", query_flat, key_slab, preferred_element_type=jnp.float32)
            * score_scale
        )

    def stats_step(running, slabs, offset):
        key_slab = slabs[0]
        visible = visible_for(offset, key_slab.shape[1])

        def stats_compute_live(current):
            highest, denominator, linear_sum = current
            masked = jnp.where(visible[None], teacher(key_slab), NEG_FLOOR)
            new_high = jnp.maximum(highest, jnp.max(masked, axis=-1))
            exponent = jnp.where(visible[None], jnp.exp(masked - new_high[..., None]), 0.0)
            denominator = denominator * jnp.exp(highest - new_high) + jnp.sum(exponent, axis=-1)
            phi_key_b = key_features(key_slab).astype(jnp.bfloat16)
            linear = jnp.einsum(
                "vrf,vwf->vrw", phi_query_b, phi_key_b, preferred_element_type=jnp.float32
            )
            linear_sum = linear_sum + jnp.sum(jnp.where(visible[None], linear, 0.0), axis=-1)
            return (new_high, denominator, linear_sum)

        return lax.cond(jnp.any(visible), stats_compute_live, lambda current: current, running)

    def grads_step(running, slabs, offset):
        key_slab = slabs[0]
        visible = visible_for(offset, key_slab.shape[1])

        def grads_compute_live(current):
            query_grad, key_weight_grad = current
            masked = jnp.where(visible[None], teacher(key_slab), NEG_FLOOR)
            exponent = jnp.where(visible[None], jnp.exp(masked - highest[..., None]), 0.0)
            teacher_prob = exponent / denominator[..., None]
            phi_key = key_features(key_slab)
            phi_key_b = phi_key.astype(jnp.bfloat16)
            linear = jnp.einsum(
                "vrf,vwf->vrw", phi_query_b, phi_key_b, preferred_element_type=jnp.float32
            )
            weights = (
                jnp.where(visible[None], 1.0 / linear_sum[..., None] - teacher_prob / linear, 0.0)
                / token_count
            ).astype(jnp.bfloat16)
            query_grad = query_grad + jnp.einsum(
                "vrw,vwf->vrf", weights, phi_key_b, preferred_element_type=jnp.float32
            )
            key_grad = jnp.einsum(
                "vrw,vrf->vwf", weights, phi_query_b, preferred_element_type=jnp.float32
            )
            key_logit_grad = feature_grad(phi_key, key_grad)
            key_weight_grad = key_weight_grad + jnp.einsum(
                "vwd,vwe->vde", key_slab.astype(jnp.float32), key_logit_grad, precision=HIGHEST
            )
            return (query_grad, key_weight_grad)

        return lax.cond(jnp.any(visible), grads_compute_live, lambda current: current, running)

    def as_heads(pieces):
        return pieces.reshape(pieces.shape[0], key_heads, -1).transpose(1, 0, 2)

    row_zeros = jnp.zeros((key_heads, rows_all), jnp.float32)
    stats_init = (jnp.full((key_heads, rows_all), NEG_FLOOR, jnp.float32), row_zeros, row_zeros)
    grads_init = (
        jnp.zeros((key_heads, rows_all, 2 * HEAD_SIZE), jnp.float32),
        jnp.zeros((key_heads, HEAD_SIZE, HEAD_SIZE), jnp.float32),
    )
    highest, denominator, linear_sum = over_blocks(
        stats_init, (as_heads(lax.all_gather(local_k, "seq", axis=0, tiled=True)),), stats_step
    )
    query_grad, key_weight_grad = over_blocks(
        grads_init, (as_heads(lax.all_gather(local_k, "seq", axis=0, tiled=True)),), grads_step
    )
    query_logit_grad = feature_grad(phi_query, query_grad).reshape(
        key_heads, group_width, rows_local, HEAD_SIZE
    )
    query_weight_grad = jnp.einsum(
        "vgnd,vgne->vgde", query_wide, query_logit_grad, precision=HIGHEST
    ).reshape(key_heads * group_width, HEAD_SIZE, HEAD_SIZE)
    query_map_gradient, key_map_gradient = lax.psum((query_weight_grad, key_weight_grad), "seq")
    return (query_map_gradient, key_map_gradient)


NT = (((1,), (1,)), ((), ()))
F32 = jnp.float32
BF16 = jnp.bfloat16


def nn(left, right):
    return jnp.dot(left, right, preferred_element_type=F32)


def nt(left, right):
    return lax.dot_general(left, right, NT, preferred_element_type=F32)


def bf16_parts(value, count):
    parts = []
    for _ in range(count):
        part = value.astype(BF16)
        parts.append(part)
        value = value - part.astype(F32)
    return jnp.concatenate(parts, axis=0)


def features_t(logits):
    up = jnp.exp2(logits - jnp.max(logits, axis=0, keepdims=True))
    down = jnp.exp2(jnp.min(logits, axis=0, keepdims=True) - logits)
    up = up * (1.0 / jnp.sum(up, axis=0, keepdims=True))
    down = down * (1.0 / jnp.sum(down, axis=0, keepdims=True))
    return jnp.concatenate([up, down], axis=0)


def feature_grad_t(feature, upstream):
    halves = []
    for half in (slice(0, HEAD_SIZE), slice(HEAD_SIZE, 2 * HEAD_SIZE)):
        value, grad = feature[half], upstream[half]
        halves.append(value * (grad - jnp.sum(grad * value, axis=0, keepdims=True)))
    return halves[0] - halves[1]


def tile_sum(value):
    return jnp.sum(value.reshape(-1, 8, value.shape[-1]), axis=0)


def tile_max(value):
    return jnp.max(value.reshape(-1, 8, value.shape[-1]), axis=0)


def side_parts(value):
    high = value.astype(BF16)
    return jnp.concatenate([high, (value - high.astype(F32)).astype(BF16)], axis=1)


def map_parts(weights):
    rest = weights.T * math.log2(math.e)
    parts = []
    for _ in range(3):
        parts.append(rest.astype(BF16))
        rest = rest - parts[-1].astype(F32)
    return jnp.concatenate(parts[::-1], axis=1)


def logits_t(parts, tokens):
    return nt(parts, jnp.concatenate([tokens] * 3, axis=1))


def send_kernel(seq_count, queries_ref, keys_ref, *refs):
    queries_out_ref, *keys_out_refs, query_buffer, key_buffer, sems, query_sems, key_sems = refs
    head_count = len(keys_out_refs)
    key_heads = keys_out_refs[0].shape[0]
    keys_in = pltpu.make_async_copy(keys_ref, key_buffer, sems.at[0])
    queries_in = pltpu.make_async_copy(queries_ref, query_buffer, sems.at[1])
    keys_in.start()
    queries_in.start()
    leaving = []
    keys_in.wait()
    for other, out_ref in enumerate(keys_out_refs):
        for number in range(key_heads):
            column = ((lax.axis_index("head") ^ other) * key_heads + number) * HEAD_SIZE
            column = pl.multiple_of(column, HEAD_SIZE)
            leaving.append(
                pltpu.make_async_copy(
                    key_buffer.at[:, pl.ds(column, HEAD_SIZE)],
                    out_ref.at[number],
                    key_sems.at[other, number],
                )
            )
            leaving[-1].start()
    queries_in.wait()
    for head in range(head_count):
        for seq in range(seq_count):
            column = (head * seq_count + seq) * HEAD_SIZE
            target = seq * head_count + head
            leaving.append(
                pltpu.make_async_copy(
                    query_buffer.at[:, column : column + HEAD_SIZE],
                    queries_out_ref.at[target],
                    query_sems.at[target],
                )
            )
            leaving[-1].start()
    for copy in leaving:
        copy.wait()


def key_turn_kernel(share, *refs):
    key_heads = refs[0].shape[0]
    in_refs, out_refs = refs[:-key_heads], refs[-key_heads:]
    mine = lax.div(lax.axis_index("seq"), share)
    for other, out_ref in enumerate(out_refs):
        for number, in_ref in enumerate(in_refs):
            out_ref[number] = in_ref[mine ^ other]


def sorted_rows(pos_ref, chunk, rows):
    per_block = BLK // rows
    first = pos_ref[lax.div(chunk, per_block)] * BLK + lax.rem(chunk, per_block) * rows
    return pl.ds(pl.multiple_of(first, rows), rows)


def block(at):
    return slice(at * BLK, (at + 1) * BLK)


def key_kernel(share, pos_ref, key_map_ref, query_map_ref, *refs):
    seq_count, head_count = lax.axis_size("seq"), lax.axis_size("head")
    piece_refs, refs = refs[:seq_count], refs[seq_count:]
    key_rows, phi, query_weights_ref, key_weights_ref = refs
    rows = piece_refs[0].shape[1]
    seq_blocks = phi.shape[2] // BLK
    blocks = phi.shape[0] * seq_blocks
    mine, plane = lax.axis_index("seq"), lax.axis_index("head")
    query_weights_ref[...] = query_map_ref[mine]
    for other in range(seq_count):
        for number in range(head_count):
            chunk = (mine ^ other) * head_count + (plane ^ number)
            key_rows[sorted_rows(pos_ref, chunk, rows), :] = piece_refs[other][number]
    key_weights_ref[...] = key_map_ref[lax.div(mine, share)]
    parts = map_parts(key_weights_ref[...])
    ahead = []
    for number in range(blocks):
        while number + len(ahead) < min(number + 3, blocks):
            ahead.append(logits_t(parts, key_rows[block(number + len(ahead)), :]))
        seq, at = divmod(number, seq_blocks)
        phi[seq, :, block(at)] = features_t(ahead.pop(0))


def pair_kernel(
    token_count,
    seq_blocks,
    pos_ref,
    arrived_ref,
    query_weights_ref,
    key_weights_ref,
    key_rows,
    phi_k_early,
    out_ref,
    query_rows,
    phi_q,
    phi_qb,
    phi_k_late,
    phi_kb,
    phi_kb_rows,
    pair_weights,
    scores,
    linears,
    acc_q,
    acc_k,
):
    rows = arrived_ref.shape[1]
    seq_tokens = seq_blocks * BLK
    sequences = token_count // seq_tokens
    acc_q[...] = jnp.zeros_like(acc_q)
    acc_k[...] = jnp.zeros_like(acc_k)
    width = 2 if seq_blocks % 2 == 0 else 1
    tiles = seq_blocks // width
    for seq in range(sequences):
        for at in range(0, seq_blocks, width):
            if width > 1:
                pair_weights[seq, at, block(at + 1), :] = jnp.zeros((BLK, BLK), BF16)
    parts = map_parts(query_weights_ref[...])
    key_parts = map_parts(key_weights_ref[...])
    early = phi_k_early.shape[0]
    lane = lax.broadcasted_iota(jnp.int32, (BLK, BLK), 1)
    sublane = lax.broadcasted_iota(jnp.int32, (BLK, BLK), 0)
    visible = sublane <= lane
    exponent_scale = HEAD_SIZE ** (-0.5) * math.log2(math.e)

    def side_by_side(pieces):
        return jnp.concatenate(list(pieces), axis=1)

    def blocks_of(here):
        return range(here.start // BLK, here.stop // BLK)

    def span(tile):
        return slice(tile * width * BLK, (tile + 1) * width * BLK)

    def flat(seq, here):
        return slice(seq * seq_tokens + here.start, seq * seq_tokens + here.stop)

    def query_logits(seq, at):
        return logits_t(parts, query_rows[flat(seq, block(at)), :])

    def query_features(seq, at, logits):
        feature = features_t(logits)
        phi_q[seq, :, block(at)] = feature
        phi_qb[seq, at] = feature.astype(BF16) * token_count

    def phi_k(seq, at):
        if seq < early:
            return phi_k_early[seq, :, block(at)]
        return phi_k_late[seq - early, :, block(at)]

    def key_logits(seq, at):
        if seq < early:
            return None
        return logits_t(key_parts, key_rows[flat(seq, block(at)), :])

    def key_features(seq, at, logits):
        if seq >= early:
            phi_k_late[seq - early, :, block(at)] = features_t(logits)

    def turn_features(seq, at):
        feature = phi_k(seq, at)
        phi_kb[seq, at] = feature.astype(BF16)
        for half in range(2):
            turned = feature[half * HEAD_SIZE : (half + 1) * HEAD_SIZE].T
            phi_kb_rows[seq, half, block(at), :] = turned.astype(BF16)

    def pair_scores(seq, tile):
        here = span(tile)
        slot = tile % 2
        teacher = nt(key_rows[flat(seq, slice(0, here.stop)), :], query_rows[flat(seq, here), :])
        student = nn(
            side_by_side(phi_kb_rows[seq, half, : here.stop, :] for half in range(2)),
            side_by_side(phi_qb[seq, at] for at in blocks_of(here)),
        )
        stats = []
        for half in range(width):
            at = tile * width + half
            highest = linear_sum = None
            for number in range(at + 1):
                score = teacher[block(number), block(half)]
                linear = student[block(number), block(half)]
                linears[seq, slot, block(number), block(half)] = linear
                if number == at:
                    score = jnp.where(visible, score, NEG_FLOOR)
                    linear = jnp.where(visible, linear, 0.0)
                scores[seq, slot, block(number), block(half)] = score
                top, total = tile_max(score), tile_sum(linear)
                highest = top if number == 0 else jnp.maximum(highest, top)
                linear_sum = total if number == 0 else linear_sum + total
            stats.append(
                (
                    jnp.max(highest, axis=0, keepdims=True),
                    jnp.sum(linear_sum, axis=0, keepdims=True),
                )
            )
        return stats

    def pair_gradients(seq, tile, half, stats):
        highest, linear_sum = stats
        slot = tile % 2
        at = tile * width + half
        denominator = None
        for number in range(at + 1):
            score = scores[seq, slot, block(number), block(half)]
            exponent = jnp.exp2((score - highest) * exponent_scale)
            scores[seq, slot, block(number), block(half)] = exponent
            total = tile_sum(exponent)
            denominator = total if number == 0 else denominator + total
        denominator = jnp.sum(denominator, axis=0, keepdims=True)
        base = 1.0 / linear_sum
        rate = 1.0 / denominator
        for number in range(at + 1):
            exponent = scores[seq, slot, block(number), block(half)]
            weights = base - exponent * rate / linears[seq, slot, block(number), block(half)]
            if number == at:
                weights = jnp.where(visible, weights, 0.0)
            pair_weights[seq, at, block(number), :] = weights.astype(BF16)

    def map_change(phis, upstream, tokens):
        changes = [
            side_parts(feature_grad_t(phi, upstream[:, block(half)]))
            for half, phi in enumerate(phis)
        ]
        twice = [tokens[block(half)] for half in range(width) for _ in range(2)]
        return nn(jnp.concatenate(changes, axis=1), jnp.concatenate(twice, axis=0))

    def query_upstream(seq, tile):
        here = span(tile)
        return nn(
            side_by_side(phi_kb[seq, at] for at in range(here.stop // BLK)),
            side_by_side(pair_weights[seq, at, : here.stop, :] for at in blocks_of(here)),
        )

    def query_change(seq, tile, upstream):
        phis = [phi_q[seq, :, block(tile * width + half)] for half in range(width)]
        acc_q[...] += map_change(phis, upstream, query_rows[flat(seq, span(tile)), :])

    def key_upstream(seq, tile):
        later = range(tile * width, seq_blocks)
        return nt(
            side_by_side(phi_qb[seq, at] for at in later),
            side_by_side(pair_weights[seq, at, span(tile), :] for at in later),
        )

    def key_change(seq, tile, upstream):
        phis = [phi_k(seq, tile * width + half) for half in range(width)]
        acc_k[...] += map_change(phis, upstream, key_rows[flat(seq, span(tile)), :])

    def feature_steps(seq):
        ahead = [key_logits(seq, at) for at in range(min(3, seq_blocks))]
        for at in range(seq_blocks):
            if at + len(ahead) < seq_blocks:
                ahead.append(key_logits(seq, at + len(ahead)))
            key_features(seq, at, ahead.pop(0))
            if at > 1:
                turn_features(seq, at - 2)
            yield
        for at in range(max(seq_blocks - 2, 0), seq_blocks):
            turn_features(seq, at)

    def feature_steps(seq):
        ahead = []
        for at in range(seq_blocks):
            while at + len(ahead) < min(at + 3, seq_blocks):
                later = at + len(ahead)
                ahead.append((key_logits(seq, later), query_logits(seq, later)))
            from_keys, from_queries = ahead.pop(0)
            key_features(seq, at, from_keys)
            query_features(seq, at, from_queries)
            if at:
                turn_features(seq, at - 1)
            yield
        turn_features(seq, seq_blocks - 1)

    def pair_steps(seq):
        order = list(reversed(range(tiles)))
        ahead = pair_scores(seq, order[0])
        behind = None
        for number, tile in enumerate(order):
            stats = ahead
            if number + 1 < tiles:
                ahead = pair_scores(seq, order[number + 1])
            for half in range(width):
                pair_gradients(seq, tile, half, stats[half])
                yield
            upstreams = query_upstream(seq, tile), key_upstream(seq, tile)
            if behind:
                query_change(seq, order[number - 1], behind[0])
                key_change(seq, order[number - 1], behind[1])
            behind = upstreams
        yield
        query_change(seq, order[-1], behind[0])
        key_change(seq, order[-1], behind[1])

    for chunk in range(token_count // rows):
        query_rows[sorted_rows(pos_ref, chunk, rows), :] = arrived_ref[chunk]
    stages = (feature_steps, pair_steps)
    for turn in range(sequences + len(stages) - 1):
        active = [
            stage(turn - number)
            for number, stage in enumerate(stages)
            if 0 <= turn - number < sequences
        ]
        while active:
            for step in active[::-1]:
                if next(step, step) is step:
                    active.remove(step)
    out_ref[:HEAD_SIZE, :] = acc_q[...].T.astype(BF16)
    out_ref[HEAD_SIZE:, :] = bf16_parts(acc_k[...].T * (1.0 / token_count), 2)


def collect_kernel(everyone_ref, queries_out_ref, keys_out_ref, buffer, sems):
    seq_count = queries_out_ref.shape[0]
    key_heads = keys_out_ref.shape[0]
    share = seq_count // key_heads
    copies = []

    def leave(number, value, out_ref):
        buffer[number] = value
        copies.append(pltpu.make_async_copy(buffer.at[number], out_ref, sems.at[number]))
        copies[-1].start()

    for number in range(seq_count):
        leave(number, everyone_ref[number, :HEAD_SIZE, :].astype(F32), queries_out_ref.at[number])
    for number in range(key_heads):
        total = None
        for seq in range(number * share, (number + 1) * share):
            for half in (1, 2):
                rows = slice(half * HEAD_SIZE, (half + 1) * HEAD_SIZE)
                value = everyone_ref[seq, rows, :].astype(F32)
                total = value if total is None else total + value
        leave(seq_count + number, total, keys_out_ref.at[number])
    for copy in copies:
        copy.wait()


def per_device_head(queries, keys, block_pos, query_map, key_map):
    seq_count = lax.axis_size("seq")
    head_count = lax.axis_size("head")
    key_heads = key_map.shape[0]
    share = seq_count // key_heads
    rows = queries.shape[0]
    devices = seq_count * head_count
    token_count = rows * devices
    seq_tokens = seq_count * BLK
    sequences = token_count // seq_tokens
    vmem = pl.BlockSpec(memory_space=pltpu.VMEM)
    smem = pl.BlockSpec(memory_space=pltpu.SMEM)

    def swap(piece, axis, bits):
        size = lax.axis_size(axis)
        return lax.ppermute(piece, axis, [(i, i ^ bits) for i in range(size)])

    small = pltpu.CompilerParams(vmem_limit_bytes=4 << 20)
    anywhere = pl.BlockSpec(memory_space=pl.ANY)
    sent, *by_plane = pl.pallas_call(
        functools.partial(send_kernel, seq_count),
        out_shape=[jax.ShapeDtypeStruct((devices, rows, HEAD_SIZE), BF16)]
        + [jax.ShapeDtypeStruct((key_heads, rows, HEAD_SIZE), BF16)] * head_count,
        in_specs=[anywhere] * 2,
        out_specs=[anywhere] * (head_count + 1),
        scratch_shapes=[
            pltpu.VMEM(queries.shape, BF16),
            pltpu.VMEM(keys.shape, BF16),
            pltpu.SemaphoreType.DMA((2,)),
            pltpu.SemaphoreType.DMA((devices,)),
            pltpu.SemaphoreType.DMA((head_count, key_heads)),
        ],
        compiler_params=pltpu.CompilerParams(vmem_limit_bytes=60 << 20),
    )(queries, keys)
    for other in range(1, head_count):
        by_plane[other] = swap(by_plane[other], "head", other)
    arrived = lax.all_to_all(sent, ("seq", "head"), split_axis=0, concat_axis=0, tiled=True)
    by_key_head = pl.pallas_call(
        functools.partial(key_turn_kernel, share),
        out_shape=[jax.ShapeDtypeStruct((head_count, rows, HEAD_SIZE), BF16)] * key_heads,
        in_specs=[vmem] * head_count,
        out_specs=[vmem] * key_heads,
        compiler_params=small,
    )(*by_plane)
    pieces = [None] * seq_count
    for other in range(0, seq_count, 2):
        piece = by_key_head[other // share]
        pieces[other] = swap(piece, "seq", other) if other else piece
    for other in range(0, seq_count, 2):
        pieces[other + 1] = swap(pieces[other], "seq", 1)
    early = max(sequences // 2, 1)
    weights_shape = jax.ShapeDtypeStruct((HEAD_SIZE, HEAD_SIZE), F32)
    key_rows, phi_k, query_weights, key_weights = pl.pallas_call(
        functools.partial(key_kernel, share),
        out_shape=(
            jax.ShapeDtypeStruct((token_count, HEAD_SIZE), BF16),
            jax.ShapeDtypeStruct((early, 2 * HEAD_SIZE, seq_tokens), F32),
            weights_shape,
            weights_shape,
        ),
        in_specs=[smem] + [vmem] * (seq_count + 2),
        out_specs=(vmem,) * 4,
        compiler_params=pltpu.CompilerParams(vmem_limit_bytes=8 << 20),
        cost_estimate=pl.CostEstimate(
            flops=token_count * HEAD_SIZE * HEAD_SIZE * 6,
            bytes_accessed=token_count * HEAD_SIZE * 12,
            transcendentals=token_count * HEAD_SIZE * 2,
        ),
    )(block_pos, key_map, query_map, *pieces)
    grads = pl.pallas_call(
        functools.partial(pair_kernel, token_count, seq_count),
        out_shape=jax.ShapeDtypeStruct((3 * HEAD_SIZE, HEAD_SIZE), BF16),
        in_specs=[smem] + [vmem] * 5,
        out_specs=vmem,
        scratch_shapes=[
            pltpu.VMEM((token_count, HEAD_SIZE), BF16),
            pltpu.VMEM((sequences, 2 * HEAD_SIZE, seq_tokens), F32),
            pltpu.VMEM((sequences, seq_count, 2 * HEAD_SIZE, BLK), BF16),
            pltpu.VMEM((max(sequences - early, 1), 2 * HEAD_SIZE, seq_tokens), F32),
            pltpu.VMEM((sequences, seq_count, 2 * HEAD_SIZE, BLK), BF16),
            pltpu.VMEM((sequences, 2, seq_tokens, HEAD_SIZE), BF16),
            pltpu.VMEM((sequences, seq_count, seq_tokens, BLK), BF16),
            pltpu.VMEM((sequences, 2, seq_tokens, 2 * BLK), F32),
            pltpu.VMEM((sequences, 2, seq_tokens, 2 * BLK), F32),
            pltpu.VMEM((HEAD_SIZE, HEAD_SIZE), F32),
            pltpu.VMEM((HEAD_SIZE, HEAD_SIZE), F32),
        ],
        compiler_params=pltpu.CompilerParams(vmem_limit_bytes=32 << 20),
    )(block_pos, arrived, query_weights, key_weights, key_rows, phi_k)
    everyone = lax.all_gather(grads, "seq", axis=0, tiled=False)
    return pl.pallas_call(
        collect_kernel,
        out_shape=(
            jax.ShapeDtypeStruct((seq_count, HEAD_SIZE, HEAD_SIZE), F32),
            jax.ShapeDtypeStruct((key_heads, HEAD_SIZE, HEAD_SIZE), F32),
        ),
        in_specs=[vmem],
        out_specs=(pl.BlockSpec(memory_space=pl.ANY),) * 2,
        scratch_shapes=[
            pltpu.VMEM((seq_count + key_heads, HEAD_SIZE, HEAD_SIZE), F32),
            pltpu.SemaphoreType.DMA((seq_count + key_heads,)),
        ],
        compiler_params=small,
    )(everyone)


def one_head_each(mesh, queries, keys, block_pos, query_map, key_map):
    del keys, block_pos
    seq_count, head_count = mesh.shape["seq"], mesh.shape["head"]
    rows = queries.shape[0] // (seq_count * head_count)
    key_heads = key_map.shape[0] // head_count
    return (
        query_map.shape[0] == seq_count * head_count
        and seq_count % (2 * key_heads) == 0
        and seq_count & (seq_count - 1) == 0
        and head_count & (head_count - 1) == 0
        and BLK % rows == 0
        and rows % 16 == 0
    )


def solution(mesh):
    in_specs = (
        P(("seq", "head"), None),
        P(("seq", "head"), None),
        P(),
        P("head", None, None),
        P("head", None, None),
    )
    out_specs = (P("head", None, None), P("head", None, None))

    def sharded(function):
        return jax.shard_map(
            function, mesh=mesh, in_specs=in_specs, out_specs=out_specs, check_vma=False
        )

    def step(*args):
        if one_head_each(mesh, *args):
            return sharded(per_device_head)(*args)
        return sharded(per_device_general)(*args)

    return step
```

```python
import functools
import math

import jax
import jax.numpy as jnp
from jax import lax
from jax.experimental import pallas as pl
from jax.experimental.pallas import tpu as pltpu
from jax.sharding import PartitionSpec as P


HEAD_SIZE = 128
BLK = 128

HIGHEST = lax.Precision.HIGHEST
NEG_FLOOR = -1e30


def softmax_pair(logits):
    return jnp.concatenate(
        [jax.nn.softmax(logits, axis=-1), jax.nn.softmax(-logits, axis=-1)], axis=-1
    )


def feature_grad(feature, upstream):
    half_width = feature.shape[-1] // 2
    positive, negative = (feature[..., :half_width], feature[..., half_width:])
    grad_positive, grad_negative = (upstream[..., :half_width], upstream[..., half_width:])
    first = positive * (grad_positive - jnp.sum(grad_positive * positive, axis=-1, keepdims=True))
    second = negative * (grad_negative - jnp.sum(grad_negative * negative, axis=-1, keepdims=True))
    return first - second


def row_places(row_index, block_pos, seq_count):
    stored = row_index // BLK
    lookup = stored[:, None] == jnp.arange(block_pos.shape[0], dtype=jnp.int32)[None, :]
    blocks = jnp.sum(jnp.where(lookup, block_pos[None, :], 0), axis=1)
    return (blocks // seq_count, blocks * BLK + row_index % BLK)


def over_blocks(running, portions, step_fn):
    row_count = portions[0].shape[1]
    step_rows = math.gcd(row_count, 512)

    def advance(number, inner_carry):
        slabs = tuple(
            (
                lax.dynamic_slice_in_dim(portion, number * step_rows, step_rows, 1)
                for portion in portions
            )
        )
        return step_fn(inner_carry, slabs, number * step_rows)

    return lax.fori_loop(0, row_count // step_rows, advance, running)


def per_device_general(queries, keys, block_pos, query_map, key_map):
    local_q, local_k = (
        lax.all_to_all(queries, "head", split_axis=1, concat_axis=0, tiled=True),
        lax.all_to_all(keys, "head", split_axis=1, concat_axis=0, tiled=True),
    )
    seq_count = lax.axis_size("seq")
    seq_rank = lax.axis_index("seq")
    rows_local = local_k.shape[0]
    token_count = rows_local * seq_count
    key_heads = key_map.shape[0]
    group_width = query_map.shape[0] // key_heads
    score_scale = HEAD_SIZE ** (-0.5)
    query_index = seq_rank * rows_local + jnp.arange(rows_local, dtype=jnp.int32)
    query_heads = local_q.reshape(rows_local, key_heads, group_width, HEAD_SIZE).transpose(
        1, 2, 0, 3
    )
    query_wide = query_heads.astype(jnp.float32)
    query_logits = jnp.einsum(
        "vgnd,vgde->vgne",
        query_wide,
        query_map.reshape(key_heads, group_width, HEAD_SIZE, HEAD_SIZE),
        precision=HIGHEST,
    )
    rows_all = group_width * rows_local
    phi_query = softmax_pair(query_logits).reshape(key_heads, rows_all, 2 * HEAD_SIZE)
    phi_query_b = phi_query.astype(jnp.bfloat16)
    query_flat = query_heads.reshape(key_heads, rows_all, HEAD_SIZE)
    query_seq, query_at = row_places(query_index, block_pos, seq_count)
    query_seq = jnp.tile(query_seq, group_width)
    query_at = jnp.tile(query_at, group_width)

    def visible_for(offset, slab_rows):
        key_index = offset + jnp.arange(slab_rows, dtype=jnp.int32)
        key_seq, key_at = row_places(key_index, block_pos, seq_count)
        return (key_seq[None, :] == query_seq[:, None]) & (key_at[None, :] <= query_at[:, None])

    def key_features(key_slab):
        logits = jnp.einsum(
            "vwd,vde->vwe", key_slab.astype(jnp.float32), key_map, precision=HIGHEST
        )
        return softmax_pair(logits)

    def teacher(key_slab):
        return (
            jnp.einsum("vrd,vwd->vrw", query_flat, key_slab, preferred_element_type=jnp.float32)
            * score_scale
        )

    def stats_step(running, slabs, offset):
        key_slab = slabs[0]
        visible = visible_for(offset, key_slab.shape[1])

        def stats_compute_live(current):
            highest, denominator, linear_sum = current
            masked = jnp.where(visible[None], teacher(key_slab), NEG_FLOOR)
            new_high = jnp.maximum(highest, jnp.max(masked, axis=-1))
            exponent = jnp.where(visible[None], jnp.exp(masked - new_high[..., None]), 0.0)
            denominator = denominator * jnp.exp(highest - new_high) + jnp.sum(exponent, axis=-1)
            phi_key_b = key_features(key_slab).astype(jnp.bfloat16)
            linear = jnp.einsum(
                "vrf,vwf->vrw", phi_query_b, phi_key_b, preferred_element_type=jnp.float32
            )
            linear_sum = linear_sum + jnp.sum(jnp.where(visible[None], linear, 0.0), axis=-1)
            return (new_high, denominator, linear_sum)

        return lax.cond(jnp.any(visible), stats_compute_live, lambda current: current, running)

    def grads_step(running, slabs, offset):
        key_slab = slabs[0]
        visible = visible_for(offset, key_slab.shape[1])

        def grads_compute_live(current):
            query_grad, key_weight_grad = current
            masked = jnp.where(visible[None], teacher(key_slab), NEG_FLOOR)
            exponent = jnp.where(visible[None], jnp.exp(masked - highest[..., None]), 0.0)
            teacher_prob = exponent / denominator[..., None]
            phi_key = key_features(key_slab)
            phi_key_b = phi_key.astype(jnp.bfloat16)
            linear = jnp.einsum(
                "vrf,vwf->vrw", phi_query_b, phi_key_b, preferred_element_type=jnp.float32
            )
            weights = (
                jnp.where(visible[None], 1.0 / linear_sum[..., None] - teacher_prob / linear, 0.0)
                / token_count
            ).astype(jnp.bfloat16)
            query_grad = query_grad + jnp.einsum(
                "vrw,vwf->vrf", weights, phi_key_b, preferred_element_type=jnp.float32
            )
            key_grad = jnp.einsum(
                "vrw,vrf->vwf", weights, phi_query_b, preferred_element_type=jnp.float32
            )
            key_logit_grad = feature_grad(phi_key, key_grad)
            key_weight_grad = key_weight_grad + jnp.einsum(
                "vwd,vwe->vde", key_slab.astype(jnp.float32), key_logit_grad, precision=HIGHEST
            )
            return (query_grad, key_weight_grad)

        return lax.cond(jnp.any(visible), grads_compute_live, lambda current: current, running)

    def as_heads(pieces):
        return pieces.reshape(pieces.shape[0], key_heads, -1).transpose(1, 0, 2)

    row_zeros = jnp.zeros((key_heads, rows_all), jnp.float32)
    stats_init = (jnp.full((key_heads, rows_all), NEG_FLOOR, jnp.float32), row_zeros, row_zeros)
    grads_init = (
        jnp.zeros((key_heads, rows_all, 2 * HEAD_SIZE), jnp.float32),
        jnp.zeros((key_heads, HEAD_SIZE, HEAD_SIZE), jnp.float32),
    )
    highest, denominator, linear_sum = over_blocks(
        stats_init, (as_heads(lax.all_gather(local_k, "seq", axis=0, tiled=True)),), stats_step
    )
    query_grad, key_weight_grad = over_blocks(
        grads_init, (as_heads(lax.all_gather(local_k, "seq", axis=0, tiled=True)),), grads_step
    )
    query_logit_grad = feature_grad(phi_query, query_grad).reshape(
        key_heads, group_width, rows_local, HEAD_SIZE
    )
    query_weight_grad = jnp.einsum(
        "vgnd,vgne->vgde", query_wide, query_logit_grad, precision=HIGHEST
    ).reshape(key_heads * group_width, HEAD_SIZE, HEAD_SIZE)
    query_map_gradient, key_map_gradient = lax.psum((query_weight_grad, key_weight_grad), "seq")
    return (query_map_gradient, key_map_gradient)


NT = (((1,), (1,)), ((), ()))
F32 = jnp.float32
BF16 = jnp.bfloat16


def nn(left, right):
    return jnp.dot(left, right, preferred_element_type=F32)


def nt(left, right):
    return lax.dot_general(left, right, NT, preferred_element_type=F32)


def bf16_parts(value, count):
    parts = []
    for _ in range(count):
        part = value.astype(BF16)
        parts.append(part)
        value = value - part.astype(F32)
    return jnp.concatenate(parts, axis=0)


def features_t(logits):
    up = jnp.exp2(logits - jnp.max(logits, axis=0, keepdims=True))
    down = jnp.exp2(jnp.min(logits, axis=0, keepdims=True) - logits)
    up = up * (1.0 / jnp.sum(up, axis=0, keepdims=True))
    down = down * (1.0 / jnp.sum(down, axis=0, keepdims=True))
    return jnp.concatenate([up, down], axis=0)


def feature_grad_t(feature, upstream):
    halves = []
    for half in (slice(0, HEAD_SIZE), slice(HEAD_SIZE, 2 * HEAD_SIZE)):
        value, grad = feature[half], upstream[half]
        halves.append(value * (grad - jnp.sum(grad * value, axis=0, keepdims=True)))
    return halves[0] - halves[1]


def tile_sum(value):
    return jnp.sum(value.reshape(-1, 8, value.shape[-1]), axis=0)


def tile_max(value):
    return jnp.max(value.reshape(-1, 8, value.shape[-1]), axis=0)


def side_parts(value):
    high = value.astype(BF16)
    return jnp.concatenate([high, (value - high.astype(F32)).astype(BF16)], axis=1)


def map_parts(weights):
    rest = weights.T * math.log2(math.e)
    parts = []
    for _ in range(3):
        parts.append(rest.astype(BF16))
        rest = rest - parts[-1].astype(F32)
    return jnp.concatenate(parts[::-1], axis=1)


def logits_t(parts, tokens):
    return nt(parts, jnp.concatenate([tokens] * 3, axis=1))


def send_kernel(seq_count, queries_ref, keys_ref, *refs):
    queries_out_ref, *keys_out_refs, query_buffer, key_buffer, sems, query_sems, key_sems = refs
    head_count = len(keys_out_refs)
    key_heads = keys_out_refs[0].shape[0]
    keys_in = pltpu.make_async_copy(keys_ref, key_buffer, sems.at[0])
    queries_in = pltpu.make_async_copy(queries_ref, query_buffer, sems.at[1])
    keys_in.start()
    queries_in.start()
    leaving = []
    keys_in.wait()
    for other, out_ref in enumerate(keys_out_refs):
        for number in range(key_heads):
            column = ((lax.axis_index("head") ^ other) * key_heads + number) * HEAD_SIZE
            column = pl.multiple_of(column, HEAD_SIZE)
            leaving.append(
                pltpu.make_async_copy(
                    key_buffer.at[:, pl.ds(column, HEAD_SIZE)],
                    out_ref.at[number],
                    key_sems.at[other, number],
                )
            )
            leaving[-1].start()
    queries_in.wait()
    for head in range(head_count):
        for seq in range(seq_count):
            column = (head * seq_count + seq) * HEAD_SIZE
            target = seq * head_count + head
            leaving.append(
                pltpu.make_async_copy(
                    query_buffer.at[:, column : column + HEAD_SIZE],
                    queries_out_ref.at[target],
                    query_sems.at[target],
                )
            )
            leaving[-1].start()
    for copy in leaving:
        copy.wait()


def key_turn_kernel(share, *refs):
    key_heads = refs[0].shape[0]
    in_refs, out_refs = refs[:-key_heads], refs[-key_heads:]
    mine = lax.div(lax.axis_index("seq"), share)
    for other, out_ref in enumerate(out_refs):
        for number, in_ref in enumerate(in_refs):
            out_ref[number] = in_ref[mine ^ other]


def sorted_rows(pos_ref, chunk, rows):
    per_block = BLK // rows
    first = pos_ref[lax.div(chunk, per_block)] * BLK + lax.rem(chunk, per_block) * rows
    return pl.ds(pl.multiple_of(first, rows), rows)


def block(at):
    return slice(at * BLK, (at + 1) * BLK)


def key_kernel(share, pos_ref, key_map_ref, query_map_ref, *refs):
    seq_count, head_count = lax.axis_size("seq"), lax.axis_size("head")
    piece_refs, refs = refs[:seq_count], refs[seq_count:]
    key_rows, phi, phi_rows, query_weights_ref, key_weights_ref = refs
    rows = piece_refs[0].shape[1]
    seq_blocks = phi.shape[2] // BLK
    blocks = phi.shape[0] * seq_blocks
    mine, plane = lax.axis_index("seq"), lax.axis_index("head")
    query_weights_ref[...] = query_map_ref[mine]
    for other in range(seq_count):
        for number in range(head_count):
            chunk = (mine ^ other) * head_count + (plane ^ number)
            key_rows[sorted_rows(pos_ref, chunk, rows), :] = piece_refs[other][number]
    key_weights_ref[...] = key_map_ref[lax.div(mine, share)]
    parts = map_parts(key_weights_ref[...])
    ahead = []
    for number in range(blocks):
        while number + len(ahead) < min(number + 3, blocks):
            ahead.append(logits_t(parts, key_rows[block(number + len(ahead)), :]))
        seq, at = divmod(number, seq_blocks)
        feature = features_t(ahead.pop(0))
        phi[seq, :, block(at)] = feature
        for half in range(2):
            turned = feature[half * HEAD_SIZE : (half + 1) * HEAD_SIZE].T
            phi_rows[seq, half, block(at), :] = turned.astype(BF16)


def pair_kernel(
    token_count,
    seq_blocks,
    pos_ref,
    arrived_ref,
    query_weights_ref,
    key_weights_ref,
    key_rows,
    phi_k_early,
    phi_kb_rows_early,
    out_ref,
    query_rows,
    phi_q,
    phi_qb,
    phi_k_late,
    phi_kb,
    phi_kb_rows,
    pair_weights,
    scores,
    linears,
    acc_q,
    acc_k,
):
    rows = arrived_ref.shape[1]
    seq_tokens = seq_blocks * BLK
    sequences = token_count // seq_tokens
    acc_q[...] = jnp.zeros_like(acc_q)
    acc_k[...] = jnp.zeros_like(acc_k)
    width = 2 if seq_blocks % 2 == 0 else 1
    tiles = seq_blocks // width
    for seq in range(sequences):
        for at in range(0, seq_blocks, width):
            if width > 1:
                pair_weights[seq, at, block(at + 1), :] = jnp.zeros((BLK, BLK), BF16)
    parts = map_parts(query_weights_ref[...])
    key_parts = map_parts(key_weights_ref[...])
    early = phi_k_early.shape[0]
    lane = lax.broadcasted_iota(jnp.int32, (BLK, BLK), 1)
    sublane = lax.broadcasted_iota(jnp.int32, (BLK, BLK), 0)
    visible = sublane <= lane
    exponent_scale = HEAD_SIZE ** (-0.5) * math.log2(math.e)

    def side_by_side(pieces):
        return jnp.concatenate(list(pieces), axis=1)

    def blocks_of(here):
        return range(here.start // BLK, here.stop // BLK)

    def span(tile):
        return slice(tile * width * BLK, (tile + 1) * width * BLK)

    def flat(seq, here):
        return slice(seq * seq_tokens + here.start, seq * seq_tokens + here.stop)

    def query_logits(seq, at):
        return logits_t(parts, query_rows[flat(seq, block(at)), :])

    def query_features(seq, at, logits):
        feature = features_t(logits)
        phi_q[seq, :, block(at)] = feature
        phi_qb[seq, at] = feature.astype(BF16) * token_count

    def phi_k(seq, at):
        if seq < early:
            return phi_k_early[seq, :, block(at)]
        return phi_k_late[seq - early, :, block(at)]

    def key_logits(seq, at):
        if seq < early:
            return None
        return logits_t(key_parts, key_rows[flat(seq, block(at)), :])

    def key_features(seq, at, logits):
        if seq >= early:
            phi_k_late[seq - early, :, block(at)] = features_t(logits)

    def turn_features(seq, at):
        feature = phi_k(seq, at)
        phi_kb[seq, at] = feature.astype(BF16)
        for half in range(2 if seq >= early else 0):
            turned = feature[half * HEAD_SIZE : (half + 1) * HEAD_SIZE].T
            phi_kb_rows[seq - early, half, block(at), :] = turned.astype(BF16)

    def key_feature_rows(seq, half, stop):
        if seq < early:
            return phi_kb_rows_early[seq, half, :stop, :]
        return phi_kb_rows[seq - early, half, :stop, :]

    def pair_scores(seq, tile):
        here = span(tile)
        slot = tile % 2
        teacher = nt(key_rows[flat(seq, slice(0, here.stop)), :], query_rows[flat(seq, here), :])
        student = nn(
            side_by_side(key_feature_rows(seq, half, here.stop) for half in range(2)),
            side_by_side(phi_qb[seq, at] for at in blocks_of(here)),
        )
        stats = []
        for half in range(width):
            at = tile * width + half
            highest = linear_sum = None
            for number in range(at + 1):
                score = teacher[block(number), block(half)]
                linear = student[block(number), block(half)]
                linears[seq, slot, block(number), block(half)] = linear
                if number == at:
                    score = jnp.where(visible, score, NEG_FLOOR)
                    linear = jnp.where(visible, linear, 0.0)
                scores[seq, slot, block(number), block(half)] = score
                top, total = tile_max(score), tile_sum(linear)
                highest = top if number == 0 else jnp.maximum(highest, top)
                linear_sum = total if number == 0 else linear_sum + total
            stats.append(
                (
                    jnp.max(highest, axis=0, keepdims=True),
                    jnp.sum(linear_sum, axis=0, keepdims=True),
                )
            )
        return stats

    def pair_gradients(seq, tile, half, stats):
        highest, linear_sum = stats
        slot = tile % 2
        at = tile * width + half
        denominator = None
        for number in range(at + 1):
            score = scores[seq, slot, block(number), block(half)]
            exponent = jnp.exp2((score - highest) * exponent_scale)
            scores[seq, slot, block(number), block(half)] = exponent
            total = tile_sum(exponent)
            denominator = total if number == 0 else denominator + total
        denominator = jnp.sum(denominator, axis=0, keepdims=True)
        base = 1.0 / linear_sum
        rate = 1.0 / denominator
        for number in range(at + 1):
            exponent = scores[seq, slot, block(number), block(half)]
            weights = base - exponent * rate / linears[seq, slot, block(number), block(half)]
            if number == at:
                weights = jnp.where(visible, weights, 0.0)
            pair_weights[seq, at, block(number), :] = weights.astype(BF16)

    def map_change(phis, upstream, tokens):
        changes = [
            side_parts(feature_grad_t(phi, upstream[:, block(half)]))
            for half, phi in enumerate(phis)
        ]
        twice = [tokens[block(half)] for half in range(width) for _ in range(2)]
        return nn(jnp.concatenate(changes, axis=1), jnp.concatenate(twice, axis=0))

    def query_upstream(seq, tile):
        here = span(tile)
        return nn(
            side_by_side(phi_kb[seq, at] for at in range(here.stop // BLK)),
            side_by_side(pair_weights[seq, at, : here.stop, :] for at in blocks_of(here)),
        )

    def query_change(seq, tile, upstream):
        phis = [phi_q[seq, :, block(tile * width + half)] for half in range(width)]
        acc_q[...] += map_change(phis, upstream, query_rows[flat(seq, span(tile)), :])

    def key_upstream(seq, tile):
        later = range(tile * width, seq_blocks)
        return nt(
            side_by_side(phi_qb[seq, at] for at in later),
            side_by_side(pair_weights[seq, at, span(tile), :] for at in later),
        )

    def key_change(seq, tile, upstream):
        phis = [phi_k(seq, tile * width + half) for half in range(width)]
        acc_k[...] += map_change(phis, upstream, key_rows[flat(seq, span(tile)), :])

    def feature_steps(seq):
        ahead = [key_logits(seq, at) for at in range(min(3, seq_blocks))]
        for at in range(seq_blocks):
            if at + len(ahead) < seq_blocks:
                ahead.append(key_logits(seq, at + len(ahead)))
            key_features(seq, at, ahead.pop(0))
            if at > 1:
                turn_features(seq, at - 2)
            yield
        for at in range(max(seq_blocks - 2, 0), seq_blocks):
            turn_features(seq, at)

    def feature_steps(seq):
        ahead = []
        for at in range(seq_blocks):
            while at + len(ahead) < min(at + 3, seq_blocks):
                later = at + len(ahead)
                ahead.append((key_logits(seq, later), query_logits(seq, later)))
            from_keys, from_queries = ahead.pop(0)
            key_features(seq, at, from_keys)
            query_features(seq, at, from_queries)
            if at:
                turn_features(seq, at - 1)
            yield
        turn_features(seq, seq_blocks - 1)

    def pair_steps(seq):
        order = list(reversed(range(tiles)))
        ahead = pair_scores(seq, order[0])
        behind = None
        for number, tile in enumerate(order):
            stats = ahead
            if number + 1 < tiles:
                ahead = pair_scores(seq, order[number + 1])
            for half in range(width):
                pair_gradients(seq, tile, half, stats[half])
                yield
            upstreams = query_upstream(seq, tile), key_upstream(seq, tile)
            if behind:
                query_change(seq, order[number - 1], behind[0])
                key_change(seq, order[number - 1], behind[1])
            behind = upstreams
        yield
        query_change(seq, order[-1], behind[0])
        key_change(seq, order[-1], behind[1])

    for chunk in range(token_count // rows):
        query_rows[sorted_rows(pos_ref, chunk, rows), :] = arrived_ref[chunk]
    stages = (feature_steps, pair_steps)
    for turn in range(sequences + len(stages) - 1):
        active = [
            stage(turn - number)
            for number, stage in enumerate(stages)
            if 0 <= turn - number < sequences
        ]
        while active:
            for step in active[::-1]:
                if next(step, step) is step:
                    active.remove(step)
    out_ref[:HEAD_SIZE, :] = acc_q[...].T.astype(BF16)
    out_ref[HEAD_SIZE:, :] = bf16_parts(acc_k[...].T * (1.0 / token_count), 2)


def collect_kernel(everyone_ref, queries_out_ref, keys_out_ref, buffer, sems):
    seq_count = queries_out_ref.shape[0]
    key_heads = keys_out_ref.shape[0]
    share = seq_count // key_heads
    copies = []

    def leave(number, value, out_ref):
        buffer[number] = value
        copies.append(pltpu.make_async_copy(buffer.at[number], out_ref, sems.at[number]))
        copies[-1].start()

    for number in range(seq_count):
        leave(number, everyone_ref[number, :HEAD_SIZE, :].astype(F32), queries_out_ref.at[number])
    for number in range(key_heads):
        total = None
        for seq in range(number * share, (number + 1) * share):
            for half in (1, 2):
                rows = slice(half * HEAD_SIZE, (half + 1) * HEAD_SIZE)
                value = everyone_ref[seq, rows, :].astype(F32)
                total = value if total is None else total + value
        leave(seq_count + number, total, keys_out_ref.at[number])
    for copy in copies:
        copy.wait()


def per_device_head(queries, keys, block_pos, query_map, key_map):
    seq_count = lax.axis_size("seq")
    head_count = lax.axis_size("head")
    key_heads = key_map.shape[0]
    share = seq_count // key_heads
    rows = queries.shape[0]
    devices = seq_count * head_count
    token_count = rows * devices
    seq_tokens = seq_count * BLK
    sequences = token_count // seq_tokens
    vmem = pl.BlockSpec(memory_space=pltpu.VMEM)
    smem = pl.BlockSpec(memory_space=pltpu.SMEM)

    def swap(piece, axis, bits):
        size = lax.axis_size(axis)
        return lax.ppermute(piece, axis, [(i, i ^ bits) for i in range(size)])

    small = pltpu.CompilerParams(vmem_limit_bytes=4 << 20)
    anywhere = pl.BlockSpec(memory_space=pl.ANY)
    sent, *by_plane = pl.pallas_call(
        functools.partial(send_kernel, seq_count),
        out_shape=[jax.ShapeDtypeStruct((devices, rows, HEAD_SIZE), BF16)]
        + [jax.ShapeDtypeStruct((key_heads, rows, HEAD_SIZE), BF16)] * head_count,
        in_specs=[anywhere] * 2,
        out_specs=[anywhere] * (head_count + 1),
        scratch_shapes=[
            pltpu.VMEM(queries.shape, BF16),
            pltpu.VMEM(keys.shape, BF16),
            pltpu.SemaphoreType.DMA((2,)),
            pltpu.SemaphoreType.DMA((devices,)),
            pltpu.SemaphoreType.DMA((head_count, key_heads)),
        ],
        compiler_params=pltpu.CompilerParams(vmem_limit_bytes=60 << 20),
    )(queries, keys)
    for other in range(1, head_count):
        by_plane[other] = swap(by_plane[other], "head", other)
    arrived = lax.all_to_all(sent, ("seq", "head"), split_axis=0, concat_axis=0, tiled=True)
    by_key_head = pl.pallas_call(
        functools.partial(key_turn_kernel, share),
        out_shape=[jax.ShapeDtypeStruct((head_count, rows, HEAD_SIZE), BF16)] * key_heads,
        in_specs=[vmem] * head_count,
        out_specs=[vmem] * key_heads,
        compiler_params=small,
    )(*by_plane)
    pieces = [None] * seq_count
    for other in range(0, seq_count, 2):
        piece = by_key_head[other // share]
        pieces[other] = swap(piece, "seq", other) if other else piece
    for other in range(0, seq_count, 2):
        pieces[other + 1] = swap(pieces[other], "seq", 1)
    early = max(sequences // 2, 1)
    weights_shape = jax.ShapeDtypeStruct((HEAD_SIZE, HEAD_SIZE), F32)
    key_rows, phi_k, phi_rows, query_weights, key_weights = pl.pallas_call(
        functools.partial(key_kernel, share),
        out_shape=(
            jax.ShapeDtypeStruct((token_count, HEAD_SIZE), BF16),
            jax.ShapeDtypeStruct((early, 2 * HEAD_SIZE, seq_tokens), F32),
            jax.ShapeDtypeStruct((early, 2, seq_tokens, HEAD_SIZE), BF16),
            weights_shape,
            weights_shape,
        ),
        in_specs=[smem] + [vmem] * (seq_count + 2),
        out_specs=(vmem,) * 5,
        compiler_params=pltpu.CompilerParams(vmem_limit_bytes=8 << 20),
        cost_estimate=pl.CostEstimate(
            flops=token_count * HEAD_SIZE * HEAD_SIZE * 6,
            bytes_accessed=token_count * HEAD_SIZE * 12,
            transcendentals=token_count * HEAD_SIZE * 2,
        ),
    )(block_pos, key_map, query_map, *pieces)
    grads = pl.pallas_call(
        functools.partial(pair_kernel, token_count, seq_count),
        out_shape=jax.ShapeDtypeStruct((3 * HEAD_SIZE, HEAD_SIZE), BF16),
        in_specs=[smem] + [vmem] * 6,
        out_specs=vmem,
        scratch_shapes=[
            pltpu.VMEM((token_count, HEAD_SIZE), BF16),
            pltpu.VMEM((sequences, 2 * HEAD_SIZE, seq_tokens), F32),
            pltpu.VMEM((sequences, seq_count, 2 * HEAD_SIZE, BLK), BF16),
            pltpu.VMEM((max(sequences - early, 1), 2 * HEAD_SIZE, seq_tokens), F32),
            pltpu.VMEM((sequences, seq_count, 2 * HEAD_SIZE, BLK), BF16),
            pltpu.VMEM((max(sequences - early, 1), 2, seq_tokens, HEAD_SIZE), BF16),
            pltpu.VMEM((sequences, seq_count, seq_tokens, BLK), BF16),
            pltpu.VMEM((sequences, 2, seq_tokens, 2 * BLK), F32),
            pltpu.VMEM((sequences, 2, seq_tokens, 2 * BLK), F32),
            pltpu.VMEM((HEAD_SIZE, HEAD_SIZE), F32),
            pltpu.VMEM((HEAD_SIZE, HEAD_SIZE), F32),
        ],
        compiler_params=pltpu.CompilerParams(vmem_limit_bytes=32 << 20),
    )(block_pos, arrived, query_weights, key_weights, key_rows, phi_k, phi_rows)
    everyone = lax.all_gather(grads, "seq", axis=0, tiled=False)
    return pl.pallas_call(
        collect_kernel,
        out_shape=(
            jax.ShapeDtypeStruct((seq_count, HEAD_SIZE, HEAD_SIZE), F32),
            jax.ShapeDtypeStruct((key_heads, HEAD_SIZE, HEAD_SIZE), F32),
        ),
        in_specs=[vmem],
        out_specs=(pl.BlockSpec(memory_space=pl.ANY),) * 2,
        scratch_shapes=[
            pltpu.VMEM((seq_count + key_heads, HEAD_SIZE, HEAD_SIZE), F32),
            pltpu.SemaphoreType.DMA((seq_count + key_heads,)),
        ],
        compiler_params=small,
    )(everyone)


def one_head_each(mesh, queries, keys, block_pos, query_map, key_map):
    del keys, block_pos
    seq_count, head_count = mesh.shape["seq"], mesh.shape["head"]
    rows = queries.shape[0] // (seq_count * head_count)
    key_heads = key_map.shape[0] // head_count
    return (
        query_map.shape[0] == seq_count * head_count
        and seq_count % (2 * key_heads) == 0
        and seq_count & (seq_count - 1) == 0
        and head_count & (head_count - 1) == 0
        and BLK % rows == 0
        and rows % 16 == 0
    )


def solution(mesh):
    in_specs = (
        P(("seq", "head"), None),
        P(("seq", "head"), None),
        P(),
        P("head", None, None),
        P("head", None, None),
    )
    out_specs = (P("head", None, None), P("head", None, None))

    def sharded(function):
        return jax.shard_map(
            function, mesh=mesh, in_specs=in_specs, out_specs=out_specs, check_vma=False
        )

    def step(*args):
        if one_head_each(mesh, *args):
            return sharded(per_device_head)(*args)
        return sharded(per_device_general)(*args)

    return step
```

```python
import functools
import math

import jax
import jax.numpy as jnp
from jax import lax
from jax.experimental import pallas as pl
from jax.experimental.pallas import tpu as pltpu
from jax.sharding import PartitionSpec as P


HEAD_SIZE = 128
BLK = 128

HIGHEST = lax.Precision.HIGHEST
NEG_FLOOR = -1e30


def softmax_pair(logits):
    return jnp.concatenate(
        [jax.nn.softmax(logits, axis=-1), jax.nn.softmax(-logits, axis=-1)], axis=-1
    )


def feature_grad(feature, upstream):
    half_width = feature.shape[-1] // 2
    positive, negative = (feature[..., :half_width], feature[..., half_width:])
    grad_positive, grad_negative = (upstream[..., :half_width], upstream[..., half_width:])
    first = positive * (grad_positive - jnp.sum(grad_positive * positive, axis=-1, keepdims=True))
    second = negative * (grad_negative - jnp.sum(grad_negative * negative, axis=-1, keepdims=True))
    return first - second


def row_places(row_index, block_pos, seq_count):
    stored = row_index // BLK
    lookup = stored[:, None] == jnp.arange(block_pos.shape[0], dtype=jnp.int32)[None, :]
    blocks = jnp.sum(jnp.where(lookup, block_pos[None, :], 0), axis=1)
    return (blocks // seq_count, blocks * BLK + row_index % BLK)


def over_blocks(running, portions, step_fn):
    row_count = portions[0].shape[1]
    step_rows = math.gcd(row_count, 512)

    def advance(number, inner_carry):
        slabs = tuple(
            (
                lax.dynamic_slice_in_dim(portion, number * step_rows, step_rows, 1)
                for portion in portions
            )
        )
        return step_fn(inner_carry, slabs, number * step_rows)

    return lax.fori_loop(0, row_count // step_rows, advance, running)


def per_device_general(queries, keys, block_pos, query_map, key_map):
    local_q, local_k = (
        lax.all_to_all(queries, "head", split_axis=1, concat_axis=0, tiled=True),
        lax.all_to_all(keys, "head", split_axis=1, concat_axis=0, tiled=True),
    )
    seq_count = lax.axis_size("seq")
    seq_rank = lax.axis_index("seq")
    rows_local = local_k.shape[0]
    token_count = rows_local * seq_count
    key_heads = key_map.shape[0]
    group_width = query_map.shape[0] // key_heads
    score_scale = HEAD_SIZE ** (-0.5)
    query_index = seq_rank * rows_local + jnp.arange(rows_local, dtype=jnp.int32)
    query_heads = local_q.reshape(rows_local, key_heads, group_width, HEAD_SIZE).transpose(
        1, 2, 0, 3
    )
    query_wide = query_heads.astype(jnp.float32)
    query_logits = jnp.einsum(
        "vgnd,vgde->vgne",
        query_wide,
        query_map.reshape(key_heads, group_width, HEAD_SIZE, HEAD_SIZE),
        precision=HIGHEST,
    )
    rows_all = group_width * rows_local
    phi_query = softmax_pair(query_logits).reshape(key_heads, rows_all, 2 * HEAD_SIZE)
    phi_query_b = phi_query.astype(jnp.bfloat16)
    query_flat = query_heads.reshape(key_heads, rows_all, HEAD_SIZE)
    query_seq, query_at = row_places(query_index, block_pos, seq_count)
    query_seq = jnp.tile(query_seq, group_width)
    query_at = jnp.tile(query_at, group_width)

    def visible_for(offset, slab_rows):
        key_index = offset + jnp.arange(slab_rows, dtype=jnp.int32)
        key_seq, key_at = row_places(key_index, block_pos, seq_count)
        return (key_seq[None, :] == query_seq[:, None]) & (key_at[None, :] <= query_at[:, None])

    def key_features(key_slab):
        logits = jnp.einsum(
            "vwd,vde->vwe", key_slab.astype(jnp.float32), key_map, precision=HIGHEST
        )
        return softmax_pair(logits)

    def teacher(key_slab):
        return (
            jnp.einsum("vrd,vwd->vrw", query_flat, key_slab, preferred_element_type=jnp.float32)
            * score_scale
        )

    def stats_step(running, slabs, offset):
        key_slab = slabs[0]
        visible = visible_for(offset, key_slab.shape[1])

        def stats_compute_live(current):
            highest, denominator, linear_sum = current
            masked = jnp.where(visible[None], teacher(key_slab), NEG_FLOOR)
            new_high = jnp.maximum(highest, jnp.max(masked, axis=-1))
            exponent = jnp.where(visible[None], jnp.exp(masked - new_high[..., None]), 0.0)
            denominator = denominator * jnp.exp(highest - new_high) + jnp.sum(exponent, axis=-1)
            phi_key_b = key_features(key_slab).astype(jnp.bfloat16)
            linear = jnp.einsum(
                "vrf,vwf->vrw", phi_query_b, phi_key_b, preferred_element_type=jnp.float32
            )
            linear_sum = linear_sum + jnp.sum(jnp.where(visible[None], linear, 0.0), axis=-1)
            return (new_high, denominator, linear_sum)

        return lax.cond(jnp.any(visible), stats_compute_live, lambda current: current, running)

    def grads_step(running, slabs, offset):
        key_slab = slabs[0]
        visible = visible_for(offset, key_slab.shape[1])

        def grads_compute_live(current):
            query_grad, key_weight_grad = current
            masked = jnp.where(visible[None], teacher(key_slab), NEG_FLOOR)
            exponent = jnp.where(visible[None], jnp.exp(masked - highest[..., None]), 0.0)
            teacher_prob = exponent / denominator[..., None]
            phi_key = key_features(key_slab)
            phi_key_b = phi_key.astype(jnp.bfloat16)
            linear = jnp.einsum(
                "vrf,vwf->vrw", phi_query_b, phi_key_b, preferred_element_type=jnp.float32
            )
            weights = (
                jnp.where(visible[None], 1.0 / linear_sum[..., None] - teacher_prob / linear, 0.0)
                / token_count
            ).astype(jnp.bfloat16)
            query_grad = query_grad + jnp.einsum(
                "vrw,vwf->vrf", weights, phi_key_b, preferred_element_type=jnp.float32
            )
            key_grad = jnp.einsum(
                "vrw,vrf->vwf", weights, phi_query_b, preferred_element_type=jnp.float32
            )
            key_logit_grad = feature_grad(phi_key, key_grad)
            key_weight_grad = key_weight_grad + jnp.einsum(
                "vwd,vwe->vde", key_slab.astype(jnp.float32), key_logit_grad, precision=HIGHEST
            )
            return (query_grad, key_weight_grad)

        return lax.cond(jnp.any(visible), grads_compute_live, lambda current: current, running)

    def as_heads(pieces):
        return pieces.reshape(pieces.shape[0], key_heads, -1).transpose(1, 0, 2)

    row_zeros = jnp.zeros((key_heads, rows_all), jnp.float32)
    stats_init = (jnp.full((key_heads, rows_all), NEG_FLOOR, jnp.float32), row_zeros, row_zeros)
    grads_init = (
        jnp.zeros((key_heads, rows_all, 2 * HEAD_SIZE), jnp.float32),
        jnp.zeros((key_heads, HEAD_SIZE, HEAD_SIZE), jnp.float32),
    )
    highest, denominator, linear_sum = over_blocks(
        stats_init, (as_heads(lax.all_gather(local_k, "seq", axis=0, tiled=True)),), stats_step
    )
    query_grad, key_weight_grad = over_blocks(
        grads_init, (as_heads(lax.all_gather(local_k, "seq", axis=0, tiled=True)),), grads_step
    )
    query_logit_grad = feature_grad(phi_query, query_grad).reshape(
        key_heads, group_width, rows_local, HEAD_SIZE
    )
    query_weight_grad = jnp.einsum(
        "vgnd,vgne->vgde", query_wide, query_logit_grad, precision=HIGHEST
    ).reshape(key_heads * group_width, HEAD_SIZE, HEAD_SIZE)
    query_map_gradient, key_map_gradient = lax.psum((query_weight_grad, key_weight_grad), "seq")
    return (query_map_gradient, key_map_gradient)


NT = (((1,), (1,)), ((), ()))
F32 = jnp.float32
BF16 = jnp.bfloat16


def nn(left, right):
    return jnp.dot(left, right, preferred_element_type=F32)


def nt(left, right):
    return lax.dot_general(left, right, NT, preferred_element_type=F32)


def bf16_parts(value, count):
    parts = []
    for _ in range(count):
        part = value.astype(BF16)
        parts.append(part)
        value = value - part.astype(F32)
    return jnp.concatenate(parts, axis=0)


def features_t(logits):
    up = jnp.exp2(logits - jnp.max(logits, axis=0, keepdims=True))
    down = jnp.exp2(jnp.min(logits, axis=0, keepdims=True) - logits)
    up = up * (1.0 / jnp.sum(up, axis=0, keepdims=True))
    down = down * (1.0 / jnp.sum(down, axis=0, keepdims=True))
    return jnp.concatenate([up, down], axis=0)


def feature_grad_t(feature, upstream):
    halves = []
    for half in (slice(0, HEAD_SIZE), slice(HEAD_SIZE, 2 * HEAD_SIZE)):
        value, grad = feature[half], upstream[half]
        halves.append(value * (grad - jnp.sum(grad * value, axis=0, keepdims=True)))
    return halves[0] - halves[1]


def tile_sum(value):
    return jnp.sum(value.reshape(-1, 8, value.shape[-1]), axis=0)


def tile_max(value):
    return jnp.max(value.reshape(-1, 8, value.shape[-1]), axis=0)


def side_parts(value):
    high = value.astype(BF16)
    return jnp.concatenate([high, (value - high.astype(F32)).astype(BF16)], axis=1)


def map_parts(weights):
    rest = weights.T * math.log2(math.e)
    parts = []
    for _ in range(3):
        parts.append(rest.astype(BF16))
        rest = rest - parts[-1].astype(F32)
    return jnp.concatenate(parts[::-1], axis=1)


def logits_t(parts, tokens):
    return nt(parts, jnp.concatenate([tokens] * 3, axis=1))


def send_kernel(seq_count, queries_ref, keys_ref, *refs):
    queries_out_ref, *keys_out_refs, query_buffer, key_buffer, sems, query_sems, key_sems = refs
    head_count = len(keys_out_refs)
    key_heads = keys_out_refs[0].shape[0]
    keys_in = pltpu.make_async_copy(keys_ref, key_buffer, sems.at[0])
    queries_in = pltpu.make_async_copy(queries_ref, query_buffer, sems.at[1])
    keys_in.start()
    queries_in.start()
    leaving = []
    keys_in.wait()
    for other, out_ref in enumerate(keys_out_refs):
        for number in range(key_heads):
            column = ((lax.axis_index("head") ^ other) * key_heads + number) * HEAD_SIZE
            column = pl.multiple_of(column, HEAD_SIZE)
            leaving.append(
                pltpu.make_async_copy(
                    key_buffer.at[:, pl.ds(column, HEAD_SIZE)],
                    out_ref.at[number],
                    key_sems.at[other, number],
                )
            )
            leaving[-1].start()
    queries_in.wait()
    for head in range(head_count):
        for seq in range(seq_count):
            column = (head * seq_count + seq) * HEAD_SIZE
            target = seq * head_count + head
            leaving.append(
                pltpu.make_async_copy(
                    query_buffer.at[:, column : column + HEAD_SIZE],
                    queries_out_ref.at[target],
                    query_sems.at[target],
                )
            )
            leaving[-1].start()
    for copy in leaving:
        copy.wait()


def key_turn_kernel(share, *refs):
    key_heads = refs[0].shape[0]
    in_refs, out_refs = refs[:-key_heads], refs[-key_heads:]
    mine = lax.div(lax.axis_index("seq"), share)
    for other, out_ref in enumerate(out_refs):
        for number, in_ref in enumerate(in_refs):
            out_ref[number] = in_ref[mine ^ other]


def sorted_rows(pos_ref, chunk, rows):
    per_block = BLK // rows
    first = pos_ref[lax.div(chunk, per_block)] * BLK + lax.rem(chunk, per_block) * rows
    return pl.ds(pl.multiple_of(first, rows), rows)


def block(at):
    return slice(at * BLK, (at + 1) * BLK)


def key_kernel(share, pos_ref, key_map_ref, query_map_ref, *refs):
    seq_count, head_count = lax.axis_size("seq"), lax.axis_size("head")
    piece_refs, refs = refs[:seq_count], refs[seq_count:]
    key_rows, phi, phi_rows, query_weights_ref, key_weights_ref = refs
    rows = piece_refs[0].shape[1]
    seq_blocks = phi.shape[2] // BLK
    blocks = phi.shape[0] * seq_blocks
    mine, plane = lax.axis_index("seq"), lax.axis_index("head")
    query_weights_ref[...] = query_map_ref[mine]
    for other in range(seq_count):
        for number in range(head_count):
            chunk = (mine ^ other) * head_count + (plane ^ number)
            key_rows[sorted_rows(pos_ref, chunk, rows), :] = piece_refs[other][number]
    key_weights_ref[...] = key_map_ref[lax.div(mine, share)]
    parts = map_parts(key_weights_ref[...])
    ahead = []
    for number in range(blocks):
        while number + len(ahead) < min(number + 3, blocks):
            ahead.append(logits_t(parts, key_rows[block(number + len(ahead)), :]))
        seq, at = divmod(number, seq_blocks)
        feature = features_t(ahead.pop(0))
        phi[seq, :, block(at)] = feature
        for half in range(2):
            turned = feature[half * HEAD_SIZE : (half + 1) * HEAD_SIZE].T
            phi_rows[seq, half, block(at), :] = turned.astype(BF16)


def pair_kernel(
    token_count,
    seq_blocks,
    pos_ref,
    arrived_ref,
    query_weights_ref,
    key_weights_ref,
    key_rows,
    phi_k_early,
    phi_kb_rows_early,
    out_ref,
    query_rows,
    phi_q,
    phi_qb,
    phi_k_late,
    phi_kb,
    phi_kb_rows,
    pair_weights,
    scores,
    linears,
    acc_q,
    acc_k,
):
    rows = arrived_ref.shape[1]
    seq_tokens = seq_blocks * BLK
    sequences = token_count // seq_tokens
    acc_q[...] = jnp.zeros_like(acc_q)
    acc_k[...] = jnp.zeros_like(acc_k)
    width = 2 if seq_blocks % 2 == 0 else 1
    tiles = seq_blocks // width
    for seq in range(sequences):
        for at in range(0, seq_blocks, width):
            if width > 1:
                pair_weights[seq, at, block(at + 1), :] = jnp.zeros((BLK, BLK), BF16)
    parts = map_parts(query_weights_ref[...])
    key_parts = map_parts(key_weights_ref[...])
    early = phi_k_early.shape[0]
    lane = lax.broadcasted_iota(jnp.int32, (BLK, BLK), 1)
    sublane = lax.broadcasted_iota(jnp.int32, (BLK, BLK), 0)
    visible = sublane <= lane
    exponent_scale = HEAD_SIZE ** (-0.5) * math.log2(math.e)

    def side_by_side(pieces):
        return jnp.concatenate(list(pieces), axis=1)

    def blocks_of(here):
        return range(here.start // BLK, here.stop // BLK)

    def span(tile):
        return slice(tile * width * BLK, (tile + 1) * width * BLK)

    def flat(seq, here):
        return slice(seq * seq_tokens + here.start, seq * seq_tokens + here.stop)

    def query_logits(seq, at):
        return logits_t(parts, query_rows[flat(seq, block(at)), :])

    def query_features(seq, at, logits):
        feature = features_t(logits)
        phi_q[seq, :, block(at)] = feature
        phi_qb[seq, at] = feature.astype(BF16) * token_count

    def phi_k(seq, at):
        if seq < early:
            return phi_k_early[seq, :, block(at)]
        return phi_k_late[seq - early, :, block(at)]

    def key_logits(seq, at):
        if seq < early:
            return None
        return logits_t(key_parts, key_rows[flat(seq, block(at)), :])

    def key_features(seq, at, logits):
        if seq >= early:
            phi_k_late[seq - early, :, block(at)] = features_t(logits)

    def turn_features(seq, at):
        feature = phi_k(seq, at)
        phi_kb[seq, at] = feature.astype(BF16)
        for half in range(2 if seq >= early else 0):
            turned = feature[half * HEAD_SIZE : (half + 1) * HEAD_SIZE].T
            phi_kb_rows[seq - early, half, block(at), :] = turned.astype(BF16)

    def key_feature_rows(seq, half, stop):
        if seq < early:
            return phi_kb_rows_early[seq, half, :stop, :]
        return phi_kb_rows[seq - early, half, :stop, :]

    def pair_scores(seq, tile):
        here = span(tile)
        slot = tile % 3
        teacher = nt(key_rows[flat(seq, slice(0, here.stop)), :], query_rows[flat(seq, here), :])
        student = nn(
            side_by_side(key_feature_rows(seq, half, here.stop) for half in range(2)),
            side_by_side(phi_qb[seq, at] for at in blocks_of(here)),
        )
        stats = []
        for half in range(width):
            at = tile * width + half
            highest = linear_sum = None
            for number in range(at + 1):
                score = teacher[block(number), block(half)]
                linear = student[block(number), block(half)]
                linears[seq, slot, block(number), block(half)] = linear
                if number == at:
                    score = jnp.where(visible, score, NEG_FLOOR)
                    linear = jnp.where(visible, linear, 0.0)
                scores[seq, slot, block(number), block(half)] = score
                top, total = tile_max(score), tile_sum(linear)
                highest = top if number == 0 else jnp.maximum(highest, top)
                linear_sum = total if number == 0 else linear_sum + total
            stats.append(
                (
                    jnp.max(highest, axis=0, keepdims=True),
                    jnp.sum(linear_sum, axis=0, keepdims=True),
                )
            )
        return stats

    def pair_gradients(seq, tile, half, stats):
        highest, linear_sum = stats
        slot = tile % 3
        at = tile * width + half
        denominator = None
        for number in range(at + 1):
            score = scores[seq, slot, block(number), block(half)]
            exponent = jnp.exp2((score - highest) * exponent_scale)
            scores[seq, slot, block(number), block(half)] = exponent
            total = tile_sum(exponent)
            denominator = total if number == 0 else denominator + total
        denominator = jnp.sum(denominator, axis=0, keepdims=True)
        base = 1.0 / linear_sum
        rate = 1.0 / denominator
        for number in range(at + 1):
            exponent = scores[seq, slot, block(number), block(half)]
            weights = base - exponent * rate / linears[seq, slot, block(number), block(half)]
            if number == at:
                weights = jnp.where(visible, weights, 0.0)
            pair_weights[seq, at, block(number), :] = weights.astype(BF16)

    def map_change(phis, upstream, tokens):
        changes = [
            side_parts(feature_grad_t(phi, upstream[:, block(half)]))
            for half, phi in enumerate(phis)
        ]
        twice = [tokens[block(half)] for half in range(width) for _ in range(2)]
        return nn(jnp.concatenate(changes, axis=1), jnp.concatenate(twice, axis=0))

    def query_upstream(seq, tile):
        here = span(tile)
        return nn(
            side_by_side(phi_kb[seq, at] for at in range(here.stop // BLK)),
            side_by_side(pair_weights[seq, at, : here.stop, :] for at in blocks_of(here)),
        )

    def query_change(seq, tile, upstream):
        phis = [phi_q[seq, :, block(tile * width + half)] for half in range(width)]
        acc_q[...] += map_change(phis, upstream, query_rows[flat(seq, span(tile)), :])

    def key_upstream(seq, tile):
        later = range(tile * width, seq_blocks)
        return nt(
            side_by_side(phi_qb[seq, at] for at in later),
            side_by_side(pair_weights[seq, at, span(tile), :] for at in later),
        )

    def key_change(seq, tile, upstream):
        phis = [phi_k(seq, tile * width + half) for half in range(width)]
        acc_k[...] += map_change(phis, upstream, key_rows[flat(seq, span(tile)), :])

    def feature_steps(seq):
        ahead = [key_logits(seq, at) for at in range(min(3, seq_blocks))]
        for at in range(seq_blocks):
            if at + len(ahead) < seq_blocks:
                ahead.append(key_logits(seq, at + len(ahead)))
            key_features(seq, at, ahead.pop(0))
            if at > 1:
                turn_features(seq, at - 2)
            yield
        for at in range(max(seq_blocks - 2, 0), seq_blocks):
            turn_features(seq, at)

    def feature_steps(seq):
        ahead = []
        for at in range(seq_blocks):
            while at + len(ahead) < min(at + 3, seq_blocks):
                later = at + len(ahead)
                ahead.append((key_logits(seq, later), query_logits(seq, later)))
            from_keys, from_queries = ahead.pop(0)
            key_features(seq, at, from_keys)
            query_features(seq, at, from_queries)
            if at:
                turn_features(seq, at - 1)
            yield
        turn_features(seq, seq_blocks - 1)

    def pair_steps(seq):
        order = list(reversed(range(tiles)))
        ahead = [pair_scores(seq, order[0])]
        behind = None
        for number, tile in enumerate(order):
            while number + len(ahead) < min(number + 3, tiles):
                ahead.append(pair_scores(seq, order[number + len(ahead)]))
            stats = ahead.pop(0)
            for half in range(width):
                pair_gradients(seq, tile, half, stats[half])
                yield
            upstreams = query_upstream(seq, tile), key_upstream(seq, tile)
            if behind:
                query_change(seq, order[number - 1], behind[0])
                key_change(seq, order[number - 1], behind[1])
            behind = upstreams
        yield
        query_change(seq, order[-1], behind[0])
        key_change(seq, order[-1], behind[1])

    for chunk in range(token_count // rows):
        query_rows[sorted_rows(pos_ref, chunk, rows), :] = arrived_ref[chunk]
    stages = (feature_steps, pair_steps)
    for turn in range(sequences + len(stages) - 1):
        active = [
            stage(turn - number)
            for number, stage in enumerate(stages)
            if 0 <= turn - number < sequences
        ]
        while active:
            for step in active[::-1]:
                if next(step, step) is step:
                    active.remove(step)
    out_ref[:HEAD_SIZE, :] = acc_q[...].T.astype(BF16)
    out_ref[HEAD_SIZE:, :] = bf16_parts(acc_k[...].T * (1.0 / token_count), 2)


def collect_kernel(everyone_ref, queries_out_ref, keys_out_ref, buffer, sems):
    seq_count = queries_out_ref.shape[0]
    key_heads = keys_out_ref.shape[0]
    share = seq_count // key_heads
    copies = []

    def leave(number, value, out_ref):
        buffer[number] = value
        copies.append(pltpu.make_async_copy(buffer.at[number], out_ref, sems.at[number]))
        copies[-1].start()

    for number in range(seq_count):
        leave(number, everyone_ref[number, :HEAD_SIZE, :].astype(F32), queries_out_ref.at[number])
    for number in range(key_heads):
        total = None
        for seq in range(number * share, (number + 1) * share):
            for half in (1, 2):
                rows = slice(half * HEAD_SIZE, (half + 1) * HEAD_SIZE)
                value = everyone_ref[seq, rows, :].astype(F32)
                total = value if total is None else total + value
        leave(seq_count + number, total, keys_out_ref.at[number])
    for copy in copies:
        copy.wait()


def per_device_head(queries, keys, block_pos, query_map, key_map):
    seq_count = lax.axis_size("seq")
    head_count = lax.axis_size("head")
    key_heads = key_map.shape[0]
    share = seq_count // key_heads
    rows = queries.shape[0]
    devices = seq_count * head_count
    token_count = rows * devices
    seq_tokens = seq_count * BLK
    sequences = token_count // seq_tokens
    vmem = pl.BlockSpec(memory_space=pltpu.VMEM)
    smem = pl.BlockSpec(memory_space=pltpu.SMEM)

    def swap(piece, axis, bits):
        size = lax.axis_size(axis)
        return lax.ppermute(piece, axis, [(i, i ^ bits) for i in range(size)])

    small = pltpu.CompilerParams(vmem_limit_bytes=4 << 20)
    anywhere = pl.BlockSpec(memory_space=pl.ANY)
    sent, *by_plane = pl.pallas_call(
        functools.partial(send_kernel, seq_count),
        out_shape=[jax.ShapeDtypeStruct((devices, rows, HEAD_SIZE), BF16)]
        + [jax.ShapeDtypeStruct((key_heads, rows, HEAD_SIZE), BF16)] * head_count,
        in_specs=[anywhere] * 2,
        out_specs=[anywhere] * (head_count + 1),
        scratch_shapes=[
            pltpu.VMEM(queries.shape, BF16),
            pltpu.VMEM(keys.shape, BF16),
            pltpu.SemaphoreType.DMA((2,)),
            pltpu.SemaphoreType.DMA((devices,)),
            pltpu.SemaphoreType.DMA((head_count, key_heads)),
        ],
        compiler_params=pltpu.CompilerParams(vmem_limit_bytes=60 << 20),
    )(queries, keys)
    for other in range(1, head_count):
        by_plane[other] = swap(by_plane[other], "head", other)
    arrived = lax.all_to_all(sent, ("seq", "head"), split_axis=0, concat_axis=0, tiled=True)
    by_key_head = pl.pallas_call(
        functools.partial(key_turn_kernel, share),
        out_shape=[jax.ShapeDtypeStruct((head_count, rows, HEAD_SIZE), BF16)] * key_heads,
        in_specs=[vmem] * head_count,
        out_specs=[vmem] * key_heads,
        compiler_params=small,
    )(*by_plane)
    pieces = [None] * seq_count
    for other in range(0, seq_count, 2):
        piece = by_key_head[other // share]
        pieces[other] = swap(piece, "seq", other) if other else piece
    for other in range(0, seq_count, 2):
        pieces[other + 1] = swap(pieces[other], "seq", 1)
    early = max(sequences // 2, 1)
    weights_shape = jax.ShapeDtypeStruct((HEAD_SIZE, HEAD_SIZE), F32)
    key_rows, phi_k, phi_rows, query_weights, key_weights = pl.pallas_call(
        functools.partial(key_kernel, share),
        out_shape=(
            jax.ShapeDtypeStruct((token_count, HEAD_SIZE), BF16),
            jax.ShapeDtypeStruct((early, 2 * HEAD_SIZE, seq_tokens), F32),
            jax.ShapeDtypeStruct((early, 2, seq_tokens, HEAD_SIZE), BF16),
            weights_shape,
            weights_shape,
        ),
        in_specs=[smem] + [vmem] * (seq_count + 2),
        out_specs=(vmem,) * 5,
        compiler_params=pltpu.CompilerParams(vmem_limit_bytes=8 << 20),
        cost_estimate=pl.CostEstimate(
            flops=token_count * HEAD_SIZE * HEAD_SIZE * 6,
            bytes_accessed=token_count * HEAD_SIZE * 12,
            transcendentals=token_count * HEAD_SIZE * 2,
        ),
    )(block_pos, key_map, query_map, *pieces)
    grads = pl.pallas_call(
        functools.partial(pair_kernel, token_count, seq_count),
        out_shape=jax.ShapeDtypeStruct((3 * HEAD_SIZE, HEAD_SIZE), BF16),
        in_specs=[smem] + [vmem] * 6,
        out_specs=vmem,
        scratch_shapes=[
            pltpu.VMEM((token_count, HEAD_SIZE), BF16),
            pltpu.VMEM((sequences, 2 * HEAD_SIZE, seq_tokens), F32),
            pltpu.VMEM((sequences, seq_count, 2 * HEAD_SIZE, BLK), BF16),
            pltpu.VMEM((max(sequences - early, 1), 2 * HEAD_SIZE, seq_tokens), F32),
            pltpu.VMEM((sequences, seq_count, 2 * HEAD_SIZE, BLK), BF16),
            pltpu.VMEM((max(sequences - early, 1), 2, seq_tokens, HEAD_SIZE), BF16),
            pltpu.VMEM((sequences, seq_count, seq_tokens, BLK), BF16),
            pltpu.VMEM((sequences, 3, seq_tokens, 2 * BLK), F32),
            pltpu.VMEM((sequences, 3, seq_tokens, 2 * BLK), F32),
            pltpu.VMEM((HEAD_SIZE, HEAD_SIZE), F32),
            pltpu.VMEM((HEAD_SIZE, HEAD_SIZE), F32),
        ],
        compiler_params=pltpu.CompilerParams(vmem_limit_bytes=32 << 20),
    )(block_pos, arrived, query_weights, key_weights, key_rows, phi_k, phi_rows)
    everyone = lax.all_gather(grads, "seq", axis=0, tiled=False)
    return pl.pallas_call(
        collect_kernel,
        out_shape=(
            jax.ShapeDtypeStruct((seq_count, HEAD_SIZE, HEAD_SIZE), F32),
            jax.ShapeDtypeStruct((key_heads, HEAD_SIZE, HEAD_SIZE), F32),
        ),
        in_specs=[vmem],
        out_specs=(pl.BlockSpec(memory_space=pl.ANY),) * 2,
        scratch_shapes=[
            pltpu.VMEM((seq_count + key_heads, HEAD_SIZE, HEAD_SIZE), F32),
            pltpu.SemaphoreType.DMA((seq_count + key_heads,)),
        ],
        compiler_params=small,
    )(everyone)


def one_head_each(mesh, queries, keys, block_pos, query_map, key_map):
    del keys, block_pos
    seq_count, head_count = mesh.shape["seq"], mesh.shape["head"]
    rows = queries.shape[0] // (seq_count * head_count)
    key_heads = key_map.shape[0] // head_count
    return (
        query_map.shape[0] == seq_count * head_count
        and seq_count % (2 * key_heads) == 0
        and seq_count & (seq_count - 1) == 0
        and head_count & (head_count - 1) == 0
        and BLK % rows == 0
        and rows % 16 == 0
    )


def solution(mesh):
    in_specs = (
        P(("seq", "head"), None),
        P(("seq", "head"), None),
        P(),
        P("head", None, None),
        P("head", None, None),
    )
    out_specs = (P("head", None, None), P("head", None, None))

    def sharded(function):
        return jax.shard_map(
            function, mesh=mesh, in_specs=in_specs, out_specs=out_specs, check_vma=False
        )

    def step(*args):
        if one_head_each(mesh, *args):
            return sharded(per_device_head)(*args)
        return sharded(per_device_general)(*args)

    return step
```
